32 devices in a mesh: step: 8 (over y, x, core), rows: 4 (over z).
Axes of the slice: x: 2, y: 2, z: 4, core: 2. Of those that a mesh axis runs over, the one named last changes fastest.
Arguments:
- init_states: float32 [8, 1, 2, 77, 384], P('step', None, None, None, 'rows'), may hold values from -63 to 63
- forcing: float32 [8, 1, 4, 384], P('step', None, None, 'rows'), may hold values from -63 to 63
- history: int32 [8, 1], P('step'), may hold values from 1 to 2
- land_mask: int32 [384], P('rows'), may hold values 0 or 1
- w_in: float32 [800, 158], replicated, may hold values from -0.5 to 0.5
- b_in: float32 [800], replicated, may hold values from -1.5 to 1.5
- w_dw: float32 [800, 7, 7], replicated, may hold values from -0.875 to 0.875
- bn_gain: float32 [800], replicated, may hold values from 0.5 to 1.5
- bn_bias: float32 [800], replicated, may hold values from -1.5 to 1.5
- w_up: float32 [3200, 800], replicated, may hold values from -0.21875 to 0.21875
- b_up: float32 [3200], replicated, may hold values from -1.5 to 1.5
- w_down: float32 [800, 3200], replicated, may hold values from -0.109375 to 0.109375
- b_down: float32 [800], replicated, may hold values from -1.5 to 1.5
- w_out: float32 [77, 800], replicated, may hold values from -0.21875 to 0.21875
- b_out: float32 [77], replicated, may hold values from -1.5 to 1.5
- cotangent: float32 [8, 8, 1, 77, 384], P('step', None, None, None, 'rows'), may hold values from -6 to 6
Outputs:
- predicted: float32 [8, 8, 1, 77, 384], P('step', None, None, None, 'rows')
- grad_init: float32 [8, 1, 2, 77, 384], P('step', None, None, None, 'rows')
- grad_forcing: float32 [8, 1, 4, 384], P('step', None, None, 'rows')
- grad_w_in: float32 [800, 158], replicated
- grad_b_in: float32 [800], replicated
- grad_w_dw: float32 [800, 7, 7], replicated
- grad_bn_gain: float32 [800], replicated
- grad_bn_bias: float32 [800], replicated
- grad_w_up: float32 [3200, 800], P('step', 'rows')
- grad_b_up: float32 [3200], replicated
- grad_w_down: float32 [800, 3200], P('rows', 'step')
- grad_b_down: float32 [800], replicated
- grad_w_out: float32 [77, 800], replicated
- grad_b_out: float32 [77], replicated
The draws below stay inside these ranges and needn't reach their ends.
All inputs are finite; a program needn't handle non-finite values. No bound on the sum of `land_mask` on one device may be relied on, other than what follows from the above.
Results may differ from the reference program's by a relative error of at most 0.0003.
Values sent between devices are 32-bit elements; how exact they have to be, the bound alone decides.
No kernel may reach another device: no remote copies, remote signals or barrier semaphores. Data moves between devices by JAX's collectives and lax.ppermute only.
A program may use at most 448 MiB of HBM per device.

```python
import math
import jax
import jax.numpy as jnp
from jax import lax

C_S = 77
C_F = 4
C_IN = 158
D = 800
FF = 3200
KW = 7
HALO = 3
ROLL = 8
DATES = 1
COLS = 32
TIMES = 8
ROWS = 12
PIX = 384


def spatial_field(key, shape):
    key_values, key_columns = jax.random.split(key)
    row_index = (jnp.arange(PIX) // COLS).astype(jnp.float32)
    values = jnp.clip(jax.random.normal(key_values, shape, jnp.float32), -4.0, 4.0)
    ramp = 3.0 ** (row_index / (ROWS - 1))
    column_scale = jnp.exp(jax.random.uniform(key_columns, (COLS,), jnp.float32, 0.0, math.log(3.3)))
    return values * (ramp * jnp.tile(column_scale, ROWS))


def draw_init_states(key, part):
    return spatial_field(jax.random.fold_in(key, 11), (TIMES, DATES, 2, C_S, PIX))


def draw_forcing(key, part):
    return spatial_field(jax.random.fold_in(key, 23), (TIMES, DATES, C_F, PIX))


def plant(result, stream_key, smallest, top_value):
    shape = result.shape
    index_at = [jax.random.randint(jax.random.fold_in(stream_key, axis), (), 0, shape[axis]) for axis in range(len(shape))]
    result = result.at[tuple(index_at)].set(smallest)
    longest = shape.index(max(shape))
    index_at[longest] = (index_at[longest] + 1) % shape[longest]
    return result.at[tuple(index_at)].set(top_value)


def block_scale(rng, dims, cuts, smallest, largest):
    loudness = 1.0
    for dim, blocks in cuts:
        heights = jax.random.uniform(jax.random.fold_in(jax.random.fold_in(rng, 6), dim), (blocks,), jnp.float32, smallest / len(cuts), largest / len(cuts))
        loudness = loudness * jnp.repeat(jnp.exp(heights), dims[dim] // blocks).reshape((-1,) + (1,) * (len(dims) - 1 - dim))
    return loudness


def noise(rng, dims, deviation, limit, pieces=(), kind=jnp.bfloat16):
    drawn = deviation * jax.random.normal(rng, dims, jnp.float32)
    if pieces:
        drawn = drawn * block_scale(rng, dims, pieces, -0.22, 0.18)
    return jnp.clip(drawn, -limit, limit).astype(kind)


def setup_inputs(seed: int = 0) -> dict:
    keys = jax.random.split(jax.random.key(seed), 17)
    return {
        "init_states": draw_init_states(jax.random.fold_in(keys[16], 71), 0),
        "forcing": draw_forcing(jax.random.fold_in(keys[16], 71), 0),
        "history": plant(jax.random.randint(keys[2], (TIMES, DATES), 1, 3), jax.random.fold_in(keys[2], 1), 1, 2).astype(jnp.int32),
        "land_mask": plant((jax.random.randint(keys[3], (PIX,), 0, 10) < 7).astype(jnp.int32), jax.random.fold_in(keys[3], 1), 0, 1),
        "w_in": noise(keys[4], (D, C_IN), C_IN ** -0.5, 0.5, (), jnp.float32),
        "b_in": noise(keys[5], (D,), 0.3, 1.5, (), jnp.float32),
        "w_dw": noise(keys[6], (D, KW, KW), (KW * KW) ** -0.5, 0.875, (), jnp.float32),
        "bn_gain": jnp.clip(1.0 + 0.1 * jax.random.normal(keys[7], (D,), jnp.float32), 0.5, 1.5),
        "bn_bias": noise(keys[8], (D,), 0.3, 1.5, (), jnp.float32),
        "w_up": noise(keys[9], (FF, D), D ** -0.5, 0.21875, (), jnp.float32),
        "b_up": noise(keys[10], (FF,), 0.3, 1.5, (), jnp.float32),
        "w_down": noise(keys[11], (D, FF), FF ** -0.5, 0.109375, (), jnp.float32),
        "b_down": noise(keys[12], (D,), 0.3, 1.5, (), jnp.float32),
        "w_out": noise(keys[13], (C_S, D), D ** -0.5, 0.21875, (), jnp.float32),
        "b_out": noise(keys[14], (C_S,), 0.3, 1.5, (), jnp.float32),
        "cotangent": noise(keys[15], (TIMES, ROLL, DATES, C_S, PIX), 1.0, 6.0, ((0, 8), (4, 4)), jnp.float32),
    }


EPSILON = 1e-05
HIGHEST = lax.Precision.HIGHEST

@jax.custom_vjp
def low(v):
    return lax.optimization_barrier(v.astype(jnp.bfloat16)).astype(jnp.float32)

@jax.custom_vjp
def low_back(v):
    return v

def low_keep(v):
    return (low(v), None)

def low_pass(kept, grad):
    return (grad,)

def back_keep(v):
    return (v, None)

def back_low(kept, grad):
    return (low(grad),)
low.defvjp(low_keep, low_pass)
low_back.defvjp(back_keep, back_low)

def depthwise(extended, kernel):
    kernel_width = kernel.shape[-1]
    reach_rows = kernel_width // 2
    rows_out = extended.shape[-1] // COLS - 2 * reach_rows
    column = jnp.arange(extended.shape[-1]) % COLS
    accumulated = jnp.zeros(extended.shape[:-1] + (rows_out * COLS,), jnp.float32)
    for tap_col in range(kernel_width):
        offset = tap_col - reach_rows
        shifted = jnp.roll(extended, -offset, axis=-1)
        inside = (column + offset >= 0) & (column + offset < COLS)
        shifted = jnp.where(inside, shifted, jnp.zeros_like(shifted))
        for tap_row in range(kernel_width):
            piece = shifted[..., tap_row * COLS:(tap_row + rows_out) * COLS]
            accumulated = accumulated + kernel[:, tap_row, tap_col, None] * piece
    return accumulated

def contract(weights, values):
    return jnp.einsum('dc,bcp->bdp', weights, values, precision=HIGHEST)

def samudra_layer(params, inputs_all, ocean_mask):
    w_in, b_in, w_dw, bn_gain, bn_bias, w_up, b_up, w_down, b_down, w_out, b_out = params
    lifted = contract(w_in, inputs_all) + b_in[:, None]
    border = jnp.zeros(lifted.shape[:-1] + (HALO * COLS,), jnp.float32)
    mixed_cells = depthwise(jnp.concatenate([border, lifted, border], axis=-1), w_dw)
    ocean_count = jnp.maximum(jnp.sum(ocean_mask), 1.0)
    average = lax.optimization_barrier(jnp.sum(mixed_cells * ocean_mask, axis=-1)) / ocean_count
    variance = lax.optimization_barrier(jnp.sum(mixed_cells * mixed_cells * ocean_mask, axis=-1)) / ocean_count - average * average
    inverse_std = lax.rsqrt(variance + EPSILON)
    normalized = (mixed_cells - average[..., None]) * inverse_std[..., None]
    normed = normalized * bn_gain[:, None] + bn_bias[:, None]
    hidden_pre = contract(w_up, normed) + b_up[:, None]
    activated = jax.nn.gelu(hidden_pre, approximate=False)
    branch = contract(w_down, activated) + b_down[:, None]
    residual = (lifted + branch) * ocean_mask
    return (contract(w_out, residual) + b_out[:, None]) * ocean_mask

def rollout(params, init_values, forcing_values, history, ocean_mask):
    current = init_values[:, :, 1]
    previous = jnp.where((history == 2)[:, :, None, None], init_values[:, :, 0], init_values[:, :, 1])
    checkpointed = jax.checkpoint(samudra_layer)
    predictions = []
    for rollout_step in range(ROLL):
        forcing_now = jnp.roll(forcing_values, -rollout_step, axis=0)
        inputs_all = jnp.concatenate([previous, current, forcing_now], axis=2)
        flat_inputs = inputs_all.reshape((-1,) + inputs_all.shape[2:])
        new_state = checkpointed(params, flat_inputs, ocean_mask).reshape(current.shape)
        predictions.append(jnp.roll(new_state, rollout_step, axis=0))
        previous, current = (current, new_state)
    return jnp.stack(predictions, axis=1)

def reference(init_states, forcing, history, land_mask, w_in, b_in, w_dw, bn_gain, bn_bias, w_up, b_up, w_down, b_down, w_out, b_out, cotangent):
    ocean_mask = land_mask.astype(jnp.float32)
    params = (w_in, b_in, w_dw, bn_gain, bn_bias, w_up, b_up, w_down, b_down, w_out, b_out)

    def forward(init_values, forcing_values, weights):
        return rollout(weights, init_values, forcing_values, history, ocean_mask)
    predicted, pullback = jax.vjp(forward, init_states, forcing, params)
    grad_init, grad_forcing, gradients = pullback(cotangent)
    return (predicted, grad_init, grad_forcing, gradients[0], gradients[1], gradients[2], gradients[3], gradients[4], gradients[5], gradients[6], gradients[7], gradients[8], gradients[9], gradients[10])
```

```python
import functools

import jax
import jax.numpy as jnp
from jax import lax
from jax.experimental import pallas as pl
from jax.experimental.pallas import tpu as pltpu
from jax.sharding import PartitionSpec as P

F32 = jnp.float32
BF16 = jnp.bfloat16
HIGHEST = lax.Precision.HIGHEST
ROLL = 8
COLS = 32
KW = 7
HALO = 3
EPSILON = 1e-05
LANES = 128
CHUNK = 256
SEG = 80
FORCE_LANE = 80
MIB = 2**20

ERF_P = 0.39
ERF_C = (0.23532534, 0.09138764, 0.64956134, -0.63540268, 0.88666585, -0.22753749)


def round_up(value, multiple):
    return -(-value // multiple) * multiple


def split(values):
    high = values.astype(BF16)
    return high, (values - high.astype(F32)).astype(BF16)


def split_outside(values):
    rounded = lax.reduce_precision(values, 8, 7)
    return rounded.astype(BF16), (values - rounded).astype(BF16)


def dot(left, right):
    return jnp.dot(left, right, preferred_element_type=F32)


def dot_t(left, right):
    return lax.dot_general(left, right, (((1,), (1,)), ((), ())), preferred_element_type=F32)


def gelu_both(v):
    e = jnp.exp(v * v * (-0.5))
    t = 1.0 / (1.0 + (ERF_P * 0.7071067811865476) * jnp.abs(v))
    q = 0.5 * ERF_C[5]
    for coefficient in ERF_C[4::-1]:
        q = q * t + 0.5 * coefficient
    q = (q * t) * e
    phi = jnp.where(v >= 0.0, 1.0 - q, q)
    return v * phi, phi + v * (e * 0.3989422804014327)


def depthwise(ext, shifted, kernel, mixed, lanes, flip, rows):
    rows_in = rows + 2 * HALO
    for q in range(KW):
        for r in range(rows_in):
            shifted[q, r] = ext[r, 5 + q : 5 + q + COLS, lanes]
    for v in range(0, COLS, 8):
        total = [None] * rows
        for q in range(KW):
            taps = [
                kernel[(KW * KW - 1 - (p * KW + q)) if flip else (p * KW + q), :, lanes]
                for p in range(KW)
            ]
            for r in range(rows_in):
                cell = shifted[q, r, v : v + 8, :]
                for p in range(KW):
                    i = r - p
                    if 0 <= i < rows:
                        term = taps[p] * cell
                        total[i] = term if total[i] is None else total[i] + term
        for i in range(rows):
            mixed[i, v : v + 8, lanes] = total[i]


def group_lanes(group):
    return pl.ds(pl.multiple_of(group * LANES, LANES), LANES)


def mix_kernel(
    at, cur, cur_edge, prev, prev_edge, force, force_edge, w_in_hi, w_in_lo, b_in, w_oi_hi, w_oi_lo, b_new, taps, ocean,
    mixed_out, stats_out, window_out, x_out, base_out,
    ext, shifted, mixed,
):
    core, part = at[0], at[1]
    px = cur.shape[0]
    edge_px = cur_edge.shape[0]
    rows = px // COLS
    width = mixed_out.shape[1]
    own = jnp.concatenate([prev[...] + force[...], cur[...]], axis=1)
    edge = jnp.concatenate([prev_edge[...] + force_edge[...], cur_edge[...]], axis=1)
    own_hi, own_lo = split(own)
    edge_hi, edge_lo = split(edge)
    both = dot(jnp.concatenate([own_hi, edge_hi, own_lo, edge_lo], axis=0), w_in_hi[...])
    high = dot(jnp.concatenate([own_hi, edge_hi], axis=0), w_in_lo[...])
    lifted = (both[: px + edge_px] + both[px + edge_px :]) + (high + b_in[...])
    base_out[...] = dot(own_hi, w_oi_hi[...]) + dot(own_lo, w_oi_hi[...]) + dot(own_hi, w_oi_lo[...]) + b_new[...]
    zeros = jnp.zeros((rows + 2 * HALO, 8, width), F32)
    ext[:, :8, :] = zeros
    ext[:, 8 + COLS :, :] = zeros
    ext[HALO : HALO + rows, 8 : 8 + COLS, :] = lifted[:px].reshape(rows, COLS, width)
    ext[pl.ds((rows + HALO) * (1 - core), HALO), 8 : 8 + COLS, :] = lifted[px:].reshape(HALO, COLS, width)
    ext[pl.ds((rows + HALO) * core, HALO), 8 : 8 + COLS, :] = jnp.zeros((HALO, COLS, width), F32)
    part_rows = window_out.shape[0] - 2 * HALO
    for i in range(window_out.shape[0]):
        window_out[i] = ext[part * part_rows + i, 8 : 8 + COLS, :]
    part_px = x_out.shape[0]
    first = part == 0
    x_out[...] = jnp.where(first, own[:part_px], own[part_px:])
    mask = ocean[...]

    def group(g, _):
        lanes = group_lanes(g)
        depthwise(ext, shifted, taps, mixed, lanes, False, rows)
        cells = mixed[:, :, lanes].reshape(px, LANES)
        mixed_out[:, lanes] = cells
        masked = cells * mask
        stats_out[0:1, lanes] = jnp.sum(masked, axis=0, keepdims=True)
        stats_out[1:2, lanes] = jnp.sum(masked * cells, axis=0, keepdims=True)
        return 0

    lax.fori_loop(0, width // LANES, group, 0)


def feed_kernel(
    at, mixed, stats, stats_other, count, gain, bias, ocean, base, w_up, b_up, w_od,
    new_out, new_edge_out, norm_out, norm_edge_out, slope_out, act_out, inv_out,
    w_vmem, stack, rem, acc, acc_lo, hold_a, hold_b, hold_act, sems, *, width, k_main, k_rem,
):
    core, part = at[0], at[1]
    px = mixed.shape[0]
    chunks = w_vmem.shape[0] // CHUNK
    part_px = act_out.shape[0]

    def fetch(t):
        rows = pl.ds(pl.multiple_of(t * CHUNK, CHUNK), CHUNK)
        return pltpu.make_async_copy(w_up.at[rows], w_vmem.at[rows], sems.at[t])

    for t in range(chunks):
        fetch(t).start()
    total = count[...]

    for g in range(width // LANES):
        lanes = slice(g * LANES, (g + 1) * LANES)
        cells = mixed[:, lanes]
        average = (stats[0:1, lanes] + stats_other[0:1, lanes]) / total
        variance = (stats[1:2, lanes] + stats_other[1:2, lanes]) / total - average * average
        inverse = lax.rsqrt(variance + EPSILON)
        inv_out[:, lanes] = jnp.broadcast_to(inverse, (8, LANES))
        normalized = (cells - average) * inverse
        norm_out[:, lanes] = normalized
        normed = normalized * gain[:, lanes] + bias[:, lanes]
        high = normed.astype(BF16)
        high_f = high.astype(F32)
        low_f = normed - high_f
        if (g + 1) * LANES <= k_main:
            stack[:px, lanes] = high
            stack[px:, lanes] = low_f.astype(BF16)
        else:
            rem[...] = (high_f + pltpu.roll(low_f, k_rem, 1) + pltpu.roll(high_f, 2 * k_rem, 1)).astype(BF16)
    edge_px = norm_edge_out.shape[0]
    norm_edge_out[...] = norm_out[pl.ds(pl.multiple_of((1 - core) * (px - edge_px), 8), edge_px), :]

    def up(t, hold):
        fetch(t).wait()
        rows = pl.ds(pl.multiple_of(t * CHUNK, CHUNK), CHUNK)
        both = dot_t(stack[...], w_vmem[rows, :k_main])
        high = dot_t(stack[:px], w_vmem[rows, k_main : 2 * k_main])
        rest = dot_t(rem[...], w_vmem[rows, 2 * k_main :])
        hold[...] = (both[:px] + both[px:]) + (high + rest)

    def act(t, hold):
        cols = pl.ds(pl.multiple_of(t * CHUNK, CHUNK), CHUNK)
        activated, slope = gelu_both(hold[...] + b_up[:, cols])
        slope_out[:, cols] = slope
        hold_act[...] = activated
        high, low = split(activated)
        acc[...] += dot(high, w_od[cols, :])
        acc_lo[...] += dot(low, w_od[cols, :LANES])
        act_out[:, cols] = hold_act[pl.ds(pl.multiple_of(part * part_px, 8), part_px), :]

    acc[...] = jnp.zeros_like(acc)
    acc_lo[...] = base[...]
    up(0, hold_a)

    def pair(i, _):
        up(2 * i + 1, hold_b)
        act(2 * i, hold_a)
        up(2 * i + 2, hold_a)
        act(2 * i + 1, hold_b)
        return 0

    lax.fori_loop(0, chunks // 2, pair, 0)
    act(chunks - 1, hold_a)
    new_out[...] = (acc[:, :LANES] + acc[:, LANES:] + acc_lo[...]) * ocean[...]
    new_edge_out[...] = new_out[pl.ds(pl.multiple_of((1 - core) * (px - edge_px), 8), edge_px), :]


def back_kernel(*refs, finish, begin, width, k_main, k_rem, states):
    refs = list(refs)

    def take(count):
        out = refs[:count]
        del refs[:count]
        return out

    (at, ocean, pending_in) = take(3)
    if finish:
        (grad_n, sent, came, norm, norm_edge, inv, gain, ocean_edge, count, grad_branch, window, taps, w_in_hi, w_in_lo) = take(14)
    if begin:
        (cot, slope, norm_now, w_out, w_od, w_up) = take(6)
    if finish:
        (carry_out, pending_out, lift_out, taps_out) = take(4)
    if begin:
        (masked_out, branch_out, hidden_out, grad_n_out, send_out) = take(5)
    if finish:
        (ext, shifted, mixed, grad_lift) = take(4)
    if begin:
        (w_vmem, sems) = take(2)
    core, part = at[0], at[1]
    px = ocean.shape[0]
    rows = px // COLS
    if begin:
        blocks = sems.shape[0]
        block = w_vmem.shape[0] // blocks

        def fetch(t):
            here = pl.ds(t * block, block)
            return pltpu.make_async_copy(w_up.at[here], w_vmem.at[here], sems.at[t])

        for t in range(blocks):
            fetch(t).start()
    if finish:
        edge_px = norm_edge.shape[0]
        total = count[...]
        zeros = jnp.zeros((rows + 2 * HALO, 8, width), F32)
        ext[:, :8, :] = zeros
        ext[:, 8 + COLS :, :] = zeros
        ext[pl.ds((rows + HALO) * core, HALO), 8 : 8 + COLS, :] = jnp.zeros((HALO, COLS, width), F32)
        part_rows = window.shape[0] - 2 * HALO
        for g in range(width // LANES):
            lanes = slice(g * LANES, (g + 1) * LANES)
            bias_sum = (sent[edge_px : edge_px + 1, lanes] + came[edge_px : edge_px + 1, lanes]) / total
            gain_sum = (sent[edge_px + 1 : edge_px + 2, lanes] + came[edge_px + 1 : edge_px + 2, lanes]) / total
            scale = inv[0:1, lanes] * gain[:, lanes]
            mix = scale * (grad_n[:, lanes] - ocean[...] * (bias_sum + norm[:, lanes] * gain_sum))
            mix_edge = scale * (came[:edge_px, lanes] - ocean_edge[...] * (bias_sum + norm_edge[:, lanes] * gain_sum))
            ext[HALO : HALO + rows, 8 : 8 + COLS, lanes] = mix.reshape(rows, COLS, LANES)
            ext[pl.ds((rows + HALO) * (1 - core), HALO), 8 : 8 + COLS, lanes] = mix_edge.reshape(HALO, COLS, LANES)

        def group(g, _):
            lanes = group_lanes(g)
            depthwise(ext, shifted, taps, mixed, lanes, True, rows)
            grad_lift[:, lanes] = mixed[:, :, lanes].reshape(px, LANES) + grad_branch[:, lanes]
            for q in range(KW):
                sums = [None] * KW
                for i in range(part_rows):
                    for v in range(0, COLS, 8):
                        grad = shifted[KW - 1 - q, HALO + part * part_rows + i, v : v + 8, :]
                        for p in range(KW):
                            term = grad * window[i + p, v : v + 8, lanes]
                            sums[p] = term if sums[p] is None else sums[p] + term
                for p in range(KW):
                    taps_out[p * KW + q : p * KW + q + 1, lanes] = jnp.sum(sums[p], axis=0, keepdims=True)
            return 0

        lax.fori_loop(0, width // LANES, group, 0)
        part_px = lift_out.shape[0]
        lift_out[...] = grad_lift[pl.ds(pl.multiple_of(part * part_px, 8), part_px), :]
        high, low = split(grad_lift[...])
        both = dot_t(jnp.concatenate([high, low], axis=0), w_in_hi[...])
        grad_x = (both[:px] + both[px:]) + dot_t(high, w_in_lo[...])
        carry = grad_x[:, LANES:] + pending_in[...]
        carry_out[...] = carry
        pending_out[...] = grad_x[:, :LANES]
    if begin:
        grad_new = cot[...] + carry if finish else cot[...]
        lane = lax.broadcasted_iota(jnp.int32, (px, LANES), 1)
        masked = jnp.where(lane < states, grad_new * ocean[...], 0.0)
        masked_out[...] = masked
        high_f = masked.astype(BF16).astype(F32)
        nothing = jnp.zeros((px, LANES), F32)
        high_w = jnp.concatenate([high_f, nothing], axis=1)
        low_w = jnp.concatenate([masked - high_f, nothing], axis=1)
        left = (high_w + pltpu.roll(low_w, SEG, 1) + pltpu.roll(high_w, 2 * SEG, 1)).astype(BF16)
        branch_out[...] = dot(left, w_out[...])
        chunks = w_od.shape[1] // CHUNK

        def chunk(t, _):
            cols = pl.ds(pl.multiple_of(t * CHUNK, CHUNK), CHUNK)
            high, low = split(dot(left, w_od[:, cols]) * slope[:, cols])
            hidden_out[:px, cols] = high
            hidden_out[px:, cols] = low
            return 0

        lax.fori_loop(0, chunks, chunk, 0)
        for t in range(blocks):
            fetch(t).wait()
        both = dot(hidden_out[...], w_vmem[:, :k_main])
        grad_n_out[:, :k_main] = (both[:px] + both[px:]) + dot(hidden_out[:px], w_vmem[:, k_main : 2 * k_main])
        rest = dot(hidden_out[...], w_vmem[:, 2 * k_main :])
        tail = rest[:px] + rest[px:] + pltpu.roll(rest[:px], LANES - 2 * k_rem, 1)
        grad_n_out[:, k_main:] = jnp.where(lane < k_rem, tail, 0.0)
        edge_px = send_out.shape[0] - 8
        for g in range(width // LANES):
            lanes = slice(g * LANES, (g + 1) * LANES)
            cells = grad_n_out[:, lanes]
            send_out[edge_px : edge_px + 1, lanes] = jnp.sum(cells, axis=0, keepdims=True)
            send_out[edge_px + 1 : edge_px + 2, lanes] = jnp.sum(cells * norm_now[:, lanes], axis=0, keepdims=True)
        send_out[:edge_px, :] = grad_n_out[pl.ds(pl.multiple_of((1 - core) * (px - edge_px), 8), edge_px), :]


def weight_kernel(n_pair, n_low, hidden, acc_in, acc_out):
    px = n_low.shape[1]

    def chunk(t, _):
        cols = pl.ds(pl.multiple_of(t * CHUNK, CHUNK), CHUNK)
        acc_out[:, cols] = acc_in[:, cols] + (dot(n_pair[...], hidden[:, cols]) + dot(n_low[...], hidden[:px, cols]))
        return 0

    lax.fori_loop(0, hidden.shape[1] // CHUNK, chunk, 0)


VMEM_SPEC = pl.BlockSpec(memory_space=pltpu.VMEM)
SMEM_SPEC = pl.BlockSpec(memory_space=pltpu.SMEM)
ANY_SPEC = pl.BlockSpec(memory_space=pl.ANY)


def out(*shape, dtype=F32):
    return jax.ShapeDtypeStruct(shape, dtype)


def call(kernel, name, args, specs, outs, scratch, limit, aliases=None):
    return pl.pallas_call(
        kernel,
        in_specs=specs,
        out_specs=[VMEM_SPEC] * len(outs),
        out_shape=outs,
        scratch_shapes=scratch,
        input_output_aliases=aliases or {},
        compiler_params=pltpu.CompilerParams(vmem_limit_bytes=limit * MIB),
        name=name,
    )(*args)


def pad_to(values, shape):
    return jnp.pad(values, [(0, size - have) for size, have in zip(shape, values.shape)])


def per_device(
    init_states, forcing, history, land_mask, w_in, b_in, w_dw, bn_gain, bn_bias, w_up, b_up, w_down, b_down, w_out, b_out, cotangent
):
    steps = lax.axis_size("step")
    devices_z = lax.axis_size("rows")
    step = lax.axis_index("step")
    depth = lax.axis_index("rows")
    core, pair = step % 2, step // 2
    side, part = depth % 2, depth // 2
    both_axes = ("step", "rows")
    block = land_mask.shape[0]
    px = 2 * block
    rows = px // COLS
    states = w_out.shape[0]
    forces = forcing.shape[2]
    channels = w_up.shape[1]
    hidden = w_up.shape[0]
    width = round_up(channels, LANES)
    wide = round_up(hidden, CHUNK)
    k_main = channels // CHUNK * CHUNK
    k_rem = channels - k_main
    col_block = channels // devices_z
    ff_block = hidden // steps

    def place(s, z):
        return s * devices_z + z

    cells = [(k, c, h, q) for k in range(steps // 2) for c in range(2) for h in range(2) for q in range(2)]
    fetch_perms = [
        [(place(2 * k + q, 2 * c + (b ^ h)), place(2 * k + c, 2 * h + q)) for k, c, h, q in cells] for b in range(2)
    ]

    def home_perm(j):
        return [(place(2 * k + c, 2 * h + q), place((2 * k + q + j) % steps, 2 * c + h)) for k, c, h, q in cells]

    siblings = [(s, s ^ 1) for s in range(steps)]

    def to_sibling(values):
        return lax.ppermute(values, "step", siblings)

    def shift_back(values, j):
        return values if j == 0 else lax.ppermute(values, "step", [((s + j) % steps, s) for s in range(steps)])

    def fetch_own(values):
        got = [lax.ppermute(values, both_axes, perm) for perm in fetch_perms]
        swap = part == 1
        return jnp.concatenate([jnp.where(swap, got[1], got[0]), jnp.where(swap, got[0], got[1])], axis=-1)

    def my_part(values, axis):
        return lax.dynamic_slice_in_dim(values, part * (values.shape[axis] // 2), values.shape[axis] // 2, axis)

    mask_row = land_mask.astype(F32)[None]
    current = init_states[0, 0, 1]
    previous = jnp.where(history[0, 0] == 2, init_states[0, 0, 0], current)
    forced = [shift_back(forcing[0, 0], j) for j in range(ROLL)]
    payload = fetch_own(jnp.concatenate([previous, current, mask_row] + forced, axis=0))
    local_count = jnp.sum(payload[2 * states])
    edge = jnp.where(core == 0, payload[:, block:], payload[:, :block])
    edge = to_sibling(jnp.concatenate([edge, jnp.full((1, block), local_count)], axis=0))
    count = jnp.full((1, LANES), jnp.maximum(local_count + edge[-1, 0], 1.0))

    def state_lanes(values):
        return pad_to(values.T, (values.shape[1], LANES))

    def force_lanes(values):
        return jnp.pad(values.T, ((0, 0), (FORCE_LANE, LANES - FORCE_LANE - forces)))

    def mask_lanes(values):
        return jnp.broadcast_to(values[:, None], (values.shape[0], LANES))

    prev, cur = state_lanes(payload[:states]), state_lanes(payload[states : 2 * states])
    prev_edge, cur_edge = state_lanes(edge[:states]), state_lanes(edge[states : 2 * states])
    ocean, ocean_edge = mask_lanes(payload[2 * states]), mask_lanes(edge[2 * states])
    base_row = 2 * states + 1
    force = [force_lanes(payload[base_row + forces * j : base_row + forces * (j + 1)]) for j in range(ROLL)]
    force_edge = [force_lanes(edge[base_row + forces * j : base_row + forces * (j + 1)]) for j in range(ROLL)]

    def in_rows(values):
        rest = LANES - FORCE_LANE - forces
        top = jnp.pad(values[:states], ((0, FORCE_LANE - states), (0, 0)))
        force_rows = jnp.pad(values[2 * states :], ((0, rest), (0, 0)))
        bottom = jnp.pad(values[states : 2 * states], ((0, LANES - states), (0, 0)))
        return jnp.concatenate([top, force_rows, bottom], axis=0)

    def row(values, size):
        return jnp.pad(values, (0, size - values.shape[0]))[None]

    w_in_hi, w_in_lo = split_outside(pad_to(in_rows(w_in.T), (2 * LANES, width)))
    w_oi = pad_to(in_rows(jnp.dot(w_out, w_in, precision=HIGHEST).T), (2 * LANES, LANES))
    w_oi_hi, w_oi_lo = split_outside(w_oi)
    b_new = row(jnp.dot(w_out, b_in + b_down, precision=HIGHEST) + b_out, LANES)
    taps = jnp.broadcast_to(
        pad_to(w_dw.reshape(channels, KW * KW).T, (KW * KW, width))[:, None], (KW * KW, 8, width)
    )
    gain, bias = row(bn_gain, width), row(bn_bias, width)
    up_hi, up_lo = split_outside(w_up)
    w_up_all = pad_to(
        jnp.concatenate(
            [up_hi[:, :k_main], up_lo[:, :k_main], up_hi[:, k_main:], up_hi[:, k_main:], up_lo[:, k_main:]], axis=1
        ),
        (wide, 2 * k_main + LANES),
    )
    w_od = jnp.dot(w_out, w_down, precision=HIGHEST)
    od_hi, od_lo = split_outside(pad_to(w_od, (SEG, wide)))
    w_od_fwd = jnp.concatenate([pad_to(od_hi, (LANES, wide)).T, pad_to(od_lo, (LANES, wide)).T], axis=1)
    w_od_bwd = pad_to(jnp.concatenate([od_hi, od_hi, od_lo], axis=0), (2 * LANES, wide))
    out_hi, out_lo = split_outside(pad_to(w_out, (SEG, width)))
    w_out_bwd = pad_to(jnp.concatenate([out_hi, out_hi, out_lo], axis=0), (2 * LANES, width))
    b_in_row, b_up_row = row(b_in, width), row(b_up, wide)
    at = jnp.stack([core, part]).astype(jnp.int32)

    cots = fetch_own(jnp.stack([shift_back(cotangent[0, j, 0], j) for j in range(ROLL)]))
    cots = jnp.pad(jnp.swapaxes(cots, 1, 2), ((0, 0), (0, 0), (0, LANES - states)))

    kept, predicted = [], []
    for j in range(ROLL):
        mixed, stats, window, x_part, base = call(
            mix_kernel, "mix",
            (at, cur, cur_edge, prev, prev_edge, force[j], force_edge[j], w_in_hi, w_in_lo, b_in_row, w_oi_hi, w_oi_lo, b_new, taps, ocean),
            [SMEM_SPEC] + [VMEM_SPEC] * 14,
            [out(px, width), out(8, width), out(3 + 2 * HALO, COLS, width), out(block, 2 * LANES), out(px, LANES)],
            [pltpu.VMEM((rows + 2 * HALO, COLS + 16, width), F32), pltpu.VMEM((KW, rows + 2 * HALO, COLS, LANES), F32), pltpu.VMEM((rows, COLS, width), F32)],
            24,
        )
        stats_other = to_sibling(stats)
        new, new_edge, norm, norm_edge, slope, act, inv = call(
            functools.partial(feed_kernel, width=width, k_main=k_main, k_rem=k_rem), "feed",
            (at, mixed, stats, stats_other, count, gain, bias, ocean, base, w_up_all, b_up_row, w_od_fwd),
            [SMEM_SPEC] + [VMEM_SPEC] * 8 + [ANY_SPEC] + [VMEM_SPEC] * 2,
            [out(px, LANES), out(block, LANES), out(px, width), out(block, width), out(px, wide), out(block, wide), out(8, width)],
            [
                pltpu.VMEM(w_up_all.shape, BF16), pltpu.VMEM((2 * px, k_main), BF16), pltpu.VMEM((px, LANES), BF16),
                pltpu.VMEM((px, CHUNK), F32), pltpu.VMEM((px, LANES), F32), pltpu.VMEM((px, CHUNK), F32), pltpu.VMEM((px, CHUNK), F32),
                pltpu.VMEM((px, CHUNK), F32), pltpu.SemaphoreType.DMA((wide // CHUNK,)),
            ],
            36,
        )
        norm_edge = to_sibling(norm_edge)
        prev, prev_edge, cur = cur, cur_edge, new
        if j < ROLL - 1:
            cur_edge = to_sibling(new_edge)
        predicted.append(lax.ppermute(my_part(new, 0)[:, :states].T, both_axes, home_perm(j)))
        kept.append((window, x_part, norm, norm_edge, slope, act, inv))

    quarter = channels // 2
    gain_q = lax.dynamic_slice_in_dim(bn_gain, part * quarter, quarter)
    bias_q = lax.dynamic_slice_in_dim(bn_bias, part * quarter, quarter)
    acc_rows = round_up(quarter + 1, 8)
    acc = jnp.zeros((acc_rows, wide), F32)
    carry, pending = None, jnp.zeros((px, LANES), F32)
    previous_step = None
    masked_parts, lifts, tap_sums, stat_sums, force_grads = [], [], [], [], []
    begin_scratch = [pltpu.VMEM(w_up_all.shape, BF16), pltpu.SemaphoreType.DMA((4,))]
    finish_scratch = [
        pltpu.VMEM((rows + 2 * HALO, COLS + 16, width), F32), pltpu.VMEM((KW, rows + 2 * HALO, COLS, LANES), F32),
        pltpu.VMEM((rows, COLS, width), F32), pltpu.VMEM((px, width), F32),
    ]
    for j in range(ROLL - 1, -2, -1):
        finish, begin = j < ROLL - 1, j >= 0
        args, specs, outs, scratch = [at, ocean, pending], [SMEM_SPEC, VMEM_SPEC, VMEM_SPEC], [], []
        if finish:
            window, x_part, norm, norm_edge, slope, act, inv = kept[j + 1]
            grad_n, sent, came, grad_branch = previous_step
            args += [grad_n, sent, came, norm, norm_edge, inv, gain, ocean_edge, count, grad_branch, window, taps, w_in_hi, w_in_lo]
            specs += [VMEM_SPEC] * 14
            outs += [out(px, LANES), out(px, LANES), out(block, width), out(round_up(KW * KW, 8), width)]
            scratch += finish_scratch
        if begin:
            args += [cots[j], kept[j][4], kept[j][2], w_out_bwd, w_od_bwd, w_up_all]
            specs += [VMEM_SPEC] * 5 + [ANY_SPEC]
            outs += [out(px, LANES), out(px, width), out(2 * px, wide, dtype=BF16), out(px, width), out(block + 8, width)]
            scratch += begin_scratch
        results = list(
            call(
                functools.partial(
                    back_kernel, finish=finish, begin=begin, width=width, k_main=k_main, k_rem=k_rem, states=states
                ),
                "back", args, specs, outs, scratch, 48,
            )
        )
        if finish:
            carry, pending, lift, tap_sum = results[:4]
            results = results[4:]
            lifts.append(lift)
            tap_sums.append(tap_sum)
            gone = my_part(pending, 0)[:, FORCE_LANE : FORCE_LANE + forces].T
            if j + 1 > 0:
                force_grads.append(lax.ppermute(gone, both_axes, home_perm(j + 1)))
        if begin:
            masked, grad_branch, hidden_now, grad_n, sent = results
            came = to_sibling(sent)
            previous_step = (grad_n, sent, came, grad_branch)
            masked_parts.append(my_part(masked, 0))
            stat_sums.append(sent[block:])
            n_q = lax.dynamic_slice_in_dim(kept[j][2], part * quarter, quarter, axis=1) * gain_q + bias_q
            n_t = jnp.concatenate([n_q.T, jnp.ones((1, px), F32), jnp.zeros((acc_rows - quarter - 1, px), F32)], axis=0)
            n_hi, n_lo = split_outside(n_t)
            (acc,) = call(
                weight_kernel, "weight", (jnp.concatenate([n_hi, n_hi], axis=1), n_lo, hidden_now, acc),
                [VMEM_SPEC] * 4, [out(acc_rows, wide)], [], 24, aliases={3: 0},
            )

    def total(values):
        return functools.reduce(jnp.add, values)

    last = jnp.concatenate([my_part(pending, 0)[:, :states], my_part(carry, 0)[:, :states], gone.T], axis=1).T
    last = lax.ppermute(last, both_axes, home_perm(0))
    grad_prev, grad_cur, gone = last[:states], last[states : 2 * states], last[2 * states :]
    grad_forcing = total(force_grads + [gone])[None, None]
    grad_init_prev = jnp.where(history[0, 0] == 2, grad_prev, 0.0)
    grad_init_cur = grad_cur + jnp.where(history[0, 0] == 1, grad_prev, 0.0)
    grad_init = jnp.stack([grad_init_prev, grad_init_cur])[None, None]

    order = range(ROLL - 1, -1, -1)
    masked_all = jnp.concatenate([m[:, :states] for m in masked_parts], axis=0)
    act_all = jnp.concatenate([kept[j][5][:, :hidden] for j in order], axis=0)
    lift_in = jnp.concatenate(
        [kept[j][0][HALO : 2 * HALO, :, :channels].reshape(block, channels) for j in order], axis=0
    )
    x_all = jnp.concatenate([kept[j][1] for j in order], axis=0)
    lift_all = jnp.concatenate([g[:, :channels] for g in lifts], axis=0)

    def outer(a, b):
        return lax.dot_general(a, b, (((0,), (0,)), ((), ())), precision=lax.Precision.HIGH, preferred_element_type=F32)

    hidden_out = outer(masked_all, act_all)
    masked_sum = jnp.sum(masked_all, axis=0)
    g_out = (
        outer(masked_all, lift_in)
        + lax.dot_general(hidden_out, w_down, (((1,), (1,)), ((), ())), precision=lax.Precision.HIGH, preferred_element_type=F32)
        + masked_sum[:, None] * b_down
    )
    g_in = outer(lift_all, x_all)
    g_in = jnp.concatenate(
        [g_in[:, :states], g_in[:, LANES : LANES + states], g_in[:, FORCE_LANE : FORCE_LANE + forces]], axis=1
    )
    first = (part == 0).astype(F32)
    stats = total(stat_sums)[:2, :channels] * first
    small = [
        g_in, jnp.sum(lift_all, axis=0), total(tap_sums)[: KW * KW, :channels].T, stats[1], stats[0],
        acc[quarter, :hidden] * first, jnp.zeros((0,), F32), g_out, masked_sum,
    ]
    flat = lax.psum(jnp.concatenate([v.reshape(-1) for v in small]), both_axes)
    pieces, offset = [], 0
    for v in small:
        pieces.append(flat[offset : offset + v.size].reshape(v.shape))
        offset += v.size
    g_w_in, g_b_in, g_w_dw, g_gain, g_bias, g_b_up, _, g_w_out, g_b_out = pieces
    g_b_down = jnp.sum(w_out * g_b_out[:, None], axis=0)

    share = lax.psum_scatter(acc[:quarter, :hidden], "step", scatter_dimension=1, tiled=True)
    mine = lax.dynamic_slice_in_dim(share, side * col_block, col_block, axis=0)
    other = lax.dynamic_slice_in_dim(share, (1 - side) * col_block, col_block, axis=0)
    share_up = (mine + lax.ppermute(other, "rows", [(z, z ^ 1) for z in range(devices_z)])).T
    hidden_share = lax.psum(lax.psum_scatter(hidden_out, "step", scatter_dimension=1, tiled=True), "rows")
    w_out_block = lax.dynamic_slice_in_dim(w_out, depth * col_block, col_block, axis=1)
    share_down = outer(w_out_block, hidden_share)
    return (
        jnp.stack(predicted)[None, :, None],
        grad_init,
        grad_forcing,
        g_w_in,
        g_b_in,
        g_w_dw.reshape(channels, KW, KW),
        g_gain,
        g_bias,
        share_up,
        g_b_up,
        share_down,
        g_b_down,
        g_w_out,
        g_b_out,
    )


def solution(mesh):
    state_spec = P("step", None, None, None, "rows")
    force_spec = P("step", None, None, "rows")
    in_specs = (state_spec, force_spec, P("step", None), P("rows")) + (P(),) * 11 + (state_spec,)
    out_specs = (state_spec, state_spec, force_spec) + (P(),) * 5 + (P("step", "rows"), P(), P("rows", "step"), P(), P(), P())
    return jax.shard_map(per_device, mesh=mesh, in_specs=in_specs, out_specs=out_specs, check_vma=False)
```

```python
import functools

import jax
import jax.numpy as jnp
from jax import lax
from jax.experimental import pallas as pl
from jax.experimental.pallas import tpu as pltpu
from jax.sharding import PartitionSpec as P

F32 = jnp.float32
BF16 = jnp.bfloat16
HIGHEST = lax.Precision.HIGHEST
ROLL = 8
COLS = 32
KW = 7
HALO = 3
EPSILON = 1e-05
LANES = 128
CHUNK = 256
SEG = 80
MIB = 2**20

ERF_P = 0.39
ERF_C = (0.23532534, 0.09138764, 0.64956134, -0.63540268, 0.88666585, -0.22753749)


def round_up(value, multiple):
    return -(-value // multiple) * multiple


def split(values):
    high = values.astype(BF16)
    return high, (values - high.astype(F32)).astype(BF16)


def split_outside(values):
    rounded = lax.reduce_precision(values, 8, 7)
    return rounded.astype(BF16), (values - rounded).astype(BF16)


def dot(left, right):
    return jnp.dot(left, right, preferred_element_type=F32)


def dot_t(left, right):
    return lax.dot_general(left, right, (((1,), (1,)), ((), ())), preferred_element_type=F32)


def gelu_both(v):
    e = jnp.exp(v * v * (-0.5))
    t = 1.0 / (1.0 + (ERF_P * 0.7071067811865476) * jnp.abs(v))
    q = 0.5 * ERF_C[5]
    for coefficient in ERF_C[4::-1]:
        q = q * t + 0.5 * coefficient
    q = (q * t) * e
    phi = jnp.where(v >= 0.0, 1.0 - q, q)
    return v * phi, phi + v * (e * 0.3989422804014327)


def depthwise(ext, shifted, kernel, mixed, lanes, flip, rows):
    rows_in = rows + 2 * HALO
    for q in range(KW):
        for r in range(rows_in):
            shifted[q, r] = ext[r, 5 + q : 5 + q + COLS, lanes]
    for v in range(0, COLS, 8):
        total = [None] * rows
        for q in range(KW):
            taps = [
                kernel[(KW * KW - 1 - (p * KW + q)) if flip else (p * KW + q), :, lanes]
                for p in range(KW)
            ]
            for r in range(rows_in):
                cell = shifted[q, r, v : v + 8, :]
                for p in range(KW):
                    i = r - p
                    if 0 <= i < rows:
                        term = taps[p] * cell
                        total[i] = term if total[i] is None else total[i] + term
        for i in range(rows):
            mixed[i, v : v + 8, lanes] = total[i]


def ocean_count(sent, came):
    last = sent.shape[0] - 1
    return jnp.maximum(sent[last:, :LANES] + came[last:, :LANES], 1.0)


def group_lanes(group):
    return pl.ds(pl.multiple_of(group * LANES, LANES), LANES)


def mix_kernel(
    at, cur, cur_edge, prev, prev_edge, force, force_edge, w_in_hi, w_in_lo, b_in, w_oi_hi, w_oi_lo, b_new, taps, ocean,
    mixed_out, stats_out, base_out, window_out, x_all, lifted_all,
    ext, shifted, mixed, x_part, sems, *, turn, cur_lanes, prev_lanes,
):
    core, part = at[0], at[1]
    px = cur.shape[0]
    edge_px = x_part.shape[0]
    rows = px // COLS
    width = mixed_out.shape[1]
    prev_now, prev_edge_now = prev[...], prev_edge[:edge_px, prev_lanes : prev_lanes + LANES]
    if turn:
        prev_now, prev_edge_now = prev_now + force[turn], prev_edge_now + force_edge[turn]
    own = jnp.concatenate([prev_now, cur[...]], axis=1)
    edge = jnp.concatenate([prev_edge_now, cur_edge[:edge_px, cur_lanes : cur_lanes + LANES]], axis=1)
    own_hi, own_lo = split(own)
    edge_hi, edge_lo = split(edge)
    both = dot(jnp.concatenate([own_hi, edge_hi, own_lo, edge_lo], axis=0), w_in_hi[...])
    high = dot(jnp.concatenate([own_hi, edge_hi], axis=0), w_in_lo[...])
    lifted = (both[: px + edge_px] + both[px + edge_px :]) + (high + b_in[...])
    base_out[...] = dot(own_hi, w_oi_hi[...]) + dot(own_lo, w_oi_hi[...]) + dot(own_hi, w_oi_lo[...]) + b_new[...]
    zeros = jnp.zeros((rows + 2 * HALO, 8, width), F32)
    ext[:, :8, :] = zeros
    ext[:, 8 + COLS :, :] = zeros
    ext[HALO : HALO + rows, 8 : 8 + COLS, :] = lifted[:px].reshape(rows, COLS, width)
    ext[pl.ds((rows + HALO) * (1 - core), HALO), 8 : 8 + COLS, :] = lifted[px:].reshape(HALO, COLS, width)
    ext[pl.ds((rows + HALO) * core, HALO), 8 : 8 + COLS, :] = jnp.zeros((HALO, COLS, width), F32)
    part_rows = window_out.shape[0] - 2 * HALO
    part_px = x_part.shape[0]
    x_part[...] = jnp.where(part == 0, own[:part_px], own[part_px:])
    here = pl.ds(turn * part_rows, part_rows)
    keeps = [
        pltpu.make_async_copy(ext.at[pl.ds(part * part_rows, window_out.shape[0]), 8 : 8 + COLS, :], window_out, sems.at[0]),
        pltpu.make_async_copy(ext.at[pl.ds(part * part_rows + HALO, part_rows), 8 : 8 + COLS, :], lifted_all.at[here], sems.at[1]),
        pltpu.make_async_copy(x_part, x_all.at[pl.ds(turn * part_px, part_px)], sems.at[2]),
    ]
    for keep in keeps:
        keep.start()
    mask = ocean[...]

    def group(g, _):
        lanes = group_lanes(g)
        depthwise(ext, shifted, taps, mixed, lanes, False, rows)
        cells = mixed[:, :, lanes].reshape(px, LANES)
        mixed_out[:, lanes] = cells
        masked = cells * mask
        stats_out[0:1, lanes] = jnp.sum(masked, axis=0, keepdims=True)
        stats_out[1:2, lanes] = jnp.sum(masked * cells, axis=0, keepdims=True)
        return 0

    lax.fori_loop(0, width // LANES, group, 0)
    for keep in keeps:
        keep.wait()


def feed_kernel(
    at, mixed, stats, stats_other, sent, came, gain, bias, ocean, base, w_up, b_up, w_od,
    new_out, new_edge_out, state_out, norm_edge_out, inv_out, norm_out, slope_out, act_all,
    stack, rem, acc, acc_lo, hold_a, hold_b, hold_act, norm, slope, act_part, sems, *, turn, width, k_main, k_rem,
):
    core, part = at[0], at[1]
    px = mixed.shape[0]
    chunks = w_up.shape[1] // CHUNK
    part_px = act_part.shape[1]
    total = ocean_count(sent, came)
    keep_norm = pltpu.make_async_copy(norm, norm_out, sems.at[2 * chunks])

    for g in range(width // LANES):
        lanes = slice(g * LANES, (g + 1) * LANES)
        cells = mixed[:, lanes]
        average = (stats[0:1, lanes] + stats_other[0:1, lanes]) / total
        variance = (stats[1:2, lanes] + stats_other[1:2, lanes]) / total - average * average
        inverse = lax.rsqrt(variance + EPSILON)
        inv_out[:, lanes] = jnp.broadcast_to(inverse, (8, LANES))
        normalized = (cells - average) * inverse
        norm[:, lanes] = normalized
        normed = normalized * gain[:, lanes] + bias[:, lanes]
        high = normed.astype(BF16)
        high_f = high.astype(F32)
        low_f = normed - high_f
        if (g + 1) * LANES <= k_main:
            stack[:px, lanes] = high
            stack[px:, lanes] = low_f.astype(BF16)
        else:
            rem[...] = (high_f + pltpu.roll(low_f, k_rem, 1) + pltpu.roll(high_f, 2 * k_rem, 1)).astype(BF16)
    keep_norm.start()
    edge_px = norm_edge_out.shape[0]
    norm_edge_out[...] = norm[pl.ds(pl.multiple_of((1 - core) * (px - edge_px), 8), edge_px), :]

    def up(t, hold):
        cols = pl.ds(pl.multiple_of(t * CHUNK, CHUNK), CHUNK)
        both = dot(stack[...], w_up[:k_main, cols])
        high = dot(stack[:px], w_up[k_main : 2 * k_main, cols])
        rest = dot(rem[...], w_up[2 * k_main :, cols])
        hold[...] = (both[:px] + both[px:]) + (high + rest)

    def keep_slope(t):
        return pltpu.make_async_copy(slope.at[t], slope_out.at[t], sems.at[t])

    def keep_act(t):
        return pltpu.make_async_copy(act_part.at[t], act_all.at[t, pl.ds(turn * part_px, part_px)], sems.at[chunks + t])

    def act(t, hold):
        cols = pl.ds(pl.multiple_of(t * CHUNK, CHUNK), CHUNK)
        activated, slope[t] = gelu_both(hold[...] + b_up[:, cols])
        hold_act[...] = activated
        high, low = split(activated)
        acc[...] += dot(high, w_od[cols, :])
        acc_lo[...] += dot(low, w_od[cols, :LANES])
        act_part[t] = hold_act[pl.ds(pl.multiple_of(part * part_px, 8), part_px), :]
        keep_slope(t).start()
        keep_act(t).start()

    acc[...] = jnp.zeros_like(acc)
    acc_lo[...] = base[...]
    up(0, hold_a)

    def pair(i, _):
        up(2 * i + 1, hold_b)
        act(2 * i, hold_a)
        up(2 * i + 2, hold_a)
        act(2 * i + 1, hold_b)
        return 0

    lax.fori_loop(0, chunks // 2, pair, 0)
    act(chunks - 1, hold_a)
    new = (acc[:, :LANES] + acc[:, LANES:] + acc_lo[...]) * ocean[...]
    new_out[...] = new
    new_edge_out[...] = new_out[pl.ds(pl.multiple_of((1 - core) * (px - edge_px), 8), edge_px), :]
    mine = jnp.where(part == 0, new[:part_px], new[part_px:])
    state_out[...] = mine.T[: state_out.shape[0]]
    keep_norm.wait()
    for t in range(chunks):
        keep_slope(t).wait()
        keep_act(t).wait()


def back_kernel(*refs, finish, begin, turn, width, k_main, k_rem, states):
    refs = list(refs)

    def take(count):
        out = refs[:count]
        del refs[:count]
        return out

    (at, ocean, pending_in) = take(3)
    if finish:
        (grad_n, sent, came, norm, norm_edge, inv, gain, first_sent, first_came, grad_branch, window, taps, w_in_hi, w_in_lo) = take(14)
    if begin:
        (cots, slope_hbm, norm_now, w_out, w_od, w_up) = take(6)
    if finish:
        (carry_out, pending_out, taps_out, home_out, lift_all) = take(5)
    if begin:
        (branch_out, hidden_out, grad_n_out, send_out, masked_all) = take(5)
    if finish:
        (ext, shifted, mixed, grad_lift, lift_sem) = take(5)
    if begin:
        (cot, slope, masked_part, begin_sems) = take(4)
    core, part = at[0], at[1]
    px = ocean.shape[0]
    rows = px // COLS
    part_px = px // 2
    if begin:
        get_cot = pltpu.make_async_copy(cots.at[turn], cot, begin_sems.at[0])
        get_slope = pltpu.make_async_copy(slope_hbm, slope, begin_sems.at[1])
        get_cot.start()
        get_slope.start()
    if finish:
        edge_px = norm_edge.shape[0]
        total = ocean_count(first_sent, first_came)
        ocean_edge = first_came[:edge_px, 2 * LANES :]
        zeros = jnp.zeros((rows + 2 * HALO, 8, width), F32)
        ext[:, :8, :] = zeros
        ext[:, 8 + COLS :, :] = zeros
        ext[pl.ds((rows + HALO) * core, HALO), 8 : 8 + COLS, :] = jnp.zeros((HALO, COLS, width), F32)
        part_rows = window.shape[0] - 2 * HALO
        for g in range(width // LANES):
            lanes = slice(g * LANES, (g + 1) * LANES)
            bias_sum = (sent[edge_px : edge_px + 1, lanes] + came[edge_px : edge_px + 1, lanes]) / total
            gain_sum = (sent[edge_px + 1 : edge_px + 2, lanes] + came[edge_px + 1 : edge_px + 2, lanes]) / total
            scale = inv[0:1, lanes] * gain[:, lanes]
            mix = scale * (grad_n[:, lanes] - ocean[...] * (bias_sum + norm[:, lanes] * gain_sum))
            mix_edge = scale * (came[:edge_px, lanes] - ocean_edge * (bias_sum + norm_edge[:, lanes] * gain_sum))
            ext[HALO : HALO + rows, 8 : 8 + COLS, lanes] = mix.reshape(rows, COLS, LANES)
            ext[pl.ds((rows + HALO) * (1 - core), HALO), 8 : 8 + COLS, lanes] = mix_edge.reshape(HALO, COLS, LANES)

        def group(g, _):
            lanes = group_lanes(g)
            depthwise(ext, shifted, taps, mixed, lanes, True, rows)
            grad_lift[:, lanes] = mixed[:, :, lanes].reshape(px, LANES) + grad_branch[:, lanes]
            for q in range(KW):
                sums = [None] * KW
                for i in range(part_rows):
                    for v in range(0, COLS, 8):
                        grad = shifted[KW - 1 - q, HALO + part * part_rows + i, v : v + 8, :]
                        for p in range(KW):
                            term = grad * window[i + p, v : v + 8, lanes]
                            sums[p] = term if sums[p] is None else sums[p] + term
                for p in range(KW):
                    taps_out[p * KW + q : p * KW + q + 1, lanes] = jnp.sum(sums[p], axis=0, keepdims=True)
            return 0

        lax.fori_loop(0, width // LANES, group, 0)
        keep_lift = pltpu.make_async_copy(
            grad_lift.at[pl.ds(pl.multiple_of(part * part_px, 8), part_px)], lift_all.at[pl.ds((turn + 1) * part_px, part_px)], lift_sem
        )
        keep_lift.start()
        high, low = split(grad_lift[...])
        both = dot_t(jnp.concatenate([high, low], axis=0), w_in_hi[...])
        grad_x = (both[:px] + both[px:]) + dot_t(high, w_in_lo[...])
        carry = grad_x[:, LANES:] + pending_in[...]
        carry_out[...] = carry
        pending_out[...] = grad_x[:, :LANES]
        part_x = jnp.where(part == 0, grad_x[:part_px, :LANES], grad_x[part_px:, :LANES])
        part_c = jnp.where(part == 0, carry[:part_px], carry[part_px:])
        home_out[:LANES] = part_x.T
        home_out[LANES:] = part_c.T
    if begin:
        get_cot.wait()
        grad_new = cot[...] + carry if finish else cot[...]
        lane = lax.broadcasted_iota(jnp.int32, (px, LANES), 1)
        masked = jnp.where(lane < states, grad_new * ocean[...], 0.0)
        masked_part[...] = jnp.where(part == 0, masked[:part_px], masked[part_px:])
        keep_masked = pltpu.make_async_copy(masked_part, masked_all.at[pl.ds(turn * part_px, part_px)], begin_sems.at[2])
        keep_masked.start()
        high_f = masked.astype(BF16).astype(F32)
        nothing = jnp.zeros((px, LANES), F32)
        high_w = jnp.concatenate([high_f, nothing], axis=1)
        low_w = jnp.concatenate([masked - high_f, nothing], axis=1)
        left = (high_w + pltpu.roll(low_w, SEG, 1) + pltpu.roll(high_w, 2 * SEG, 1)).astype(BF16)
        branch_out[...] = dot(left, w_out[...])
        chunks = w_od.shape[1] // CHUNK
        get_slope.wait()

        def chunk(t, _):
            cols = pl.ds(pl.multiple_of(t * CHUNK, CHUNK), CHUNK)
            high, low = split(dot(left, w_od[:, cols]) * slope[t])
            hidden_out[:px, cols] = high
            hidden_out[px:, cols] = low
            return 0

        lax.fori_loop(0, chunks, chunk, 0)
        both = dot_t(hidden_out[...], w_up[:k_main])
        grad_n_out[:, :k_main] = (both[:px] + both[px:]) + dot_t(hidden_out[:px], w_up[k_main : 2 * k_main])
        rest = dot_t(hidden_out[...], w_up[2 * k_main :])
        tail = rest[:px] + rest[px:] + pltpu.roll(rest[:px], LANES - 2 * k_rem, 1)
        grad_n_out[:, k_main:] = jnp.where(lane < k_rem, tail, 0.0)
        edge_px = send_out.shape[0] - 8
        for g in range(width // LANES):
            lanes = slice(g * LANES, (g + 1) * LANES)
            cells = grad_n_out[:, lanes]
            send_out[edge_px : edge_px + 1, lanes] = jnp.sum(cells, axis=0, keepdims=True)
            send_out[edge_px + 1 : edge_px + 2, lanes] = jnp.sum(cells * norm_now[:, lanes], axis=0, keepdims=True)
        send_out[edge_px + 2 :, :] = jnp.zeros((6, width), F32)
        send_out[:edge_px, :] = grad_n_out[pl.ds(pl.multiple_of((1 - core) * (px - edge_px), 8), edge_px), :]
        keep_masked.wait()
    if finish:
        keep_lift.wait()


def weight_kernel(at, norm, gain, bias, hidden, send, *rest, quarter, finish):
    if finish:
        taps, keep_in, give_in, sums_in, keep_out, give_out, sums_out = rest
    else:
        keep_out, give_out, sums_out = rest
    core = at[0]
    part = at[1]
    px = norm.shape[0]
    tap_rows = sums_out.shape[0] - 8
    if finish:
        sums_out[:tap_rows] = sums_in[:tap_rows] + taps[...]
        sums_out[tap_rows:] = sums_in[tap_rows:] + send[send.shape[0] - 8 :]
    else:
        sums_out[:tap_rows] = jnp.zeros((tap_rows, sums_out.shape[1]), F32)
        sums_out[tap_rows:] = send[send.shape[0] - 8 :]
    window = round_up(quarter, LANES)
    base = (quarter // LANES) * LANES
    normed = norm[...] * gain[...] + bias[...]
    second = pltpu.roll(normed[:, base : base + window], window - (quarter - base), 1)
    mine = jnp.where(part == 0, normed[:, :window], second)
    lane = lax.broadcasted_iota(jnp.int32, (px, window), 1)
    mine = jnp.where(lane < quarter, mine, jnp.where(lane == quarter, 1.0, 0.0))
    high, low = split(mine.T[: keep_out.shape[0]])
    half = keep_out.shape[1]

    def chunk(side, start, size):
        acc_out = (keep_out, give_out)[side]
        here = pl.ds(start, size)
        actual = core if side == 0 else 1 - core
        cols = pl.ds(pl.multiple_of(actual * half + start, LANES), size)
        new = dot(high, hidden[:px, cols]) + dot(high, hidden[px:, cols]) + dot(low, hidden[:px, cols])
        acc_out[:, here] = (keep_in, give_in)[side][:, here] + new if finish else new

    for side in range(2):

        def step(t, _):
            chunk(side, pl.multiple_of(t * CHUNK, CHUNK), CHUNK)
            return 0

        lax.fori_loop(0, half // CHUNK, step, 0)
        if half % CHUNK:
            chunk(side, half // CHUNK * CHUNK, half % CHUNK)


VMEM_SPEC = pl.BlockSpec(memory_space=pltpu.VMEM)
SMEM_SPEC = pl.BlockSpec(memory_space=pltpu.SMEM)
HBM_SPEC = pl.BlockSpec(memory_space=pltpu.HBM)


def out(*shape, dtype=F32):
    return jax.ShapeDtypeStruct(shape, dtype)


def in_hbm(values):
    return pltpu.with_memory_space_constraint(values, pltpu.HBM)


def call(kernel, name, args, outs, scratch, limit, *, micros, smem=0, hbm=(), hbm_outs=(), vmem_outs=(), aliases=None, stacked=()):
    args = [in_hbm(a) if i in hbm else a for i, a in enumerate(args)]
    specs = [SMEM_SPEC if i < smem else HBM_SPEC if i in hbm else VMEM_SPEC for i in range(len(args))]
    hbm_outs = tuple(hbm_outs) + tuple(i for i, _ in stacked)
    aliases = dict(aliases or {})
    used = len(args)
    for i, buffer in stacked:
        if buffer is not None:
            aliases[len(args)] = i
            args.append(in_hbm(buffer))
            specs.append(HBM_SPEC)
    extra = len(args) - used

    def body(*refs):
        kernel(*refs[:used], *refs[used + extra :])

    return pl.pallas_call(
        body,
        in_specs=specs,
        out_specs=[HBM_SPEC if i in hbm_outs else VMEM_SPEC for i in range(len(outs))],
        out_shape=[
            pltpu.HBM(o.shape, o.dtype) if i in hbm_outs else pltpu.VMEM(o.shape, o.dtype) if i in vmem_outs else o
            for i, o in enumerate(outs)
        ],
        scratch_shapes=scratch,
        input_output_aliases=aliases,
        compiler_params=pltpu.CompilerParams(vmem_limit_bytes=limit * MIB),
        cost_estimate=pl.CostEstimate(flops=int(micros * 1.1e9), bytes_accessed=1024, transcendentals=0),
        name=name,
    )(*args)


def start_kernel(at, first, second, prev_out, cur_out, ocean_out, send_out, *, states, forces):
    core, part = at[0], at[1]
    block = first.shape[1]
    rows = first.shape[0]
    mask_row = 2 * states + forces

    def turn(values):
        prev = jnp.concatenate([values[: states + forces], jnp.zeros((LANES - states - forces, block), F32)], axis=0).T
        cur = jnp.concatenate([values[states + forces : mask_row], jnp.zeros((LANES - states, block), F32)], axis=0).T
        mask = jnp.broadcast_to(values[mask_row : mask_row + 1], (LANES, block)).T
        return prev, cur, mask

    zero, one = first[...], second[...]
    swap = part == 1
    top, low = jnp.where(swap, one, zero), jnp.where(swap, zero, one)
    count = jnp.sum(top[mask_row : mask_row + 1]) + jnp.sum(low[mask_row : mask_row + 1])
    for i, values in enumerate((top, low)):
        prev, cur, mask = turn(values)
        here = slice(i * block, (i + 1) * block)
        prev_out[here] = prev
        cur_out[here] = cur
        ocean_out[here] = mask
    at_edge = pl.ds(pl.multiple_of((1 - core) * block, 8), block)
    send_out[:block, :LANES] = prev_out[at_edge, :]
    send_out[:block, LANES : 2 * LANES] = cur_out[at_edge, :]
    send_out[:block, 2 * LANES :] = ocean_out[at_edge, :]
    send_out[block:] = jnp.full((8, 3 * LANES), count)


def pack_kernel(at, first, second, force_out, force_send, cot_out, *, states, forces):
    core, part = at[0], at[1]
    steps, rows, block = first.shape
    lane = lax.broadcasted_iota(jnp.int32, (block, LANES), 1)
    for j in range(steps):
        turned = [
            jnp.concatenate([values[j], jnp.zeros((LANES - rows, block), F32)], axis=0).T for values in (first, second)
        ]
        top, low = jnp.where(part == 1, turned[1], turned[0]), jnp.where(part == 1, turned[0], turned[1])
        for i, values in enumerate((top, low)):
            cot_out[j, i * block : (i + 1) * block] = jnp.where(lane < states, values, 0.0)
            force_out[j, i * block : (i + 1) * block] = jnp.where(lane < states, 0.0, values)
        force_send[j] = force_out[j, pl.ds(pl.multiple_of((1 - core) * block, 8), block), :]


def reorder(source, target, spans):
    for start, size, place in spans:
        target[:, place : place + size] = source[:, start : start + size]


def up_kernel(w_up_t, up_all, raw, turned, sems, *, k_main, k_rem, spans):
    slots, block = raw.shape[0], raw.shape[1]
    blocks = k_main // block

    def get(t, size):
        slot = lax.rem(t, slots)
        return pltpu.make_async_copy(
            w_up_t.at[pl.ds(pl.multiple_of(t * block, 8), size)], raw.at[slot, pl.ds(0, size)], sems.at[slot]
        )

    for t in range(slots):
        get(t, block).start()
    turned[...] = jnp.zeros_like(turned)

    def main(t, _):
        get(t, block).wait()
        reorder(raw.at[lax.rem(t, slots)], turned, spans)

        @pl.when(t + slots < blocks)
        def _():
            get(t + slots, block).start()

        @pl.when(t + slots == blocks)
        def _():
            get(t + slots, k_rem).start()

        high, low = split(turned[...])
        up_all[pl.ds(pl.multiple_of(t * block, block), block), :] = high
        up_all[pl.ds(pl.multiple_of(k_main + t * block, block), block), :] = low
        return 0

    lax.fori_loop(0, blocks, main, 0)
    get(blocks, k_rem).wait()
    reorder(raw.at[blocks % slots, pl.ds(0, k_rem)], turned.at[pl.ds(0, k_rem)], spans)
    high, low = split(turned[:k_rem])
    base = 2 * k_main
    up_all[base : base + k_rem] = high
    up_all[base + k_rem : base + 2 * k_rem] = high
    up_all[base + 2 * k_rem : base + 3 * k_rem] = low
    up_all[base + 3 * k_rem :] = jnp.zeros((LANES - 3 * k_rem, up_all.shape[1]), BF16)


def down_kernel(w_down, out_parts, od_fwd, od_bwd, down, product, ordered, sems, *, spans):
    pieces = sems.shape[0]
    piece = down.shape[1] // pieces

    def get(t):
        cols = pl.ds(pl.multiple_of(t * piece, LANES), piece)
        return pltpu.make_async_copy(w_down.at[:, cols], down.at[:, cols], sems.at[t])

    for t in range(pieces):
        get(t).start()
    ordered[...] = jnp.zeros_like(ordered)

    def multiply(t, _):
        cols = pl.ds(pl.multiple_of(t * piece, LANES), piece)
        get(t).wait()
        high, low = split(down[:, cols])
        both = dot(out_parts[...], high)
        product[:, cols] = (both[:SEG] + both[SEG:]) + dot(out_parts[:SEG], low)
        return 0

    lax.fori_loop(0, pieces, multiply, 0)
    reorder(product, ordered.at[pl.ds(0, SEG)], spans)

    def spread(t, _):
        cols = pl.ds(pl.multiple_of(t * CHUNK, CHUNK), CHUNK)
        values = ordered[:, cols]
        high, low = split(values)
        od_bwd[:SEG, cols] = high[:SEG]
        od_bwd[SEG : 2 * SEG, cols] = high[:SEG]
        od_bwd[2 * SEG : 3 * SEG, cols] = low[:SEG]
        od_bwd[3 * SEG :, cols] = jnp.zeros((od_bwd.shape[0] - 3 * SEG, CHUNK), BF16)
        high, low = split(values.T)
        od_fwd[cols, :LANES] = high
        od_fwd[cols, LANES:] = low
        return 0

    lax.fori_loop(0, ordered.shape[1] // CHUNK, spread, 0)


def last_kernel(
    at, masked_hbm, x_hbm, lifts_hbm, lifted_hbm, act_hbm, down_hbm, b_down, sums, taps, table, hidden_keep, hidden_give,
    masked, x_parts, lifts, lifted, act, down, masked_t, x_t, g_hidden, natural, g_parts, sems, *, spans, blocks,
):
    chunks = act.shape[0]
    half = hidden_keep.shape[1]
    width = table.shape[1]
    scale = (at[1] == 0).astype(F32)
    tap_rows = taps.shape[0]
    pairs = [(masked_hbm, masked), (x_hbm, x_parts), (lifts_hbm, lifts), (lifted_hbm, lifted)]
    firsts = [pltpu.make_async_copy(pair[0], pair[1], sems.at[i]) for i, pair in enumerate(pairs)]
    downs = [
        pltpu.make_async_copy(down_hbm.at[pl.ds(start, size)], down.at[pl.ds(start, size)], sems.at[4 + i])
        for i, (start, size) in enumerate(blocks)
    ]

    def get(t):
        return pltpu.make_async_copy(act_hbm.at[t], act.at[t], sems.at[4 + len(blocks) + t])

    firsts[0].start()
    for t in range(chunks):
        get(t).start()
    for copy in firsts[1:] + downs:
        copy.start()
    firsts[0].wait()
    turned = masked[...].T[:SEG]
    high = turned.astype(BF16)
    masked_t[:SEG] = high
    masked_t[SEG:] = (turned - high.astype(F32)).astype(BF16)
    total = jnp.sum(turned, axis=1, keepdims=True)

    def chunk(t, _):
        get(t).wait()
        high, low = split(act[t])
        both = dot(masked_t[...], high)
        sums_now = (both[:SEG] + both[SEG:]) + dot(masked_t[:SEG], low)
        g_hidden[:, pl.ds(pl.multiple_of(t * CHUNK, CHUNK), CHUNK)] = sums_now
        return 0

    lax.fori_loop(0, chunks, chunk, 0)
    hidden_keep[...] = g_hidden[:, pl.ds(pl.multiple_of(at[0] * half, LANES), half)]
    hidden_give[...] = g_hidden[:, pl.ds(pl.multiple_of((1 - at[0]) * half, LANES), half)]
    for start, size, place in spans:
        natural[:, start : start + size] = g_hidden[:, place : place + size]
    high, low = split(natural[...])
    g_parts[:SEG] = high
    g_parts[SEG:] = low
    for copy in firsts[1:]:
        copy.wait()
    high, low = split(x_parts[...].T)
    x_t[0] = high
    x_t[1] = low
    for start in range(0, width, CHUNK):
        size = min(CHUNK, width - start)
        lanes = slice(start, start + size)
        high, low = split(lifted[:, :, lanes].reshape(lifts.shape[0], size))
        both = dot(masked_t[...], high)
        lifted_sum = (both[:SEG] + both[SEG:]) + dot(masked_t[:SEG], low)
        grads = lifts[:, lanes]
        high, low = split(grads)
        g_in = dot(x_t[0], high) + dot(x_t[1], high) + dot(x_t[0], low)
        table[:88, lanes] = g_in[:88]
        table[88:168, lanes] = g_in[LANES : LANES + 80]
        table[168:224, lanes] = sums[:tap_rows, lanes] + taps[:, lanes]
        table[224:304, lanes] = lifted_sum + total * b_down[:, lanes]
        table[304:311, lanes] = sums[tap_rows : tap_rows + 7, lanes] * scale
        table[311:312, lanes] = jnp.sum(grads, axis=0, keepdims=True)
    for (start, size), copy in zip(blocks, downs):
        copy.wait()
        high, low = split(down[start : start + size])
        both = dot_t(g_parts[...], high)
        g_out = (both[:SEG] + both[SEG:]) + dot_t(g_parts[:SEG], low)
        table[224:304, start : start + size] += g_out


def pad_to(values, shape):
    return jnp.pad(values, [(0, size - have) for size, have in zip(shape, values.shape)])


def per_device(
    init_states, forcing, history, land_mask, w_in, b_in, w_dw, bn_gain, bn_bias, w_up, b_up, w_down, b_down, w_out, b_out, cotangent
):
    steps = lax.axis_size("step")
    devices_z = lax.axis_size("rows")
    step = lax.axis_index("step")
    depth = lax.axis_index("rows")
    core, pair = step % 2, step // 2
    side, part = depth % 2, depth // 2
    both_axes = ("step", "rows")
    block = land_mask.shape[0]
    px = 2 * block
    rows = px // COLS
    states = w_out.shape[0]
    forces = forcing.shape[2]
    channels = w_up.shape[1]
    hidden = w_up.shape[0]
    width = round_up(channels, LANES)
    ff_block = hidden // steps
    half = round_up(hidden // 2, LANES)
    wide = 2 * half
    spans = [(s * ff_block, ff_block, (s % 2) * half + (s // 2) * ff_block) for s in range(steps)]
    k_main = channels // CHUNK * CHUNK
    k_rem = channels - k_main
    col_block = channels // devices_z

    def place(s, z):
        return s * devices_z + z

    cells = [(k, c, h, q) for k in range(steps // 2) for c in range(2) for h in range(2) for q in range(2)]
    fetch_perms = [
        [(place(2 * k + q, 2 * c + (b ^ h)), place(2 * k + c, 2 * h + q)) for k, c, h, q in cells] for b in range(2)
    ]

    siblings = [(s, s ^ 1) for s in range(steps)]

    def to_sibling(values):
        return lax.ppermute(values, "step", siblings)

    def shift_back(values, j):
        return values if j == 0 else lax.ppermute(values, "step", [((s + j) % steps, s) for s in range(steps)])

    def fetch_own(values):
        got = [lax.ppermute(values, both_axes, perm) for perm in fetch_perms]
        return got

    def turn_round(values):
        doubled = jnp.flip(jnp.concatenate([values, values]), axis=0)
        return lax.dynamic_slice_in_dim(doubled, steps - 1 - step, steps, axis=0)

    def rotate(values, by):
        return lax.dynamic_slice_in_dim(jnp.concatenate([values, values]), by, steps, axis=0)

    def from_later(values):
        if steps == ROLL:
            return rotate(lax.all_to_all(turn_round(values), "step", 0, 0, tiled=True), step)
        return jnp.stack([shift_back(values[j], j) for j in range(ROLL)])

    def to_later(values):
        if steps == ROLL:
            return turn_round(lax.all_to_all(rotate(values, (steps - step) % steps), "step", 0, 0, tiled=True))
        return jnp.stack([lax.ppermute(values[j], "step", [(s, (s + j) % steps) for s in range(steps)]) for j in range(ROLL)])

    at = jnp.stack([core, part]).astype(jnp.int32)
    mask_row = land_mask.astype(F32)[None]
    current = init_states[0, 0, 1]
    previous = jnp.where(history[0, 0] == 2, init_states[0, 0, 0], current)
    payload = jnp.concatenate([previous, forcing[0, 0], current, mask_row], axis=0)
    timed = jnp.concatenate([cotangent[0, :, 0], jnp.broadcast_to(forcing[0], (ROLL,) + forcing.shape[2:])], axis=1)
    payload, timed = lax.optimization_barrier((payload, timed))
    payload = fetch_own(payload)
    timed = from_later(timed)

    def in_rows(values):
        top = jnp.concatenate([values[:states], values[2 * states :]], axis=0)
        bottom = values[states : 2 * states]
        return jnp.concatenate([jnp.pad(v, ((0, LANES - v.shape[0]), (0, 0))) for v in (top, bottom)], axis=0)

    def row(values, size):
        return jnp.pad(values, (0, size - values.shape[0]))[None]

    w_in_hi, w_in_lo = split_outside(pad_to(in_rows(w_in.T), (2 * LANES, width)))
    w_oi = pad_to(in_rows(jnp.dot(w_out, w_in, precision=HIGHEST).T), (2 * LANES, LANES))
    w_oi_hi, w_oi_lo = split_outside(w_oi)
    b_new = row(jnp.dot(w_out, b_in + b_down, precision=HIGHEST) + b_out, LANES)
    taps = jnp.broadcast_to(
        pad_to(w_dw.reshape(channels, KW * KW).T, (KW * KW, width))[:, None], (KW * KW, 8, width)
    )
    gain, bias = row(bn_gain, width), row(bn_bias, width)
    row_hi, row_lo = split_outside(pad_to(w_out, (SEG, channels)))
    out_parts = jnp.concatenate([row_hi, row_lo], axis=0)
    pieces = 5
    w_od_fwd, w_od_bwd = call(
        functools.partial(down_kernel, spans=spans), "down", (w_down, out_parts),
        [out(wide, 2 * LANES, dtype=BF16), out(2 * LANES, wide, dtype=BF16)],
        [pltpu.VMEM((channels, hidden), F32), pltpu.VMEM((SEG, hidden), F32), pltpu.VMEM((LANES, wide), F32), pltpu.SemaphoreType.DMA((pieces,))],
        20, micros=7, hbm=(0,), vmem_outs=(0, 1),
    )
    out_hi, out_lo = split_outside(pad_to(w_out, (SEG, width)))
    w_out_bwd = pad_to(jnp.concatenate([out_hi, out_hi, out_lo], axis=0), (2 * LANES, width))
    b_in_row = row(b_in, width)
    b_up_row = pad_to(b_up.reshape(steps // 2, 2, ff_block).swapaxes(0, 1).reshape(2, hidden // 2), (2, half)).reshape(1, wide)
    b_down_row = row(b_down, width)
    prev, cur, ocean, first_sent = call(
        functools.partial(start_kernel, states=states, forces=forces), "start", (at, *payload),
        [out(px, LANES), out(px, LANES), out(px, LANES), out(block + 8, 3 * LANES)], [], 4, micros=1, smem=1,
    )
    first_came = to_sibling(first_sent)
    ready = lax.optimization_barrier(
        (w_up.T, timed, w_in_hi, w_in_lo, w_oi_hi, w_oi_lo, b_new, taps, gain, bias, w_out_bwd, b_in_row, b_up_row, b_down_row, at, first_sent)
    )
    up_source, timed, w_in_hi, w_in_lo, w_oi_hi, w_oi_lo, b_new, taps, gain, bias, w_out_bwd, b_in_row, b_up_row, b_down_row, at, first_sent = ready
    timed = fetch_own(timed)
    (w_up_all,) = call(
        functools.partial(up_kernel, k_main=k_main, k_rem=k_rem, spans=spans), "up", (up_source,),
        [out(2 * k_main + LANES, wide, dtype=BF16)],
        [pltpu.VMEM((3, k_main // 8, hidden), F32), pltpu.VMEM((k_main // 8, wide), F32), pltpu.SemaphoreType.DMA((3,))],
        10, micros=7, hbm=(0,), vmem_outs=(0,),
    )
    first_came, w_up_all = lax.optimization_barrier((first_came, w_up_all))
    force, force_send, cots = call(
        functools.partial(pack_kernel, states=states, forces=forces), "pack", (at, *timed),
        [out(ROLL, px, LANES), out(ROLL, block, LANES), out(ROLL, px, LANES)], [], 6, micros=2, smem=1,
    )
    force_edge = to_sibling(force_send)

    chunks = wide // CHUNK
    x_all, lifted_all, act_all = None, None, None
    kept, predicted = [], []
    prev_edge, cur_edge, prev_lanes, cur_lanes = first_came, first_came, 0, LANES
    for j in range(ROLL):
        mixed, stats, base, window, x_all, lifted_all = call(
            functools.partial(mix_kernel, turn=j, cur_lanes=cur_lanes, prev_lanes=prev_lanes), "mix",
            (at, cur, cur_edge, prev, prev_edge) + ((force, force_edge) if j else (at, at)) + (w_in_hi, w_in_lo, b_in_row, w_oi_hi, w_oi_lo, b_new, taps, ocean),
            [
                out(px, width), out(8, width), out(px, LANES), out(HALO + 2 * HALO, COLS, width), out(ROLL * block, 2 * LANES),
                out(ROLL * HALO, COLS, width),
            ],
            [
                pltpu.VMEM((rows + 2 * HALO, COLS + 16, width), F32), pltpu.VMEM((KW, rows + 2 * HALO, COLS, LANES), F32),
                pltpu.VMEM((rows, COLS, width), F32), pltpu.VMEM((block, 2 * LANES), F32), pltpu.SemaphoreType.DMA((3,)),
            ],
            12, micros=4.5, smem=1, hbm_outs=(3,), stacked=((4, x_all), (5, lifted_all)),
        )
        stats_other = to_sibling(stats)
        new, new_edge, state, norm_edge, inv, norm, slope, act_all = call(
            functools.partial(feed_kernel, turn=j, width=width, k_main=k_main, k_rem=k_rem), "feed",
            (at, mixed, stats, stats_other, first_sent, first_came, gain, bias, ocean, base, w_up_all, b_up_row, w_od_fwd),
            [
                out(px, LANES), out(block, LANES), out(SEG, block), out(block, width), out(8, width), out(px, width),
                out(chunks, px, CHUNK), out(chunks, ROLL * block, CHUNK),
            ],
            [
                pltpu.VMEM((2 * px, k_main), BF16), pltpu.VMEM((px, LANES), BF16),
                pltpu.VMEM((px, CHUNK), F32), pltpu.VMEM((px, LANES), F32), pltpu.VMEM((px, CHUNK), F32), pltpu.VMEM((px, CHUNK), F32),
                pltpu.VMEM((px, CHUNK), F32), pltpu.VMEM((px, width), F32), pltpu.VMEM((chunks, px, CHUNK), F32),
                pltpu.VMEM((chunks, block, CHUNK), F32), pltpu.SemaphoreType.DMA((2 * chunks + 1,)),
            ],
            14, micros=8.5, smem=1, hbm_outs=(5, 6), stacked=((7, act_all),),
        )
        prev, prev_edge, prev_lanes, cur = cur, cur_edge, cur_lanes, new
        if j < ROLL - 1:
            cur_edge, cur_lanes = to_sibling(new_edge), 0
        norm_edge = to_sibling(norm_edge)
        predicted.append(state)
        kept.append((window, norm, norm_edge, slope, inv))

    quarter = channels // 2
    acc_rows = round_up(quarter + 1, 8)
    tap_rows = round_up(KW * KW, 8)
    carry, pending = None, jnp.zeros((px, LANES), F32)
    previous_step, keep_acc, give_acc, sums, lift_all, masked_all = None, None, None, None, None, None
    homes = []
    begin_scratch = [
        pltpu.VMEM((px, LANES), F32), pltpu.VMEM((chunks, px, CHUNK), F32), pltpu.VMEM((block, LANES), F32), pltpu.SemaphoreType.DMA((3,)),
    ]
    finish_scratch = [
        pltpu.VMEM((rows + 2 * HALO, COLS + 16, width), F32), pltpu.VMEM((KW, rows + 2 * HALO, COLS, LANES), F32),
        pltpu.VMEM((rows, COLS, width), F32), pltpu.VMEM((px, width), F32), pltpu.SemaphoreType.DMA,
    ]
    for j in range(ROLL - 1, -2, -1):
        finish, begin = j < ROLL - 1, j >= 0
        if finish:
            pending, keep_acc, give_acc = lax.optimization_barrier((pending, keep_acc, give_acc))
        args, outs, scratch, stacked, hbm = [at, ocean, pending], [], [], [], ()
        if finish:
            window, norm, norm_edge, slope, inv = kept[j + 1]
            grad_n, sent, came, grad_branch = previous_step
            args += [grad_n, sent, came, norm, norm_edge, inv, gain, first_sent, first_came, grad_branch, window, taps, w_in_hi, w_in_lo]
            outs += [out(px, LANES), out(px, LANES), out(tap_rows, width), out(2 * LANES, block), out(ROLL * block, width)]
            stacked.append((4, lift_all))
            scratch += finish_scratch
        if begin:
            hbm = (len(args), len(args) + 1)
            args += [cots, kept[j][3], kept[j][1], w_out_bwd, w_od_bwd, w_up_all]
            outs += [out(px, width), out(2 * px, wide, dtype=BF16), out(px, width), out(block + 8, width), out(ROLL * block, LANES)]
            stacked.append((len(outs) - 1, masked_all))
            scratch += begin_scratch
        kernel = functools.partial(
            back_kernel, finish=finish, begin=begin, turn=j, width=width, k_main=k_main, k_rem=k_rem, states=states
        )
        results = list(
            call(kernel, "back", args, outs, scratch, 18, micros=7 * finish + 7.5 * begin, smem=1, hbm=hbm, stacked=stacked)
        )
        if finish:
            carry, pending, tap_sum, home, lift_all = results[:5]
            results = results[5:]
            homes.append(home)
        if begin:
            grad_branch, hidden_now, grad_n, sent, masked_all = results
            came = to_sibling(sent)
            previous_step = (grad_n, sent, came, grad_branch)
            keep_acc, give_acc, sums = call(
                functools.partial(weight_kernel, quarter=quarter, finish=finish), "weight",
                (at, kept[j][1], gain, bias, hidden_now, sent) + ((tap_sum, keep_acc, give_acc, sums) if finish else ()),
                [out(acc_rows, half), out(acc_rows, half), out(tap_rows + 8, width)], [], 8, micros=5, smem=1,
                aliases=({7: 0, 8: 1, 9: 2} if j else {7: 0, 9: 2}) if finish else None, vmem_outs=(0, 1, 2) if j else (),
            )

    def trade(values, axis, flip):
        return lax.ppermute(values, axis, [(i, i ^ flip) for i in range(lax.axis_size(axis))])

    def pick(first, second, bit):
        return jnp.where(bit == 0, first, second), jnp.where(bit == 0, second, first)

    def at_index(values, index):
        return lax.dynamic_index_in_dim(values, index, keepdims=False)

    def cut(values, k):
        return values[..., k * ff_block : (k + 1) * ff_block]

    def sum_z(values):
        near = values + trade(values, "rows", 1)
        return near + trade(near, "rows", 2)

    direct = steps == 8 and devices_z == 4
    bit_x, bit_y = pair % 2, pair // 2
    mine_up = keep_acc + trade(give_acc, "step", 1)
    masked_all, mine_up, lift_all = lax.optimization_barrier((masked_all, mine_up, lift_all))
    if direct:
        rows_a, rows_b = mine_up[:col_block], mine_up[col_block : 2 * col_block]
        even = jnp.stack([cut(rows_a, 0), cut(rows_a, 2)])
        odd = jnp.stack([cut(rows_a, 1), cut(rows_a, 3)])
        keep_a, give_a = pick(even, odd, bit_x)
        low = jnp.stack([cut(rows_b, 0), cut(rows_b, 1)])
        top = jnp.stack([cut(rows_b, 2), cut(rows_b, 3)])
        keep_b, give_b = pick(low, top, bit_y)
        got_a = keep_a + trade(give_a, "step", 2)
        got_b = keep_b + trade(give_b, "step", 4)
    part_px = ROLL * block
    blocks = [(start, min(CHUNK, channels - start)) for start in range(0, channels, CHUNK)]
    table, hidden_keep, hidden_give = call(
        functools.partial(last_kernel, spans=spans, blocks=blocks), "last",
        (
            at, masked_all, x_all, lift_all, lifted_all, act_all, w_down, b_down_row, sums, tap_sum,
        ),
        [out(312, width), out(SEG, half), out(SEG, half)],
        [
            pltpu.VMEM((part_px, LANES), F32), pltpu.VMEM((part_px, 2 * LANES), F32), pltpu.VMEM((part_px, width), F32),
            pltpu.VMEM(lifted_all.shape, F32), pltpu.VMEM((chunks, part_px, CHUNK), F32), pltpu.VMEM((channels, hidden), F32),
            pltpu.VMEM((2 * SEG, part_px), BF16), pltpu.VMEM((2, 2 * LANES, part_px), BF16), pltpu.VMEM((SEG, wide), F32),
            pltpu.VMEM((SEG, hidden), F32), pltpu.VMEM((2 * SEG, hidden), BF16),
            pltpu.SemaphoreType.DMA((4 + len(blocks) + chunks,)),
        ],
        44, micros=12, smem=1, hbm=(1, 2, 3, 4, 5, 6),
    )
    if direct:
        table, got_a, got_b = lax.optimization_barrier((table, got_a, got_b))
    first_table = table
    up_row = jnp.stack(pick(keep_acc[quarter], give_acc[quarter], core)).reshape(wide) * (part == 0).astype(F32)
    masked_sum = jnp.sum(masked_all, axis=0)
    extra = jnp.concatenate([pad_to(up_row, (4 * width,)).reshape(4, width), row(masked_sum, width), jnp.zeros((3, width), F32)], axis=0)
    table = jnp.concatenate([table, extra], axis=0)
    mine_down = hidden_keep + trade(hidden_give, "step", 1)
    if direct:
        table = table.reshape(2, -1, width)
        own = at_index(table, core) + trade(at_index(table, 1 - core), "step", 1)
        own = own.reshape(4, -1, width)
        rest = [trade(at_index(own, pair ^ b), "step", 2 * b) for b in (1, 2, 3)]
        own = (at_index(own, pair) + rest[0]) + (rest[1] + rest[2])

        keep_a, give_a = pick(got_a[0], got_a[1], bit_y)
        keep_b, give_b = pick(got_b[0], got_b[1], bit_x)
        got_a = keep_a + trade(give_a, "step", 4)
        got_b = keep_b + trade(give_b, "step", 2)

        rest = [trade(own, "rows", b) for b in (1, 2, 3)]
        own = (own + rest[0]) + (rest[1] + rest[2])
        keep, give = pick(got_a, got_b, side)
        share_up = (keep + trade(give, "rows", 1)).T
        rest = jnp.stack([own] + [trade(own, "step", 2 * b) for b in (1, 2, 3)])
        own = jnp.concatenate([at_index(rest, pair ^ b) for b in range(4)], axis=0)
        other = trade(own, "step", 1)
        table = jnp.concatenate(pick(own, other, core), axis=0)

        pieces = jnp.stack([cut(mine_down, k) for k in range(4)])
        near = at_index(pieces, pair) + trade(at_index(pieces, pair ^ 1), "step", 2)
        far = trade(at_index(pieces, pair ^ 2), "step", 4) + trade(at_index(pieces, pair ^ 3), "step", 6)
        hidden_share = sum_z(near + far)
    else:
        units = steps // 2
        same_core = [[2 * k + c for k in range(units)] for c in range(2)]
        share = lax.psum_scatter(mine_up[:, : hidden // 2], "step", scatter_dimension=1, axis_index_groups=same_core, tiled=True)
        keep, give = pick(share[:col_block], share[col_block : 2 * col_block], side)
        share_up = (keep + trade(give, "rows", 1)).T
        hidden_share = lax.psum(
            lax.psum_scatter(mine_down[:, : hidden // 2], "step", scatter_dimension=1, axis_index_groups=same_core, tiled=True), "rows"
        )
        table = lax.psum(table, both_axes)

    g_w_in = jnp.concatenate([table[:states], table[88 : 88 + states], table[states : states + forces]], axis=0)[:, :channels].T
    g_w_dw = table[168 : 168 + KW * KW, :channels].T.reshape(channels, KW, KW)
    g_w_out = table[224 : 224 + states, :channels]
    g_bias, g_gain, g_b_in = table[304, :channels], table[305, :channels], table[311, :channels]
    g_b_up = table[312:316].reshape(-1)[:wide].reshape(2, half)[:, : hidden // 2].reshape(2, steps // 2, ff_block).swapaxes(0, 1).reshape(-1)
    g_b_out = table[316, :states]
    g_b_down = jnp.sum(w_out * g_b_out[:, None], axis=0)

    *late, _ = lax.optimization_barrier((*predicted, *homes, first_table))
    predicted, homes = late[:ROLL], late[ROLL:]
    going = jnp.stack([jnp.concatenate([predicted[j][:states], homes[ROLL - 1 - j][states : states + forces]], axis=0) for j in range(ROLL)])
    ending = jnp.concatenate([homes[-1][:states], homes[-1][LANES : LANES + states]], axis=0)
    flat = jnp.concatenate([going.reshape(-1, block), ending], axis=0)
    flat = lax.ppermute(flat, both_axes, [(place(2 * k + c, 2 * h + q), place(2 * k + q, 2 * c + h)) for k, c, h, q in cells])
    gone = to_later(flat[: going.shape[0] * going.shape[1]].reshape(going.shape))
    grad_prev, grad_cur = flat[-2 * states : -states], flat[-states:]
    grad_forcing = jnp.sum(gone[:, states:], axis=0)[None, None]
    grad_init_prev = jnp.where(history[0, 0] == 2, grad_prev, 0.0)
    grad_init_cur = grad_cur + jnp.where(history[0, 0] == 1, grad_prev, 0.0)
    grad_init = jnp.stack([grad_init_prev, grad_init_cur])[None, None]
    w_out_block = lax.dynamic_slice_in_dim(w_out, depth * col_block, col_block, axis=1)
    share_down = lax.dot_general(
        w_out_block, hidden_share[:states], (((0,), (0,)), ((), ())), precision=lax.Precision.HIGH, preferred_element_type=F32
    )
    return (
        gone[None, :, None, :states],
        grad_init,
        grad_forcing,
        g_w_in,
        g_b_in,
        g_w_dw,
        g_gain,
        g_bias,
        share_up,
        g_b_up,
        share_down,
        g_b_down,
        g_w_out,
        g_b_out,
    )


def solution(mesh):
    state_spec = P("step", None, None, None, "rows")
    force_spec = P("step", None, None, "rows")
    in_specs = (state_spec, force_spec, P("step", None), P("rows")) + (P(),) * 11 + (state_spec,)
    out_specs = (state_spec, state_spec, force_spec) + (P(),) * 5 + (P("step", "rows"), P(), P("rows", "step"), P(), P(), P())
    return jax.shard_map(per_device, mesh=mesh, in_specs=in_specs, out_specs=out_specs, check_vma=False)
```

```python
import functools

import jax
import jax.numpy as jnp
from jax import lax
from jax.experimental import pallas as pl
from jax.experimental.pallas import tpu as pltpu
from jax.sharding import PartitionSpec as P

F32 = jnp.float32
BF16 = jnp.bfloat16
HIGHEST = lax.Precision.HIGHEST
ROLL = 8
COLS = 32
KW = 7
HALO = 3
EPSILON = 1e-05
LANES = 128
CHUNK = 256
SEG = 80
MIB = 2**20

ERF_P = 0.39
ERF_C = (0.23532534, 0.09138764, 0.64956134, -0.63540268, 0.88666585, -0.22753749)


def round_up(value, multiple):
    return -(-value // multiple) * multiple


def split(values):
    high = values.astype(BF16)
    return high, (values - high.astype(F32)).astype(BF16)


def split_outside(values):
    rounded = lax.reduce_precision(values, 8, 7)
    return rounded.astype(BF16), (values - rounded).astype(BF16)


def dot(left, right):
    return jnp.dot(left, right, preferred_element_type=F32)


def dot_t(left, right):
    return lax.dot_general(left, right, (((1,), (1,)), ((), ())), preferred_element_type=F32)


def gelu_both(v):
    e = jnp.exp(v * v * (-0.5))
    t = 1.0 / (1.0 + (ERF_P * 0.7071067811865476) * jnp.abs(v))
    q = 0.5 * ERF_C[5]
    for coefficient in ERF_C[4::-1]:
        q = q * t + 0.5 * coefficient
    q = (q * t) * e
    phi = jnp.where(v >= 0.0, 1.0 - q, q)
    return v * phi, phi + v * (e * 0.3989422804014327)


def depthwise(ext, shifted, kernel, mixed, lanes, flip, rows):
    rows_in = rows + 2 * HALO
    for q in range(KW):
        for r in range(rows_in):
            shifted[q, r] = ext[r, 5 + q : 5 + q + COLS, lanes]
    for v in range(0, COLS, 8):
        total = [None] * rows
        for q in range(KW):
            taps = [
                kernel[(KW * KW - 1 - (p * KW + q)) if flip else (p * KW + q), :, lanes]
                for p in range(KW)
            ]
            for r in range(rows_in):
                cell = shifted[q, r, v : v + 8, :]
                for p in range(KW):
                    i = r - p
                    if 0 <= i < rows:
                        term = taps[p] * cell
                        total[i] = term if total[i] is None else total[i] + term
        for i in range(rows):
            mixed[i, v : v + 8, lanes] = total[i]


def ocean_count(sent, came):
    last = sent.shape[0] - 1
    return jnp.maximum(sent[last:, :LANES] + came[last:, :LANES], 1.0)


def group_lanes(group):
    return pl.ds(pl.multiple_of(group * LANES, LANES), LANES)


def mix_kernel(
    at, cur, cur_edge, prev, prev_edge, force, force_edge, w_in_hi, w_in_lo, b_in, w_oi_hi, w_oi_lo, b_new, taps, ocean,
    mixed_out, stats_out, base_out, window_out, x_all, lifted_all,
    ext, shifted, mixed, x_part, sems, *, turn, cur_lanes, prev_lanes,
):
    core, part = at[0], at[1]
    px = cur.shape[0]
    edge_px = x_part.shape[0]
    rows = px // COLS
    width = mixed_out.shape[1]
    prev_now, prev_edge_now = prev[...], prev_edge[:edge_px, prev_lanes : prev_lanes + LANES]
    if turn:
        prev_now, prev_edge_now = prev_now + force[turn], prev_edge_now + force_edge[turn]
    own = jnp.concatenate([prev_now, cur[...]], axis=1)
    edge = jnp.concatenate([prev_edge_now, cur_edge[:edge_px, cur_lanes : cur_lanes + LANES]], axis=1)
    own_hi, own_lo = split(own)
    edge_hi, edge_lo = split(edge)
    both = dot(jnp.concatenate([own_hi, edge_hi, own_lo, edge_lo], axis=0), w_in_hi[...])
    high = dot(jnp.concatenate([own_hi, edge_hi], axis=0), w_in_lo[...])
    lifted = (both[: px + edge_px] + both[px + edge_px :]) + (high + b_in[...])
    base_out[...] = dot(own_hi, w_oi_hi[...]) + dot(own_lo, w_oi_hi[...]) + dot(own_hi, w_oi_lo[...]) + b_new[...]
    zeros = jnp.zeros((rows + 2 * HALO, 8, width), F32)
    ext[:, :8, :] = zeros
    ext[:, 8 + COLS :, :] = zeros
    ext[HALO : HALO + rows, 8 : 8 + COLS, :] = lifted[:px].reshape(rows, COLS, width)
    ext[pl.ds((rows + HALO) * (1 - core), HALO), 8 : 8 + COLS, :] = lifted[px:].reshape(HALO, COLS, width)
    ext[pl.ds((rows + HALO) * core, HALO), 8 : 8 + COLS, :] = jnp.zeros((HALO, COLS, width), F32)
    part_rows = window_out.shape[0] - 2 * HALO
    part_px = x_part.shape[0]
    x_part[...] = jnp.where(part == 0, own[:part_px], own[part_px:])
    here = pl.ds(turn * part_rows, part_rows)
    keeps = [
        pltpu.make_async_copy(ext.at[pl.ds(part * part_rows, window_out.shape[0]), 8 : 8 + COLS, :], window_out, sems.at[0]),
        pltpu.make_async_copy(ext.at[pl.ds(part * part_rows + HALO, part_rows), 8 : 8 + COLS, :], lifted_all.at[here], sems.at[1]),
        pltpu.make_async_copy(x_part, x_all.at[pl.ds(turn * part_px, part_px)], sems.at[2]),
    ]
    for keep in keeps:
        keep.start()
    mask = ocean[...]

    def group(g, _):
        lanes = group_lanes(g)
        depthwise(ext, shifted, taps, mixed, lanes, False, rows)
        cells = mixed[:, :, lanes].reshape(px, LANES)
        mixed_out[:, lanes] = cells
        masked = cells * mask
        stats_out[0:1, lanes] = jnp.sum(masked, axis=0, keepdims=True)
        stats_out[1:2, lanes] = jnp.sum(masked * cells, axis=0, keepdims=True)
        return 0

    lax.fori_loop(0, width // LANES, group, 0)
    for keep in keeps:
        keep.wait()


def feed_kernel(
    at, mixed, stats, stats_other, sent, came, gain, bias, ocean, base, w_up, b_up, w_od,
    new_out, new_edge_out, norm_edge_out, inv_out, norm_out, slope_out, act_all, state_all,
    stack, rem, acc, acc_lo, hold_a, hold_b, hold_act, norm, slope, act_part, state, sems, *, turn, width, k_main, k_rem,
):
    core, part = at[0], at[1]
    px = mixed.shape[0]
    chunks = w_up.shape[1] // CHUNK
    part_px = act_part.shape[1]
    total = ocean_count(sent, came)
    keep_norm = pltpu.make_async_copy(norm, norm_out, sems.at[2 * chunks])

    for g in range(width // LANES):
        lanes = slice(g * LANES, (g + 1) * LANES)
        cells = mixed[:, lanes]
        average = (stats[0:1, lanes] + stats_other[0:1, lanes]) / total
        variance = (stats[1:2, lanes] + stats_other[1:2, lanes]) / total - average * average
        inverse = lax.rsqrt(variance + EPSILON)
        inv_out[:, lanes] = jnp.broadcast_to(inverse, (8, LANES))
        normalized = (cells - average) * inverse
        norm[:, lanes] = normalized
        normed = normalized * gain[:, lanes] + bias[:, lanes]
        high = normed.astype(BF16)
        high_f = high.astype(F32)
        low_f = normed - high_f
        if (g + 1) * LANES <= k_main:
            stack[:px, lanes] = high
            stack[px:, lanes] = low_f.astype(BF16)
        else:
            rem[...] = (high_f + pltpu.roll(low_f, k_rem, 1) + pltpu.roll(high_f, 2 * k_rem, 1)).astype(BF16)
    keep_norm.start()
    edge_px = norm_edge_out.shape[0]
    norm_edge_out[...] = norm[pl.ds(pl.multiple_of((1 - core) * (px - edge_px), 8), edge_px), :]

    def up(t, hold):
        cols = pl.ds(pl.multiple_of(t * CHUNK, CHUNK), CHUNK)
        both = dot(stack[...], w_up[:k_main, cols])
        high = dot(stack[:px], w_up[k_main : 2 * k_main, cols])
        rest = dot(rem[...], w_up[2 * k_main :, cols])
        hold[...] = (both[:px] + both[px:]) + (high + rest)

    def keep_slope(t):
        return pltpu.make_async_copy(slope.at[t], slope_out.at[t], sems.at[t])

    def keep_act(t):
        return pltpu.make_async_copy(act_part.at[t], act_all.at[t, pl.ds(turn * part_px, part_px)], sems.at[chunks + t])

    def act(t, hold):
        cols = pl.ds(pl.multiple_of(t * CHUNK, CHUNK), CHUNK)
        activated, slope[t] = gelu_both(hold[...] + b_up[:, cols])
        hold_act[...] = activated
        high, low = split(activated)
        acc[...] += dot(high, w_od[cols, :])
        acc_lo[...] += dot(low, w_od[cols, :LANES])
        act_part[t] = hold_act[pl.ds(pl.multiple_of(part * part_px, 8), part_px), :]
        keep_slope(t).start()
        keep_act(t).start()

    acc[...] = jnp.zeros_like(acc)
    acc_lo[...] = base[...]
    up(0, hold_a)

    def pair(i, _):
        up(2 * i + 1, hold_b)
        act(2 * i, hold_a)
        up(2 * i + 2, hold_a)
        act(2 * i + 1, hold_b)
        return 0

    lax.fori_loop(0, chunks // 2, pair, 0)
    act(chunks - 1, hold_a)
    new = (acc[:, :LANES] + acc[:, LANES:] + acc_lo[...]) * ocean[...]
    new_out[...] = new
    new_edge_out[...] = new_out[pl.ds(pl.multiple_of((1 - core) * (px - edge_px), 8), edge_px), :]
    mine = jnp.where(part == 0, new[:part_px], new[part_px:])
    state[...] = mine.T[: state.shape[0]]
    keep_state = pltpu.make_async_copy(state, state_all.at[turn], sems.at[2 * chunks + 1])
    keep_state.start()
    keep_norm.wait()
    keep_state.wait()
    for t in range(chunks):
        keep_slope(t).wait()
        keep_act(t).wait()


def back_kernel(*refs, finish, begin, turn, width, k_main, k_rem, states):
    refs = list(refs)

    def take(count):
        out = refs[:count]
        del refs[:count]
        return out

    (at, ocean, pending_in) = take(3)
    if finish:
        (grad_n, sent, came, norm, norm_edge, inv, gain, first_sent, first_came, grad_branch, window, taps, w_in_hi, w_in_lo) = take(14)
    if begin:
        (cots, slope_hbm, norm_now, w_out, w_od, w_up) = take(6)
    if finish:
        (carry_out, pending_out, taps_out, home_out, lift_all) = take(5)
    if begin:
        (branch_out, hidden_out, grad_n_out, send_out, masked_all) = take(5)
    if finish:
        (ext, shifted, mixed, grad_lift, lift_sem) = take(5)
    if begin:
        (cot, slope, masked_part, begin_sems) = take(4)
    core, part = at[0], at[1]
    px = ocean.shape[0]
    rows = px // COLS
    part_px = px // 2
    if begin:
        get_cot = pltpu.make_async_copy(cots.at[turn], cot, begin_sems.at[0])
        get_slope = pltpu.make_async_copy(slope_hbm, slope, begin_sems.at[1])
        get_cot.start()
        get_slope.start()
    if finish:
        edge_px = norm_edge.shape[0]
        total = ocean_count(first_sent, first_came)
        ocean_edge = first_came[:edge_px, 2 * LANES :]
        zeros = jnp.zeros((rows + 2 * HALO, 8, width), F32)
        ext[:, :8, :] = zeros
        ext[:, 8 + COLS :, :] = zeros
        ext[pl.ds((rows + HALO) * core, HALO), 8 : 8 + COLS, :] = jnp.zeros((HALO, COLS, width), F32)
        part_rows = window.shape[0] - 2 * HALO
        for g in range(width // LANES):
            lanes = slice(g * LANES, (g + 1) * LANES)
            bias_sum = (sent[edge_px : edge_px + 1, lanes] + came[edge_px : edge_px + 1, lanes]) / total
            gain_sum = (sent[edge_px + 1 : edge_px + 2, lanes] + came[edge_px + 1 : edge_px + 2, lanes]) / total
            scale = inv[0:1, lanes] * gain[:, lanes]
            mix = scale * (grad_n[:, lanes] - ocean[...] * (bias_sum + norm[:, lanes] * gain_sum))
            mix_edge = scale * (came[:edge_px, lanes] - ocean_edge * (bias_sum + norm_edge[:, lanes] * gain_sum))
            ext[HALO : HALO + rows, 8 : 8 + COLS, lanes] = mix.reshape(rows, COLS, LANES)
            ext[pl.ds((rows + HALO) * (1 - core), HALO), 8 : 8 + COLS, lanes] = mix_edge.reshape(HALO, COLS, LANES)

        def group(g, _):
            lanes = group_lanes(g)
            depthwise(ext, shifted, taps, mixed, lanes, True, rows)
            grad_lift[:, lanes] = mixed[:, :, lanes].reshape(px, LANES) + grad_branch[:, lanes]
            for q in range(KW):
                sums = [None] * KW
                for i in range(part_rows):
                    for v in range(0, COLS, 8):
                        grad = shifted[KW - 1 - q, HALO + part * part_rows + i, v : v + 8, :]
                        for p in range(KW):
                            term = grad * window[i + p, v : v + 8, lanes]
                            sums[p] = term if sums[p] is None else sums[p] + term
                for p in range(KW):
                    taps_out[p * KW + q : p * KW + q + 1, lanes] = jnp.sum(sums[p], axis=0, keepdims=True)
            return 0

        lax.fori_loop(0, width // LANES, group, 0)
        keep_lift = pltpu.make_async_copy(
            grad_lift.at[pl.ds(pl.multiple_of(part * part_px, 8), part_px)], lift_all.at[pl.ds((turn + 1) * part_px, part_px)], lift_sem
        )
        keep_lift.start()
        high, low = split(grad_lift[...])
        both = dot_t(jnp.concatenate([high, low], axis=0), w_in_hi[...])
        grad_x = (both[:px] + both[px:]) + dot_t(high, w_in_lo[...])
        carry = grad_x[:, LANES:] + pending_in[...]
        carry_out[...] = carry
        pending_out[...] = grad_x[:, :LANES]
        part_x = jnp.where(part == 0, grad_x[:part_px, :LANES], grad_x[part_px:, :LANES])
        part_c = jnp.where(part == 0, carry[:part_px], carry[part_px:])
        home_out[:LANES] = part_x.T
        home_out[LANES:] = part_c.T
    if begin:
        get_cot.wait()
        grad_new = cot[...] + carry if finish else cot[...]
        lane = lax.broadcasted_iota(jnp.int32, (px, LANES), 1)
        masked = jnp.where(lane < states, grad_new * ocean[...], 0.0)
        masked_part[...] = jnp.where(part == 0, masked[:part_px], masked[part_px:])
        keep_masked = pltpu.make_async_copy(masked_part, masked_all.at[pl.ds(turn * part_px, part_px)], begin_sems.at[2])
        keep_masked.start()
        high_f = masked.astype(BF16).astype(F32)
        nothing = jnp.zeros((px, LANES), F32)
        high_w = jnp.concatenate([high_f, nothing], axis=1)
        low_w = jnp.concatenate([masked - high_f, nothing], axis=1)
        left = (high_w + pltpu.roll(low_w, SEG, 1) + pltpu.roll(high_w, 2 * SEG, 1)).astype(BF16)
        branch_out[...] = dot(left, w_out[...])
        chunks = w_od.shape[1] // CHUNK
        get_slope.wait()

        def chunk(t, _):
            cols = pl.ds(pl.multiple_of(t * CHUNK, CHUNK), CHUNK)
            high, low = split(dot(left, w_od[:, cols]) * slope[t])
            hidden_out[:px, cols] = high
            hidden_out[px:, cols] = low
            return 0

        lax.fori_loop(0, chunks, chunk, 0)
        both = dot_t(hidden_out[...], w_up[:k_main])
        grad_n_out[:, :k_main] = (both[:px] + both[px:]) + dot_t(hidden_out[:px], w_up[k_main : 2 * k_main])
        rest = dot_t(hidden_out[...], w_up[2 * k_main :])
        tail = rest[:px] + rest[px:] + pltpu.roll(rest[:px], LANES - 2 * k_rem, 1)
        grad_n_out[:, k_main:] = jnp.where(lane < k_rem, tail, 0.0)
        edge_px = send_out.shape[0] - 8
        for g in range(width // LANES):
            lanes = slice(g * LANES, (g + 1) * LANES)
            cells = grad_n_out[:, lanes]
            send_out[edge_px : edge_px + 1, lanes] = jnp.sum(cells, axis=0, keepdims=True)
            send_out[edge_px + 1 : edge_px + 2, lanes] = jnp.sum(cells * norm_now[:, lanes], axis=0, keepdims=True)
        send_out[edge_px + 2 :, :] = jnp.zeros((6, width), F32)
        send_out[:edge_px, :] = grad_n_out[pl.ds(pl.multiple_of((1 - core) * (px - edge_px), 8), edge_px), :]
        keep_masked.wait()
    if finish:
        keep_lift.wait()


def weight_kernel(at, norm, gain, bias, hidden, send, *rest, quarter, finish):
    if finish:
        taps, keep_in, give_in, sums_in, keep_out, give_out, sums_out, *up_row = rest
    else:
        keep_out, give_out, sums_out, *up_row = rest
    core = at[0]
    part = at[1]
    px = norm.shape[0]
    tap_rows = sums_out.shape[0] - 8
    if finish:
        sums_out[:tap_rows] = sums_in[:tap_rows] + taps[...]
        sums_out[tap_rows:] = sums_in[tap_rows:] + send[send.shape[0] - 8 :]
    else:
        sums_out[:tap_rows] = jnp.zeros((tap_rows, sums_out.shape[1]), F32)
        sums_out[tap_rows:] = send[send.shape[0] - 8 :]
    window = round_up(quarter, LANES)
    base = (quarter // LANES) * LANES
    normed = norm[...] * gain[...] + bias[...]
    second = pltpu.roll(normed[:, base : base + window], window - (quarter - base), 1)
    mine = jnp.where(part == 0, normed[:, :window], second)
    lane = lax.broadcasted_iota(jnp.int32, (px, window), 1)
    mine = jnp.where(lane < quarter, mine, jnp.where(lane == quarter, 1.0, 0.0))
    high, low = split(mine.T[: keep_out.shape[0]])
    half = keep_out.shape[1]

    def chunk(side, start, size):
        acc_out = (keep_out, give_out)[side]
        here = pl.ds(start, size)
        actual = core if side == 0 else 1 - core
        cols = pl.ds(pl.multiple_of(actual * half + start, LANES), size)
        new = dot(high, hidden[:px, cols]) + dot(high, hidden[px:, cols]) + dot(low, hidden[:px, cols])
        acc_out[:, here] = (keep_in, give_in)[side][:, here] + new if finish else new

    for side in range(2):

        def step(t, _):
            chunk(side, pl.multiple_of(t * CHUNK, CHUNK), CHUNK)
            return 0

        lax.fori_loop(0, half // CHUNK, step, 0)
        if half % CHUNK:
            chunk(side, half // CHUNK * CHUNK, half % CHUNK)
    if up_row:
        line = quarter // 8 * 8
        for side, acc_out in ((core, keep_out), (1 - core, give_out)):
            up_row[0][:, pl.ds(pl.multiple_of(side * half, LANES), half)] = acc_out[line : line + 8, :]


VMEM_SPEC = pl.BlockSpec(memory_space=pltpu.VMEM)
SMEM_SPEC = pl.BlockSpec(memory_space=pltpu.SMEM)
HBM_SPEC = pl.BlockSpec(memory_space=pltpu.HBM)


def out(*shape, dtype=F32):
    return jax.ShapeDtypeStruct(shape, dtype)


def in_hbm(values):
    return pltpu.with_memory_space_constraint(values, pltpu.HBM)


def call(kernel, name, args, outs, scratch, limit, *, micros, smem=0, hbm=(), hbm_outs=(), vmem_outs=(), aliases=None, stacked=()):
    args = [in_hbm(a) if i in hbm else a for i, a in enumerate(args)]
    specs = [SMEM_SPEC if i < smem else HBM_SPEC if i in hbm else VMEM_SPEC for i in range(len(args))]
    hbm_outs = tuple(hbm_outs) + tuple(i for i, _ in stacked)
    aliases = dict(aliases or {})
    used = len(args)
    for i, buffer in stacked:
        if buffer is not None:
            aliases[len(args)] = i
            args.append(in_hbm(buffer))
            specs.append(HBM_SPEC)
    extra = len(args) - used

    def body(*refs):
        kernel(*refs[:used], *refs[used + extra :])

    return pl.pallas_call(
        body,
        in_specs=specs,
        out_specs=[HBM_SPEC if i in hbm_outs else VMEM_SPEC for i in range(len(outs))],
        out_shape=[
            pltpu.HBM(o.shape, o.dtype) if i in hbm_outs else pltpu.VMEM(o.shape, o.dtype) if i in vmem_outs else o
            for i, o in enumerate(outs)
        ],
        scratch_shapes=scratch,
        input_output_aliases=aliases,
        compiler_params=pltpu.CompilerParams(vmem_limit_bytes=limit * MIB),
        cost_estimate=pl.CostEstimate(flops=int(micros * 1.1e9), bytes_accessed=1024, transcendentals=0),
        name=name,
    )(*args)


def start_kernel(at, first, second, prev_out, cur_out, ocean_out, send_out, *, states, forces):
    core, part = at[0], at[1]
    block = first.shape[1]
    rows = first.shape[0]
    mask_row = 2 * states + forces

    def turn(values):
        prev = jnp.concatenate([values[: states + forces], jnp.zeros((LANES - states - forces, block), F32)], axis=0).T
        cur = jnp.concatenate([values[states + forces : mask_row], jnp.zeros((LANES - states, block), F32)], axis=0).T
        mask = jnp.broadcast_to(values[mask_row : mask_row + 1], (LANES, block)).T
        return prev, cur, mask

    zero, one = first[...], second[...]
    swap = part == 1
    top, low = jnp.where(swap, one, zero), jnp.where(swap, zero, one)
    count = jnp.sum(top[mask_row : mask_row + 1]) + jnp.sum(low[mask_row : mask_row + 1])
    for i, values in enumerate((top, low)):
        prev, cur, mask = turn(values)
        here = slice(i * block, (i + 1) * block)
        prev_out[here] = prev
        cur_out[here] = cur
        ocean_out[here] = mask
    at_edge = pl.ds(pl.multiple_of((1 - core) * block, 8), block)
    send_out[:block, :LANES] = prev_out[at_edge, :]
    send_out[:block, LANES : 2 * LANES] = cur_out[at_edge, :]
    send_out[:block, 2 * LANES :] = ocean_out[at_edge, :]
    send_out[block:] = jnp.full((8, 3 * LANES), count)


def pack_kernel(at, first, second, force_out, force_send, cot_out, *, states, forces):
    core, part = at[0], at[1]
    steps, rows, block = first.shape
    lane = lax.broadcasted_iota(jnp.int32, (block, LANES), 1)
    for j in range(steps):
        turned = [
            jnp.concatenate([values[j], jnp.zeros((LANES - rows, block), F32)], axis=0).T for values in (first, second)
        ]
        top, low = jnp.where(part == 1, turned[1], turned[0]), jnp.where(part == 1, turned[0], turned[1])
        for i, values in enumerate((top, low)):
            cot_out[j, i * block : (i + 1) * block] = jnp.where(lane < states, values, 0.0)
            force_out[j, i * block : (i + 1) * block] = jnp.where(lane < states, 0.0, values)
        force_send[j] = force_out[j, pl.ds(pl.multiple_of((1 - core) * block, 8), block), :]


def reorder(source, target, spans):
    for start, size, place in spans:
        target[:, place : place + size] = source[:, start : start + size]


def up_kernel(w_up_t, up_all, raw, turned, sems, *, k_main, k_rem, spans):
    slots, block = raw.shape[0], raw.shape[1]
    blocks = k_main // block

    def get(t, size):
        slot = lax.rem(t, slots)
        return pltpu.make_async_copy(
            w_up_t.at[pl.ds(pl.multiple_of(t * block, 8), size)], raw.at[slot, pl.ds(0, size)], sems.at[slot]
        )

    for t in range(slots):
        get(t, block).start()
    turned[...] = jnp.zeros_like(turned)

    def main(t, _):
        get(t, block).wait()
        reorder(raw.at[lax.rem(t, slots)], turned, spans)

        @pl.when(t + slots < blocks)
        def _():
            get(t + slots, block).start()

        @pl.when(t + slots == blocks)
        def _():
            get(t + slots, k_rem).start()

        high, low = split(turned[...])
        up_all[pl.ds(pl.multiple_of(t * block, block), block), :] = high
        up_all[pl.ds(pl.multiple_of(k_main + t * block, block), block), :] = low
        return 0

    lax.fori_loop(0, blocks, main, 0)
    get(blocks, k_rem).wait()
    reorder(raw.at[blocks % slots, pl.ds(0, k_rem)], turned.at[pl.ds(0, k_rem)], spans)
    high, low = split(turned[:k_rem])
    base = 2 * k_main
    up_all[base : base + k_rem] = high
    up_all[base + k_rem : base + 2 * k_rem] = high
    up_all[base + 2 * k_rem : base + 3 * k_rem] = low
    up_all[base + 3 * k_rem :] = jnp.zeros((LANES - 3 * k_rem, up_all.shape[1]), BF16)


def down_kernel(w_down, out_parts, od_fwd, od_bwd, down, product, ordered, sems, *, spans):
    pieces = sems.shape[0]
    piece = down.shape[1] // pieces

    def get(t):
        cols = pl.ds(pl.multiple_of(t * piece, LANES), piece)
        return pltpu.make_async_copy(w_down.at[:, cols], down.at[:, cols], sems.at[t])

    for t in range(pieces):
        get(t).start()
    ordered[...] = jnp.zeros_like(ordered)

    def multiply(t, _):
        cols = pl.ds(pl.multiple_of(t * piece, LANES), piece)
        get(t).wait()
        high, low = split(down[:, cols])
        both = dot(out_parts[...], high)
        product[:, cols] = (both[:SEG] + both[SEG:]) + dot(out_parts[:SEG], low)
        return 0

    lax.fori_loop(0, pieces, multiply, 0)
    reorder(product, ordered.at[pl.ds(0, SEG)], spans)

    def spread(t, _):
        cols = pl.ds(pl.multiple_of(t * CHUNK, CHUNK), CHUNK)
        values = ordered[:, cols]
        high, low = split(values)
        od_bwd[:SEG, cols] = high[:SEG]
        od_bwd[SEG : 2 * SEG, cols] = high[:SEG]
        od_bwd[2 * SEG : 3 * SEG, cols] = low[:SEG]
        od_bwd[3 * SEG :, cols] = jnp.zeros((od_bwd.shape[0] - 3 * SEG, CHUNK), BF16)
        high, low = split(values.T)
        od_fwd[cols, :LANES] = high
        od_fwd[cols, LANES:] = low
        return 0

    lax.fori_loop(0, ordered.shape[1] // CHUNK, spread, 0)


def last_kernel(
    at, masked_hbm, x_hbm, lifts_hbm, lifted_hbm, act_hbm, down_hbm, b_down, sums, taps, up_row, token, table_keep, table_give, hidden_keep, hidden_give,
    table,    masked, x_parts, lifts, lifted, act, down, masked_t, x_t, g_hidden, natural, g_parts, sems, *, spans, blocks,
):
    chunks = act.shape[0]
    half = hidden_keep.shape[1]
    width = table.shape[1]
    scale = (at[1] == 0).astype(F32)
    tap_rows = taps.shape[0]
    pairs = [(masked_hbm, masked), (x_hbm, x_parts), (lifts_hbm, lifts), (lifted_hbm, lifted)]
    firsts = [pltpu.make_async_copy(pair[0], pair[1], sems.at[i]) for i, pair in enumerate(pairs)]
    downs = [
        pltpu.make_async_copy(down_hbm.at[pl.ds(start, size)], down.at[pl.ds(start, size)], sems.at[4 + i])
        for i, (start, size) in enumerate(blocks)
    ]

    def get(t):
        return pltpu.make_async_copy(act_hbm.at[t], act.at[t], sems.at[4 + len(blocks) + t])

    firsts[0].start()
    for t in range(chunks):
        get(t).start()
    for copy in firsts[1:] + downs:
        copy.start()
    firsts[0].wait()
    turned = masked[...].T[:SEG]
    high = turned.astype(BF16)
    masked_t[:SEG] = high
    masked_t[SEG:] = (turned - high.astype(F32)).astype(BF16)
    total = jnp.sum(turned, axis=1, keepdims=True)

    def chunk(t, _):
        get(t).wait()
        high, low = split(act[t])
        both = dot(masked_t[...], high)
        sums_now = (both[:SEG] + both[SEG:]) + dot(masked_t[:SEG], low)
        g_hidden[:, pl.ds(pl.multiple_of(t * CHUNK, CHUNK), CHUNK)] = sums_now
        return 0

    lax.fori_loop(0, chunks, chunk, 0)
    hidden_keep[...] = g_hidden[:, pl.ds(pl.multiple_of(at[0] * half, LANES), half)]
    hidden_give[...] = g_hidden[:, pl.ds(pl.multiple_of((1 - at[0]) * half, LANES), half)]
    for start, size, place in spans:
        natural[:, start : start + size] = g_hidden[:, place : place + size]
    high, low = split(natural[...])
    g_parts[:SEG] = high
    g_parts[SEG:] = low
    for copy in firsts[1:]:
        copy.wait()
    high, low = split(x_parts[...].T)
    x_t[0] = high
    x_t[1] = low
    for start in range(0, width, CHUNK):
        size = min(CHUNK, width - start)
        lanes = slice(start, start + size)
        high, low = split(lifted[:, :, lanes].reshape(lifts.shape[0], size))
        both = dot(masked_t[...], high)
        lifted_sum = (both[:SEG] + both[SEG:]) + dot(masked_t[:SEG], low)
        grads = lifts[:, lanes]
        high, low = split(grads)
        g_in = dot(x_t[0], high) + dot(x_t[1], high) + dot(x_t[0], low)
        table[:88, lanes] = g_in[:88]
        table[88:168, lanes] = g_in[LANES : LANES + 80]
        table[168:224, lanes] = sums[:tap_rows, lanes] + taps[:, lanes]
        table[224:304, lanes] = lifted_sum + total * b_down[:, lanes]
        table[304:311, lanes] = sums[tap_rows : tap_rows + 7, lanes] * scale
        table[311:312, lanes] = jnp.sum(grads, axis=0, keepdims=True)
    for (start, size), copy in zip(blocks, downs):
        copy.wait()
        high, low = split(down[start : start + size])
        both = dot_t(g_parts[...], high)
        g_out = (both[:SEG] + both[SEG:]) + dot_t(g_parts[:SEG], low)
        table[224:304, start : start + size] += g_out
    table[312:] = jnp.zeros((table.shape[0] - 312, width), F32)
    for i, start in enumerate(range(0, up_row.shape[1], width)):
        size = min(width, up_row.shape[1] - start)
        table[312 + i : 313 + i, :size] = up_row[:1, start : start + size] * scale
    table[316:317, :LANES] = jnp.sum(masked[...], axis=0, keepdims=True)
    rows = table_keep.shape[0]
    table_keep[...] = table[pl.ds(pl.multiple_of(at[0] * rows, 8), rows), :]
    table_give[...] = table[pl.ds(pl.multiple_of((1 - at[0]) * rows, 8), rows), :]


def flags(at):
    return at[3], at[4], at[5], at[2]


def cut_first_kernel(at, keep, got, keep_a, give_a, keep_b, give_b, *, rows, cols):
    x, y, _, _ = flags(at)

    def part(row, k):
        here = (slice(row * rows, (row + 1) * rows), slice(k * cols, (k + 1) * cols))
        return keep[here] + got[here]

    for i, (even, odd) in enumerate(((0, 1), (2, 3))):
        one, two = part(0, even), part(0, odd)
        keep_a[i] = jnp.where(x == 0, one, two)
        give_a[i] = jnp.where(x == 0, two, one)
    for i, (low, top) in enumerate(((0, 2), (1, 3))):
        one, two = part(1, low), part(1, top)
        keep_b[i] = jnp.where(y == 0, one, two)
        give_b[i] = jnp.where(y == 0, two, one)


def cut_second_kernel(at, keep_a, got_a, keep_b, got_b, keep_a_out, give_a_out, keep_b_out, give_b_out):
    x, y, _, _ = flags(at)
    for bit, keep, got, keep_out, give_out in (
        (y, keep_a, got_a, keep_a_out, give_a_out),
        (x, keep_b, got_b, keep_b_out, give_b_out),
    ):
        keep_out[...] = keep[bit] + got[bit]
        give_out[...] = keep[1 - bit] + got[1 - bit]


def cut_third_kernel(at, keep_a, got_a, keep_b, got_b, keep_out, give_out):
    _, _, _, side = flags(at)
    one, two = keep_a[...] + got_a[...], keep_b[...] + got_b[...]
    keep_out[...] = jnp.where(side == 0, one, two)
    give_out[...] = jnp.where(side == 0, two, one)


def turn_sum_kernel(at, keep, got, out_ref):
    out_ref[...] = (keep[...] + got[...]).T


def quarter_rows_kernel(at, keep, got, *outs):
    rows = outs[0].shape[0]
    pair = at[5]
    for b, out_ref in enumerate(outs):
        place = pl.multiple_of((pair ^ b) * rows, 8)
        out_ref[...] = keep[pl.ds(place, rows), :] + got[pl.ds(place, rows), :]


def quarter_cols_kernel(at, keep, got, *outs):
    cols = outs[0].shape[1]
    pair = at[5]
    parts = [keep[:, k * cols : (k + 1) * cols] + got[:, k * cols : (k + 1) * cols] for k in range(4)]
    for b, out_ref in enumerate(outs):
        k = pair ^ b
        low = jnp.where(k == 0, parts[0], parts[1])
        top = jnp.where(k == 2, parts[2], parts[3])
        out_ref[...] = jnp.where(k < 2, low, top)


def sum_two_kernel(at, a, b, out_ref):
    out_ref[...] = a[...] + b[...]


def sum_four_kernel(at, a, b, c, d, out_ref):
    out_ref[...] = (a[...] + b[...]) + (c[...] + d[...])


def join_rows_kernel(at, a, b, c, d, out_ref):
    rows = a.shape[0]
    for flip, ref in enumerate((a, b, c, d)):
        out_ref[pl.ds(pl.multiple_of((at[5] ^ flip) * rows, 8), rows), :] = ref[...]


def share_down_kernel(at, a, b, w_hi, w_lo, out_ref):
    high, low = split(a[...] + b[...])
    out_ref[...] = dot(w_hi[...], high) + dot(w_hi[...], low) + dot(w_lo[...], high)


def table_kernel(at, mine, other, g_in, g_dw, g_out, rows_out, *, states, forces):
    core = at[0]
    half = mine.shape[0]
    channels = g_in.shape[1]

    def get(start, size):
        pieces = []
        for base in (0, half):
            low, top = max(start, base), min(start + size, base + half)
            if low < top:
                here = slice(low - base, top - base)
                pieces.append(jnp.where(core == (base > 0), mine[here, :channels], other[here, :channels]))
        return pieces[0] if len(pieces) == 1 else jnp.concatenate(pieces, axis=0)

    g_in[:states] = get(0, 88)[:states]
    g_in[states : 2 * states] = get(88, 80)[:states]
    g_in[2 * states :] = get(0, 88)[states : states + forces]
    taps = get(168, 56)
    for p in range(KW):
        g_dw[p] = taps[p * KW : (p + 1) * KW]
    g_out[...] = get(224, 80)[:states]
    for i, start in enumerate((304, 312)):
        piece = jnp.where(core == (start >= half), mine[start % half : start % half + 8], other[start % half : start % half + 8])
        rows_out[8 * i : 8 * i + 8] = piece


def going_kernel(at, *refs, states, forces):
    homes, out_ref = refs[:-1], refs[-1]
    steps = len(homes)
    block = out_ref.shape[1]
    for j in range(steps):
        out_ref[8 * j : 8 * j + 8] = jnp.concatenate([homes[j][states : states + forces], jnp.zeros((8 - forces, block), F32)], axis=0)
    out_ref[8 * steps : 8 * steps + 80] = homes[0][:80]
    out_ref[8 * steps + 80 :] = homes[0][LANES : LANES + 80]


def roll_kernel(at, states, forces, out_ref):
    steps = out_ref.shape[0]
    high = states.shape[1]
    for i in range(steps):
        here = lax.rem(i - at[6] + steps, steps)
        out_ref[i, :high] = states[here]
        out_ref[i, high:] = forces[pl.ds(pl.multiple_of(here * 8, 8), 8), :]


def home_kernel(at, gone, ending, predicted, grad_forcing, grad_init, *, states):
    steps = gone.shape[0]
    total = gone[0, SEG:]
    for i in range(steps):
        predicted[i] = gone[lax.rem(at[6] - i + steps, steps), :states]
        if i:
            total = total + gone[i, SEG:]
    grad_forcing[...] = total
    base = 8 * steps
    prev, cur = ending[base : base + SEG][:states], ending[base + SEG : base + 2 * SEG][:states]
    single = at[7] == 1
    grad_init[0] = jnp.where(single, 0.0, prev)
    grad_init[1] = jnp.where(single, cur + prev, cur)


def pad_to(values, shape):
    return jnp.pad(values, [(0, size - have) for size, have in zip(shape, values.shape)])


def per_device(
    init_states, forcing, history, land_mask, w_in, b_in, w_dw, bn_gain, bn_bias, w_up, b_up, w_down, b_down, w_out, b_out, cotangent
):
    steps = lax.axis_size("step")
    devices_z = lax.axis_size("rows")
    step = lax.axis_index("step")
    depth = lax.axis_index("rows")
    core, pair = step % 2, step // 2
    side, part = depth % 2, depth // 2
    both_axes = ("step", "rows")
    block = land_mask.shape[0]
    px = 2 * block
    rows = px // COLS
    states = w_out.shape[0]
    forces = forcing.shape[2]
    channels = w_up.shape[1]
    hidden = w_up.shape[0]
    width = round_up(channels, LANES)
    ff_block = hidden // steps
    half = round_up(hidden // 2, LANES)
    wide = 2 * half
    spans = [(s * ff_block, ff_block, (s % 2) * half + (s // 2) * ff_block) for s in range(steps)]
    k_main = channels // CHUNK * CHUNK
    k_rem = channels - k_main
    col_block = channels // devices_z

    def place(s, z):
        return s * devices_z + z

    cells = [(k, c, h, q) for k in range(steps // 2) for c in range(2) for h in range(2) for q in range(2)]
    fetch_perms = [
        [(place(2 * k + q, 2 * c + (b ^ h)), place(2 * k + c, 2 * h + q)) for k, c, h, q in cells] for b in range(2)
    ]

    column_perm = [(place(2 * k + c, 2 * h + q), place(2 * k + q, 2 * c + h)) for k, c, h, q in cells]
    siblings = [(s, s ^ 1) for s in range(steps)]

    def to_sibling(values):
        return lax.ppermute(values, "step", siblings)

    def shift_back(values, j):
        return values if j == 0 else lax.ppermute(values, "step", [((s + j) % steps, s) for s in range(steps)])

    def fetch_own(values):
        got = [lax.ppermute(values, both_axes, perm) for perm in fetch_perms]
        return got

    def turn_round(values):
        n = values.shape[0]
        doubled = jnp.flip(jnp.concatenate([values, values]), axis=0)
        return lax.dynamic_slice_in_dim(doubled, n - 1 - step % n, n, axis=0)

    def rotate(values, by):
        return lax.dynamic_slice_in_dim(jnp.concatenate([values, values]), by, steps, axis=0)

    def from_later(values):
        if steps == ROLL:
            return rotate(lax.all_to_all(turn_round(values), "step", 0, 0, tiled=True), step)
        return jnp.stack([shift_back(values[j], j) for j in range(ROLL)])

    def to_later(values):
        if steps == ROLL:
            return turn_round(lax.all_to_all(rotate(values, (steps - step) % steps), "step", 0, 0, tiled=True))
        return jnp.stack([lax.ppermute(values[j], "step", [(s, (s + j) % steps) for s in range(steps)]) for j in range(ROLL)])

    at = jnp.stack([core, part, side, pair % 2, (pair // 2) % 2, pair, step % ROLL, history[0, 0]]).astype(jnp.int32)
    mask_row = land_mask.astype(F32)[None]
    current = init_states[0, 0, 1]
    previous = jnp.where(history[0, 0] == 2, init_states[0, 0, 0], current)
    payload = jnp.concatenate([previous, forcing[0, 0], current, mask_row], axis=0)
    timed = jnp.concatenate([cotangent[0, :, 0], jnp.broadcast_to(forcing[0], (ROLL,) + forcing.shape[2:])], axis=1)
    payload, timed = lax.optimization_barrier((payload, timed))
    payload = fetch_own(payload)
    timed = from_later(timed)

    def in_rows(values):
        top = jnp.concatenate([values[:states], values[2 * states :]], axis=0)
        bottom = values[states : 2 * states]
        return jnp.concatenate([jnp.pad(v, ((0, LANES - v.shape[0]), (0, 0))) for v in (top, bottom)], axis=0)

    def row(values, size):
        return jnp.pad(values, (0, size - values.shape[0]))[None]

    w_in_hi, w_in_lo = split_outside(pad_to(in_rows(w_in.T), (2 * LANES, width)))
    w_oi = pad_to(in_rows(jnp.dot(w_out, w_in, precision=HIGHEST).T), (2 * LANES, LANES))
    w_oi_hi, w_oi_lo = split_outside(w_oi)
    b_new = row(jnp.dot(w_out, b_in + b_down, precision=HIGHEST) + b_out, LANES)
    taps = jnp.broadcast_to(
        pad_to(w_dw.reshape(channels, KW * KW).T, (KW * KW, width))[:, None], (KW * KW, 8, width)
    )
    gain, bias = row(bn_gain, width), row(bn_bias, width)
    row_hi, row_lo = split_outside(pad_to(w_out, (SEG, channels)))
    out_parts = jnp.concatenate([row_hi, row_lo], axis=0)
    pieces = 5
    w_od_fwd, w_od_bwd = call(
        functools.partial(down_kernel, spans=spans), "down", (w_down, out_parts),
        [out(wide, 2 * LANES, dtype=BF16), out(2 * LANES, wide, dtype=BF16)],
        [pltpu.VMEM((channels, hidden), F32), pltpu.VMEM((SEG, hidden), F32), pltpu.VMEM((LANES, wide), F32), pltpu.SemaphoreType.DMA((pieces,))],
        20, micros=7, hbm=(0,), vmem_outs=(0, 1),
    )
    out_hi, out_lo = split_outside(pad_to(w_out, (SEG, width)))
    w_out_bwd = pad_to(jnp.concatenate([out_hi, out_hi, out_lo], axis=0), (2 * LANES, width))
    b_in_row = row(b_in, width)
    b_up_row = pad_to(b_up.reshape(steps // 2, 2, ff_block).swapaxes(0, 1).reshape(2, hidden // 2), (2, half)).reshape(1, wide)
    b_down_row = row(b_down, width)
    w_block = lax.dynamic_slice_in_dim(w_out, depth * col_block, col_block, axis=1).T
    w_block_hi, w_block_lo = split_outside(pad_to(w_block, (col_block, SEG)))
    prev, cur, ocean, first_sent = call(
        functools.partial(start_kernel, states=states, forces=forces), "start", (at, *payload),
        [out(px, LANES), out(px, LANES), out(px, LANES), out(block + 8, 3 * LANES)], [], 4, micros=1, smem=1,
    )
    first_came = to_sibling(first_sent)
    ready = lax.optimization_barrier(
        (w_up.T, timed, w_in_hi, w_in_lo, w_oi_hi, w_oi_lo, b_new, taps, gain, bias, w_out_bwd, b_in_row, b_up_row, b_down_row, w_block_hi, w_block_lo, at, first_sent)
    )
    up_source, timed, w_in_hi, w_in_lo, w_oi_hi, w_oi_lo, b_new, taps, gain, bias, w_out_bwd, b_in_row, b_up_row, b_down_row, w_block_hi, w_block_lo, at, first_sent = ready
    timed = fetch_own(timed)
    (w_up_all,) = call(
        functools.partial(up_kernel, k_main=k_main, k_rem=k_rem, spans=spans), "up", (up_source,),
        [out(2 * k_main + LANES, wide, dtype=BF16)],
        [pltpu.VMEM((3, k_main // 8, hidden), F32), pltpu.VMEM((k_main // 8, wide), F32), pltpu.SemaphoreType.DMA((3,))],
        10, micros=7, hbm=(0,), vmem_outs=(0,),
    )
    first_came, w_up_all = lax.optimization_barrier((first_came, w_up_all))
    force, force_send, cots = call(
        functools.partial(pack_kernel, states=states, forces=forces), "pack", (at, *timed),
        [out(ROLL, px, LANES), out(ROLL, block, LANES), out(ROLL, px, LANES)], [], 6, micros=2, smem=1,
    )
    force_edge = to_sibling(force_send)

    chunks = wide // CHUNK
    x_all, lifted_all, act_all, state_all = None, None, None, None
    kept = []
    prev_edge, cur_edge, prev_lanes, cur_lanes = first_came, first_came, 0, LANES
    for j in range(ROLL):
        mixed, stats, base, window, x_all, lifted_all = call(
            functools.partial(mix_kernel, turn=j, cur_lanes=cur_lanes, prev_lanes=prev_lanes), "mix",
            (at, cur, cur_edge, prev, prev_edge) + ((force, force_edge) if j else (at, at)) + (w_in_hi, w_in_lo, b_in_row, w_oi_hi, w_oi_lo, b_new, taps, ocean),
            [
                out(px, width), out(8, width), out(px, LANES), out(HALO + 2 * HALO, COLS, width), out(ROLL * block, 2 * LANES),
                out(ROLL * HALO, COLS, width),
            ],
            [
                pltpu.VMEM((rows + 2 * HALO, COLS + 16, width), F32), pltpu.VMEM((KW, rows + 2 * HALO, COLS, LANES), F32),
                pltpu.VMEM((rows, COLS, width), F32), pltpu.VMEM((block, 2 * LANES), F32), pltpu.SemaphoreType.DMA((3,)),
            ],
            12, micros=4.5, smem=1, hbm_outs=(3,), stacked=((4, x_all), (5, lifted_all)),
        )
        stats_other = to_sibling(stats)
        new, new_edge, norm_edge, inv, norm, slope, act_all, state_all = call(
            functools.partial(feed_kernel, turn=j, width=width, k_main=k_main, k_rem=k_rem), "feed",
            (at, mixed, stats, stats_other, first_sent, first_came, gain, bias, ocean, base, w_up_all, b_up_row, w_od_fwd),
            [
                out(px, LANES), out(block, LANES), out(block, width), out(8, width), out(px, width),
                out(chunks, px, CHUNK), out(chunks, ROLL * block, CHUNK), out(ROLL, SEG, block),
            ],
            [
                pltpu.VMEM((2 * px, k_main), BF16), pltpu.VMEM((px, LANES), BF16),
                pltpu.VMEM((px, CHUNK), F32), pltpu.VMEM((px, LANES), F32), pltpu.VMEM((px, CHUNK), F32), pltpu.VMEM((px, CHUNK), F32),
                pltpu.VMEM((px, CHUNK), F32), pltpu.VMEM((px, width), F32), pltpu.VMEM((chunks, px, CHUNK), F32),
                pltpu.VMEM((chunks, block, CHUNK), F32), pltpu.VMEM((SEG, block), F32), pltpu.SemaphoreType.DMA((2 * chunks + 2,)),
            ],
            14, micros=8.5, smem=1, hbm_outs=(4, 5), stacked=((6, act_all), (7, state_all)),
        )
        prev, prev_edge, prev_lanes, cur = cur, cur_edge, cur_lanes, new
        if j < ROLL - 1:
            cur_edge, cur_lanes = to_sibling(new_edge), 0
        norm_edge = to_sibling(norm_edge)
        kept.append((window, norm, norm_edge, slope, inv))

    states_home = lax.ppermute(state_all, both_axes, column_perm)
    quarter = channels // 2
    acc_rows = round_up(quarter + 1, 8)
    tap_rows = round_up(KW * KW, 8)
    carry, pending = None, jnp.zeros((px, LANES), F32)
    previous_step, keep_acc, give_acc, sums, lift_all, masked_all = None, None, None, None, None, None
    homes = []
    begin_scratch = [
        pltpu.VMEM((px, LANES), F32), pltpu.VMEM((chunks, px, CHUNK), F32), pltpu.VMEM((block, LANES), F32), pltpu.SemaphoreType.DMA((3,)),
    ]
    finish_scratch = [
        pltpu.VMEM((rows + 2 * HALO, COLS + 16, width), F32), pltpu.VMEM((KW, rows + 2 * HALO, COLS, LANES), F32),
        pltpu.VMEM((rows, COLS, width), F32), pltpu.VMEM((px, width), F32), pltpu.SemaphoreType.DMA,
    ]
    for j in range(ROLL - 1, -2, -1):
        finish, begin = j < ROLL - 1, j >= 0
        if finish:
            pending, keep_acc, give_acc = lax.optimization_barrier((pending, keep_acc, give_acc))
        if j == ROLL - 4:
            pending, states_home = lax.optimization_barrier((pending, states_home))
        args, outs, scratch, stacked, hbm = [at, ocean, pending], [], [], [], ()
        if finish:
            window, norm, norm_edge, slope, inv = kept[j + 1]
            grad_n, sent, came, grad_branch = previous_step
            args += [grad_n, sent, came, norm, norm_edge, inv, gain, first_sent, first_came, grad_branch, window, taps, w_in_hi, w_in_lo]
            outs += [out(px, LANES), out(px, LANES), out(tap_rows, width), out(2 * LANES, block), out(ROLL * block, width)]
            stacked.append((4, lift_all))
            scratch += finish_scratch
        if begin:
            hbm = (len(args), len(args) + 1)
            args += [cots, kept[j][3], kept[j][1], w_out_bwd, w_od_bwd, w_up_all]
            outs += [out(px, width), out(2 * px, wide, dtype=BF16), out(px, width), out(block + 8, width), out(ROLL * block, LANES)]
            stacked.append((len(outs) - 1, masked_all))
            scratch += begin_scratch
        kernel = functools.partial(
            back_kernel, finish=finish, begin=begin, turn=j, width=width, k_main=k_main, k_rem=k_rem, states=states
        )
        results = list(
            call(kernel, "back", args, outs, scratch, 18, micros=7 * finish + 7.5 * begin, smem=1, hbm=hbm, stacked=stacked)
        )
        if finish:
            carry, pending, tap_sum, home, lift_all = results[:5]
            results = results[5:]
            homes.append(home)
        if begin:
            grad_branch, hidden_now, grad_n, sent, masked_all = results
            came = to_sibling(sent)
            previous_step = (grad_n, sent, came, grad_branch)
            keep_acc, give_acc, sums, *up_row = call(
                functools.partial(weight_kernel, quarter=quarter, finish=finish), "weight",
                (at, kept[j][1], gain, bias, hidden_now, sent) + ((tap_sum, keep_acc, give_acc, sums) if finish else ()),
                [out(acc_rows, half), out(acc_rows, half), out(tap_rows + 8, width)] + ([] if j else [out(8, wide)]), [], 8, micros=5, smem=1,
                aliases=({7: 0, 8: 1, 9: 2} if j else {7: 0, 9: 2}) if finish else None, vmem_outs=(0, 1, 2) if j else (),
            )
            if j == 0:
                window, norm, norm_edge, slope, inv = kept[0]
                give_acc, came, norm_edge = lax.optimization_barrier((give_acc, came, norm_edge))
                kept[0] = (window, norm, norm_edge, slope, inv)
                previous_step = (grad_n, sent, came, grad_branch)

    def trade(values, axis, flip):
        return lax.ppermute(values, axis, [(i, i ^ flip) for i in range(lax.axis_size(axis))])

    def pick(first, second, bit):
        return jnp.where(bit == 0, first, second), jnp.where(bit == 0, second, first)

    token = [tap_sum]

    def local(kernel, args, outs, limit=8, **options):
        def body(at_ref, *refs):
            kernel(at_ref, *refs[: len(args)], *refs[len(args) + 1 : -1], **options)
            refs[-1][...] = refs[len(args)][:8, :LANES]

        results = call(body, kernel.__name__, (at, *args, token[0]), outs + [out(8, LANES)], [], limit, micros=1, smem=1)
        token[0] = results[-1]
        return results[:-1]

    direct = steps == 8 and devices_z == 4
    home_outs = [out(ROLL, states, block), out(8, block), out(2, states, block)]
    got = trade(give_acc, "step", 1)
    if direct:
        pieces = [out(2, col_block, ff_block)] * 4
        keep_a, give_a, keep_b, give_b = local(cut_first_kernel, (keep_acc, got), pieces, 16, rows=col_block, cols=ff_block)
        got_a, got_b = trade(give_a, "step", 2), trade(give_b, "step", 4)
    part_px = ROLL * block
    blocks = [(start, min(CHUNK, channels - start)) for start in range(0, channels, CHUNK)]
    table_keep, table_give, hidden_keep, hidden_give = call(
        functools.partial(last_kernel, spans=spans, blocks=blocks), "last",
        (
            at, masked_all, x_all, lift_all, lifted_all, act_all, w_down, b_down_row, sums,
            tap_sum, *up_row, token[0],
        ),
        [out(160, width), out(160, width), out(SEG, half), out(SEG, half)],
        [
            pltpu.VMEM((320, width), F32),
            pltpu.VMEM((part_px, LANES), F32), pltpu.VMEM((part_px, 2 * LANES), F32), pltpu.VMEM((part_px, width), F32),
            pltpu.VMEM(lifted_all.shape, F32), pltpu.VMEM((chunks, part_px, CHUNK), F32), pltpu.VMEM((channels, hidden), F32),
            pltpu.VMEM((2 * SEG, part_px), BF16), pltpu.VMEM((2, 2 * LANES, part_px), BF16), pltpu.VMEM((SEG, wide), F32),
            pltpu.VMEM((SEG, hidden), F32), pltpu.VMEM((2 * SEG, hidden), BF16),
            pltpu.SemaphoreType.DMA((4 + len(blocks) + chunks,)),
        ],
        44, micros=12, smem=1, hbm=(1, 2, 3, 4, 5, 6),
    )
    other = trade(table_give, "step", 1)
    hidden_other = trade(hidden_give, "step", 1)
    if direct:
        fours = (1, 2, 3)
        token[0] = table_keep
        keep_a, give_a, keep_b, give_b = local(cut_second_kernel, (keep_a, got_a, keep_b, got_b), [out(col_block, ff_block)] * 4)
        got_a, got_b = trade(give_a, "step", 4), trade(give_b, "step", 2)
        own = local(quarter_rows_kernel, (table_keep, other), [out(40, width)] * 4)
        from_xy = [trade(own[b], "step", 2 * b) for b in fours]
        h_own = local(quarter_cols_kernel, (hidden_keep, hidden_other), [out(SEG, ff_block)] * 4)
        h_xy = [trade(h_own[b], "step", 2 * b) for b in fours]
        (ending,) = local(going_kernel, homes[::-1], [out(8 * ROLL + 160, block)], states=states, forces=forces)
        ending = lax.ppermute(ending, both_axes, column_perm)
        (piece,) = local(sum_four_kernel, (own[0], *from_xy), [out(40, width)])
        near = trade(piece, "rows", 1)
        (h_piece,) = local(sum_four_kernel, (h_own[0], *h_xy), [out(SEG, ff_block)])
        h_near = trade(h_piece, "rows", 1)
        (piece,) = local(sum_two_kernel, (piece, near), [out(40, width)])
        far = trade(piece, "rows", 2)
        (h_piece,) = local(sum_two_kernel, (h_piece, h_near), [out(SEG, ff_block)])
        h_far = trade(h_piece, "rows", 2)
        keep, give = local(cut_third_kernel, (keep_a, got_a, keep_b, got_b), [out(col_block, ff_block)] * 2)
        got = trade(give, "rows", 1)
        (rolled,) = local(roll_kernel, (states_home, ending), [out(ROLL, 88, block)])
        gone = lax.all_to_all(rolled, "step", 0, 0, tiled=True)
        (piece,) = local(sum_two_kernel, (piece, far), [out(40, width)])
        from_xy = [trade(piece, "step", 2 * b) for b in fours]
        (share_down,) = local(share_down_kernel, (h_piece, h_far, w_block_hi, w_block_lo), [out(col_block, ff_block)])
        (share_up,) = local(turn_sum_kernel, (keep, got), [out(ff_block, col_block)])
        predicted, grad_forcing, grad_init = local(home_kernel, (gone, ending), home_outs, states=states)
        (mine,) = local(join_rows_kernel, (piece, *from_xy), [out(160, width)])
        other = trade(mine, "step", 1)
    else:
        units = steps // 2
        same_core = [[2 * k + c for k in range(units)] for c in range(2)]
        mine_up = keep_acc + got
        share = lax.psum_scatter(mine_up[:, : hidden // 2], "step", scatter_dimension=1, axis_index_groups=same_core, tiled=True)
        keep, give = pick(share[:col_block], share[col_block : 2 * col_block], side)
        share_up = (keep + trade(give, "rows", 1)).T
        mine_down = hidden_keep + hidden_other
        hidden_share = lax.psum(
            lax.psum_scatter(mine_down[:, : hidden // 2], "step", scatter_dimension=1, axis_index_groups=same_core, tiled=True), "rows"
        )
        nothing = jnp.zeros_like(hidden_share)
        (share_down,) = local(share_down_kernel, (hidden_share, nothing, w_block_hi, w_block_lo), [out(col_block, ff_block)])
        mine, other = pick(*[lax.psum(v, both_axes) for v in pick(table_keep, table_give, core)], core)
        (ending,) = local(going_kernel, homes[::-1], [out(8 * ROLL + 160, block)], states=states, forces=forces)
        ending = lax.ppermute(ending, both_axes, column_perm)
        gone = turn_round(to_later(jnp.concatenate([states_home, ending[: 8 * ROLL].reshape(ROLL, 8, block)], axis=1)))
        predicted, grad_forcing, grad_init = local(home_kernel, (gone, ending), home_outs, states=states)
    g_in, g_dw, g_w_out, lines = local(
        table_kernel, (mine, other),
        [out(2 * states + forces, channels), out(KW, KW, channels), out(states, channels), out(16, width)], states=states, forces=forces,
    )
    g_bias, g_gain, g_b_in = lines[0, :channels], lines[1, :channels], lines[7, :channels]
    g_b_up = lines[8:12].reshape(-1)[:wide].reshape(2, half)[:, : hidden // 2].reshape(2, steps // 2, ff_block).swapaxes(0, 1).reshape(-1)
    g_b_out = lines[12, :states]
    g_b_down = jnp.sum(w_out * g_b_out[:, None], axis=0)
    return (
        predicted[None, :, None],
        grad_init[None, None],
        grad_forcing[None, None, :forces],
        g_in.T,
        g_b_in,
        g_dw.transpose(2, 0, 1),
        g_gain,
        g_bias,
        share_up,
        g_b_up,
        share_down,
        g_b_down,
        g_w_out,
        g_b_out,
    )


def solution(mesh):
    state_spec = P("step", None, None, None, "rows")
    force_spec = P("step", None, None, "rows")
    in_specs = (state_spec, force_spec, P("step", None), P("rows")) + (P(),) * 11 + (state_spec,)
    out_specs = (state_spec, state_spec, force_spec) + (P(),) * 5 + (P("step", "rows"), P(), P("rows", "step"), P(), P(), P())
    return jax.shard_map(per_device, mesh=mesh, in_specs=in_specs, out_specs=out_specs, check_vma=False)
```

```python
import functools

import jax
import jax.numpy as jnp
from jax import lax
from jax.experimental import pallas as pl
from jax.experimental.pallas import tpu as pltpu
from jax.sharding import PartitionSpec as P

F32 = jnp.float32
BF16 = jnp.bfloat16
HIGHEST = lax.Precision.HIGHEST
ROLL = 8
COLS = 32
KW = 7
HALO = 3
EPSILON = 1e-05
LANES = 128
CHUNK = 256
SEG = 80
MIB = 2**20

ERF_P = 0.39
ERF_C = (0.23532534, 0.09138764, 0.64956134, -0.63540268, 0.88666585, -0.22753749)


def round_up(value, multiple):
    return -(-value // multiple) * multiple


def split(values):
    high = values.astype(BF16)
    return high, (values - high.astype(F32)).astype(BF16)


def split_outside(values):
    rounded = lax.reduce_precision(values, 8, 7)
    return rounded.astype(BF16), (values - rounded).astype(BF16)


def dot(left, right):
    return jnp.dot(left, right, preferred_element_type=F32)


def dot_t(left, right):
    return lax.dot_general(left, right, (((1,), (1,)), ((), ())), preferred_element_type=F32)


def gelu_both(v):
    e = jnp.exp(v * v * (-0.5))
    t = 1.0 / (1.0 + (ERF_P * 0.7071067811865476) * jnp.abs(v))
    q = 0.5 * ERF_C[5]
    for coefficient in ERF_C[4::-1]:
        q = q * t + 0.5 * coefficient
    q = (q * t) * e
    phi = jnp.where(v >= 0.0, 1.0 - q, q)
    return v * phi, phi + v * (e * 0.3989422804014327)


def depthwise(ext, shifted, kernel, mixed, lanes, flip, rows):
    rows_in = rows + 2 * HALO
    for q in range(KW):
        for r in range(rows_in):
            shifted[q, r] = ext[r, 5 + q : 5 + q + COLS, lanes]
    for v in range(0, COLS, 8):
        total = [None] * rows
        for q in range(KW):
            taps = [
                kernel[(KW * KW - 1 - (p * KW + q)) if flip else (p * KW + q), :, lanes]
                for p in range(KW)
            ]
            for r in range(rows_in):
                cell = shifted[q, r, v : v + 8, :]
                for p in range(KW):
                    i = r - p
                    if 0 <= i < rows:
                        term = taps[p] * cell
                        total[i] = term if total[i] is None else total[i] + term
        for i in range(rows):
            mixed[i, v : v + 8, lanes] = total[i]


def ocean_count(sent, came):
    last = sent.shape[0] - 1
    return jnp.maximum(sent[last:, :LANES] + came[last:, :LANES], 1.0)


def group_lanes(group):
    return pl.ds(pl.multiple_of(group * LANES, LANES), LANES)


def mix_kernel(
    at, cur, cur_edge, prev, prev_edge, force, force_edge, w_in_hi, w_in_lo, b_in, w_oi_hi, w_oi_lo, b_new, taps, ocean,
    mixed_out, stats_out, base_out, window_out, x_all, lifted_all,
    ext, shifted, mixed, x_part, sems, *, turn, cur_lanes, prev_lanes,
):
    core, part = at[0], at[1]
    px = cur.shape[0]
    edge_px = x_part.shape[0]
    rows = px // COLS
    width = mixed_out.shape[1]
    prev_now, prev_edge_now = prev[...], prev_edge[:edge_px, prev_lanes : prev_lanes + LANES]
    if turn:
        prev_now, prev_edge_now = prev_now + force[turn], prev_edge_now + force_edge[turn]
    own = jnp.concatenate([prev_now, cur[...]], axis=1)
    edge = jnp.concatenate([prev_edge_now, cur_edge[:edge_px, cur_lanes : cur_lanes + LANES]], axis=1)
    own_hi, own_lo = split(own)
    edge_hi, edge_lo = split(edge)
    both = dot(jnp.concatenate([own_hi, edge_hi, own_lo, edge_lo], axis=0), w_in_hi[...])
    high = dot(jnp.concatenate([own_hi, edge_hi], axis=0), w_in_lo[...])
    lifted = (both[: px + edge_px] + both[px + edge_px :]) + (high + b_in[...])
    base_out[...] = dot(own_hi, w_oi_hi[...]) + dot(own_lo, w_oi_hi[...]) + dot(own_hi, w_oi_lo[...]) + b_new[...]
    zeros = jnp.zeros((rows + 2 * HALO, 8, width), F32)
    ext[:, :8, :] = zeros
    ext[:, 8 + COLS :, :] = zeros
    ext[HALO : HALO + rows, 8 : 8 + COLS, :] = lifted[:px].reshape(rows, COLS, width)
    ext[pl.ds((rows + HALO) * (1 - core), HALO), 8 : 8 + COLS, :] = lifted[px:].reshape(HALO, COLS, width)
    ext[pl.ds((rows + HALO) * core, HALO), 8 : 8 + COLS, :] = jnp.zeros((HALO, COLS, width), F32)
    part_rows = window_out.shape[0] - 2 * HALO
    part_px = x_part.shape[0]
    x_part[...] = jnp.where(part == 0, own[:part_px], own[part_px:])
    here = pl.ds(turn * part_rows, part_rows)
    keeps = [
        pltpu.make_async_copy(ext.at[pl.ds(part * part_rows, window_out.shape[0]), 8 : 8 + COLS, :], window_out, sems.at[0]),
        pltpu.make_async_copy(ext.at[pl.ds(part * part_rows + HALO, part_rows), 8 : 8 + COLS, :], lifted_all.at[here], sems.at[1]),
        pltpu.make_async_copy(x_part, x_all.at[pl.ds(turn * part_px, part_px)], sems.at[2]),
    ]
    for keep in keeps:
        keep.start()
    mask = ocean[...]

    def group(g, _):
        lanes = group_lanes(g)
        depthwise(ext, shifted, taps, mixed, lanes, False, rows)
        cells = mixed[:, :, lanes].reshape(px, LANES)
        mixed_out[:, lanes] = cells
        masked = cells * mask
        stats_out[0:1, lanes] = jnp.sum(masked, axis=0, keepdims=True)
        stats_out[1:2, lanes] = jnp.sum(masked * cells, axis=0, keepdims=True)
        return 0

    lax.fori_loop(0, width // LANES, group, 0)
    for keep in keeps:
        keep.wait()


def feed_kernel(
    at, mixed, stats, stats_other, sent, came, gain, bias, ocean, base, w_up, b_up, w_od,
    new_out, new_edge_out, norm_edge_out, inv_out, norm_out, slope_out, act_all, state_all,
    stack, rem, acc, acc_lo, hold_a, hold_b, hold_act, norm, slope, act_part, state, sems, *, turn, width, k_main, k_rem,
):
    core, part = at[0], at[1]
    px = mixed.shape[0]
    chunks = w_up.shape[1] // CHUNK
    part_px = act_part.shape[1]
    total = ocean_count(sent, came)
    keep_norm = pltpu.make_async_copy(norm, norm_out, sems.at[2 * chunks])

    for g in range(width // LANES):
        lanes = slice(g * LANES, (g + 1) * LANES)
        cells = mixed[:, lanes]
        average = (stats[0:1, lanes] + stats_other[0:1, lanes]) / total
        variance = (stats[1:2, lanes] + stats_other[1:2, lanes]) / total - average * average
        inverse = lax.rsqrt(variance + EPSILON)
        inv_out[:, lanes] = jnp.broadcast_to(inverse, (8, LANES))
        normalized = (cells - average) * inverse
        norm[:, lanes] = normalized
        normed = normalized * gain[:, lanes] + bias[:, lanes]
        high = normed.astype(BF16)
        high_f = high.astype(F32)
        low_f = normed - high_f
        if (g + 1) * LANES <= k_main:
            stack[:px, lanes] = high
            stack[px:, lanes] = low_f.astype(BF16)
        else:
            rem[...] = (high_f + pltpu.roll(low_f, k_rem, 1) + pltpu.roll(high_f, 2 * k_rem, 1)).astype(BF16)
    keep_norm.start()
    edge_px = norm_edge_out.shape[0]
    norm_edge_out[...] = norm[pl.ds(pl.multiple_of((1 - core) * (px - edge_px), 8), edge_px), :]

    def up(t, hold):
        cols = pl.ds(pl.multiple_of(t * CHUNK, CHUNK), CHUNK)
        both = dot(stack[...], w_up[:k_main, cols])
        high = dot(stack[:px], w_up[k_main : 2 * k_main, cols])
        rest = dot(rem[...], w_up[2 * k_main :, cols])
        hold[...] = (both[:px] + both[px:]) + (high + rest)

    def keep_slope(t):
        return pltpu.make_async_copy(slope.at[t], slope_out.at[t], sems.at[t])

    def keep_act(t):
        return pltpu.make_async_copy(act_part.at[t], act_all.at[t, pl.ds(turn * part_px, part_px)], sems.at[chunks + t])

    def act(t, hold):
        cols = pl.ds(pl.multiple_of(t * CHUNK, CHUNK), CHUNK)
        activated, slope[t] = gelu_both(hold[...] + b_up[:, cols])
        hold_act[...] = activated
        high, low = split(activated)
        acc[...] += dot(high, w_od[cols, :])
        acc_lo[...] += dot(low, w_od[cols, :LANES])
        act_part[t] = hold_act[pl.ds(pl.multiple_of(part * part_px, 8), part_px), :]
        keep_slope(t).start()
        keep_act(t).start()

    acc[...] = jnp.zeros_like(acc)
    acc_lo[...] = base[...]
    up(0, hold_a)

    def pair(i, _):
        up(2 * i + 1, hold_b)
        act(2 * i, hold_a)
        up(2 * i + 2, hold_a)
        act(2 * i + 1, hold_b)
        return 0

    lax.fori_loop(0, chunks // 2, pair, 0)
    act(chunks - 1, hold_a)
    new = (acc[:, :LANES] + acc[:, LANES:] + acc_lo[...]) * ocean[...]
    new_out[...] = new
    new_edge_out[...] = new_out[pl.ds(pl.multiple_of((1 - core) * (px - edge_px), 8), edge_px), :]
    mine = jnp.where(part == 0, new[:part_px], new[part_px:])
    state[...] = mine.T[: state.shape[0]]
    keep_state = pltpu.make_async_copy(state, state_all.at[turn], sems.at[2 * chunks + 1])
    keep_state.start()
    keep_norm.wait()
    keep_state.wait()
    for t in range(chunks):
        keep_slope(t).wait()
        keep_act(t).wait()


def back_kernel(*refs, finish, begin, turn, width, k_main, k_rem, states):
    refs = list(refs)

    def take(count):
        out = refs[:count]
        del refs[:count]
        return out

    (at, ocean, pending_in) = take(3)
    if finish:
        (grad_n, sent, came, norm, norm_edge, inv, gain, first_sent, first_came, grad_branch, window, taps, w_in_hi, w_in_lo) = take(14)
    if begin:
        (cots, slope_hbm, norm_now, w_out, w_od, w_up) = take(6)
    if finish:
        (carry_out, pending_out, taps_out, home_out, lift_all) = take(5)
    if begin:
        (branch_out, hidden_out, grad_n_out, send_out, masked_all) = take(5)
    if finish:
        (ext, shifted, mixed, grad_lift, lift_sem) = take(5)
    if begin:
        (cot, slope, masked_part, pulled, begin_sems) = take(5)
    core, part = at[0], at[1]
    px = ocean.shape[0]
    rows = px // COLS
    part_px = px // 2
    if begin:
        get_cot = pltpu.make_async_copy(cots.at[turn], cot, begin_sems.at[0])
        get_slope = pltpu.make_async_copy(slope_hbm, slope, begin_sems.at[1])
        get_cot.start()
        get_slope.start()
    if finish:
        edge_px = norm_edge.shape[0]
        total = ocean_count(first_sent, first_came)
        ocean_edge = first_came[:edge_px, 2 * LANES :]
        zeros = jnp.zeros((rows + 2 * HALO, 8, width), F32)
        ext[:, :8, :] = zeros
        ext[:, 8 + COLS :, :] = zeros
        ext[pl.ds((rows + HALO) * core, HALO), 8 : 8 + COLS, :] = jnp.zeros((HALO, COLS, width), F32)
        part_rows = window.shape[0] - 2 * HALO
        for g in range(width // LANES):
            lanes = slice(g * LANES, (g + 1) * LANES)
            bias_sum = (sent[edge_px : edge_px + 1, lanes] + came[edge_px : edge_px + 1, lanes]) / total
            gain_sum = (sent[edge_px + 1 : edge_px + 2, lanes] + came[edge_px + 1 : edge_px + 2, lanes]) / total
            scale = inv[0:1, lanes] * gain[:, lanes]
            mix = scale * (grad_n[:, lanes] - ocean[...] * (bias_sum + norm[:, lanes] * gain_sum))
            mix_edge = scale * (came[:edge_px, lanes] - ocean_edge * (bias_sum + norm_edge[:, lanes] * gain_sum))
            ext[HALO : HALO + rows, 8 : 8 + COLS, lanes] = mix.reshape(rows, COLS, LANES)
            ext[pl.ds((rows + HALO) * (1 - core), HALO), 8 : 8 + COLS, lanes] = mix_edge.reshape(HALO, COLS, LANES)

        def group(g, _):
            lanes = group_lanes(g)
            depthwise(ext, shifted, taps, mixed, lanes, True, rows)
            grad_lift[:, lanes] = mixed[:, :, lanes].reshape(px, LANES) + grad_branch[:, lanes]
            for q in range(KW):
                sums = [None] * KW
                for i in range(part_rows):
                    for v in range(0, COLS, 8):
                        grad = shifted[KW - 1 - q, HALO + part * part_rows + i, v : v + 8, :]
                        for p in range(KW):
                            term = grad * window[i + p, v : v + 8, lanes]
                            sums[p] = term if sums[p] is None else sums[p] + term
                for p in range(KW):
                    taps_out[p * KW + q : p * KW + q + 1, lanes] = jnp.sum(sums[p], axis=0, keepdims=True)
            return 0

        lax.fori_loop(0, width // LANES, group, 0)
        keep_lift = pltpu.make_async_copy(
            grad_lift.at[pl.ds(pl.multiple_of(part * part_px, 8), part_px)], lift_all.at[pl.ds((turn + 1) * part_px, part_px)], lift_sem
        )
        keep_lift.start()
        high, low = split(grad_lift[...])
        both = dot_t(jnp.concatenate([high, low], axis=0), w_in_hi[...])
        grad_x = (both[:px] + both[px:]) + dot_t(high, w_in_lo[...])
        carry = grad_x[:, LANES:] + pending_in[...]
        carry_out[...] = carry
        pending_out[...] = grad_x[:, :LANES]
        part_x = jnp.where(part == 0, grad_x[:part_px, :LANES], grad_x[part_px:, :LANES])
        part_c = jnp.where(part == 0, carry[:part_px], carry[part_px:])
        home_out[:LANES] = part_x.T
        home_out[LANES:] = part_c.T
    if begin:
        get_cot.wait()
        grad_new = cot[...] + carry if finish else cot[...]
        lane = lax.broadcasted_iota(jnp.int32, (px, LANES), 1)
        masked = jnp.where(lane < states, grad_new * ocean[...], 0.0)
        masked_part[...] = jnp.where(part == 0, masked[:part_px], masked[part_px:])
        keep_masked = pltpu.make_async_copy(masked_part, masked_all.at[pl.ds(turn * part_px, part_px)], begin_sems.at[2])
        keep_masked.start()
        high_f = masked.astype(BF16).astype(F32)
        nothing = jnp.zeros((px, LANES), F32)
        high_w = jnp.concatenate([high_f, nothing], axis=1)
        low_w = jnp.concatenate([masked - high_f, nothing], axis=1)
        left = (high_w + pltpu.roll(low_w, SEG, 1) + pltpu.roll(high_w, 2 * SEG, 1)).astype(BF16)
        branch_out[...] = dot(left, w_out[...])
        chunks = w_od.shape[1] // CHUNK
        get_slope.wait()

        half = w_od.shape[1] // 2

        def pull(t, _):
            cols = pl.ds(pl.multiple_of(t * half, half), half)
            pulled[:, cols] = dot(left, w_od[:, cols])
            return 0

        lax.fori_loop(0, 2, pull, 0)

        def chunk(t, _):
            cols = pl.ds(pl.multiple_of(t * CHUNK, CHUNK), CHUNK)
            high, low = split(pulled[:, cols] * slope[t])
            hidden_out[:px, cols] = high
            hidden_out[px:, cols] = low
            return 0

        lax.fori_loop(0, chunks, chunk, 0)
        both = dot_t(hidden_out[...], w_up[:k_main])
        grad_n_out[:, :k_main] = (both[:px] + both[px:]) + dot_t(hidden_out[:px], w_up[k_main : 2 * k_main])
        rest = dot_t(hidden_out[...], w_up[2 * k_main :])
        tail = rest[:px] + rest[px:] + pltpu.roll(rest[:px], LANES - 2 * k_rem, 1)
        grad_n_out[:, k_main:] = jnp.where(lane < k_rem, tail, 0.0)
        edge_px = send_out.shape[0] - 8
        for g in range(width // LANES):
            lanes = slice(g * LANES, (g + 1) * LANES)
            cells = grad_n_out[:, lanes]
            send_out[edge_px : edge_px + 1, lanes] = jnp.sum(cells, axis=0, keepdims=True)
            send_out[edge_px + 1 : edge_px + 2, lanes] = jnp.sum(cells * norm_now[:, lanes], axis=0, keepdims=True)
        send_out[edge_px + 2 :, :] = jnp.zeros((6, width), F32)
        send_out[:edge_px, :] = grad_n_out[pl.ds(pl.multiple_of((1 - core) * (px - edge_px), 8), edge_px), :]
        keep_masked.wait()
    if finish:
        keep_lift.wait()


def weight_kernel(at, norm, gain, bias, hidden, send, *rest, quarter, finish):
    if finish:
        taps, keep_in, give_in, sums_in, keep_out, give_out, sums_out, *up_row = rest
    else:
        keep_out, give_out, sums_out, *up_row = rest
    core = at[0]
    part = at[1]
    px = norm.shape[0]
    tap_rows = sums_out.shape[0] - 8
    if finish:
        sums_out[:tap_rows] = sums_in[:tap_rows] + taps[...]
        sums_out[tap_rows:] = sums_in[tap_rows:] + send[send.shape[0] - 8 :]
    else:
        sums_out[:tap_rows] = jnp.zeros((tap_rows, sums_out.shape[1]), F32)
        sums_out[tap_rows:] = send[send.shape[0] - 8 :]
    window = round_up(quarter, LANES)
    base = (quarter // LANES) * LANES
    normed = norm[...] * gain[...] + bias[...]
    second = pltpu.roll(normed[:, base : base + window], window - (quarter - base), 1)
    mine = jnp.where(part == 0, normed[:, :window], second)
    lane = lax.broadcasted_iota(jnp.int32, (px, window), 1)
    mine = jnp.where(lane < quarter, mine, jnp.where(lane == quarter, 1.0, 0.0))
    high, low = split(mine.T[: keep_out.shape[0]])
    half = keep_out.shape[1]

    for side, acc_out in enumerate((keep_out, give_out)):
        actual = core if side == 0 else 1 - core
        cols = pl.ds(pl.multiple_of(actual * half, LANES), half)
        new = dot(high, hidden[:px, cols]) + dot(high, hidden[px:, cols]) + dot(low, hidden[:px, cols])
        acc_out[...] = (keep_in, give_in)[side][...] + new if finish else new
    if up_row:
        line = quarter // 8 * 8
        for side, acc_out in ((core, keep_out), (1 - core, give_out)):
            up_row[0][:, pl.ds(pl.multiple_of(side * half, LANES), half)] = acc_out[line : line + 8, :]


VMEM_SPEC = pl.BlockSpec(memory_space=pltpu.VMEM)
SMEM_SPEC = pl.BlockSpec(memory_space=pltpu.SMEM)
HBM_SPEC = pl.BlockSpec(memory_space=pltpu.HBM)


def out(*shape, dtype=F32):
    return jax.ShapeDtypeStruct(shape, dtype)


def in_hbm(values):
    return pltpu.with_memory_space_constraint(values, pltpu.HBM)


def call(kernel, name, args, outs, scratch, limit, *, micros, smem=0, hbm=(), hbm_outs=(), vmem_outs=(), aliases=None, stacked=()):
    args = [in_hbm(a) if i in hbm else a for i, a in enumerate(args)]
    specs = [SMEM_SPEC if i < smem else HBM_SPEC if i in hbm else VMEM_SPEC for i in range(len(args))]
    hbm_outs = tuple(hbm_outs) + tuple(i for i, _ in stacked)
    aliases = dict(aliases or {})
    used = len(args)
    for i, buffer in stacked:
        if buffer is not None:
            aliases[len(args)] = i
            args.append(in_hbm(buffer))
            specs.append(HBM_SPEC)
    extra = len(args) - used

    def body(*refs):
        kernel(*refs[:used], *refs[used + extra :])

    return pl.pallas_call(
        body,
        in_specs=specs,
        out_specs=[HBM_SPEC if i in hbm_outs else VMEM_SPEC for i in range(len(outs))],
        out_shape=[
            pltpu.HBM(o.shape, o.dtype) if i in hbm_outs else pltpu.VMEM(o.shape, o.dtype) if i in vmem_outs else o
            for i, o in enumerate(outs)
        ],
        scratch_shapes=scratch,
        input_output_aliases=aliases,
        compiler_params=pltpu.CompilerParams(vmem_limit_bytes=limit * MIB),
        cost_estimate=pl.CostEstimate(flops=int(micros * 1.1e9), bytes_accessed=1024, transcendentals=0),
        name=name,
    )(*args)


def start_kernel(at, first, second, prev_out, cur_out, ocean_out, send_out, *, states, forces):
    core, part = at[0], at[1]
    block = first.shape[1]
    rows = first.shape[0]
    mask_row = 2 * states + forces

    def turn(values):
        prev = jnp.concatenate([values[: states + forces], jnp.zeros((LANES - states - forces, block), F32)], axis=0).T
        cur = jnp.concatenate([values[states + forces : mask_row], jnp.zeros((LANES - states, block), F32)], axis=0).T
        mask = jnp.broadcast_to(values[mask_row : mask_row + 1], (LANES, block)).T
        return prev, cur, mask

    zero, one = first[...], second[...]
    swap = part == 1
    top, low = jnp.where(swap, one, zero), jnp.where(swap, zero, one)
    count = jnp.sum(top[mask_row : mask_row + 1]) + jnp.sum(low[mask_row : mask_row + 1])
    for i, values in enumerate((top, low)):
        prev, cur, mask = turn(values)
        here = slice(i * block, (i + 1) * block)
        prev_out[here] = prev
        cur_out[here] = cur
        ocean_out[here] = mask
    at_edge = pl.ds(pl.multiple_of((1 - core) * block, 8), block)
    send_out[:block, :LANES] = prev_out[at_edge, :]
    send_out[:block, LANES : 2 * LANES] = cur_out[at_edge, :]
    send_out[:block, 2 * LANES :] = ocean_out[at_edge, :]
    send_out[block:] = jnp.full((8, 3 * LANES), count)


def pack_kernel(at, first, second, force_out, force_send, cot_out, *, states, forces):
    core, part = at[0], at[1]
    steps, rows, block = first.shape
    lane = lax.broadcasted_iota(jnp.int32, (block, LANES), 1)
    for j in range(steps):
        turned = [
            jnp.concatenate([values[j], jnp.zeros((LANES - rows, block), F32)], axis=0).T for values in (first, second)
        ]
        top, low = jnp.where(part == 1, turned[1], turned[0]), jnp.where(part == 1, turned[0], turned[1])
        for i, values in enumerate((top, low)):
            cot_out[j, i * block : (i + 1) * block] = jnp.where(lane < states, values, 0.0)
            force_out[j, i * block : (i + 1) * block] = jnp.where(lane < states, 0.0, values)
        force_send[j] = force_out[j, pl.ds(pl.multiple_of((1 - core) * block, 8), block), :]


def reorder(source, target, spans):
    for start, size, place in spans:
        target[:, place : place + size] = source[:, start : start + size]


def up_kernel(w_up_t, up_all, raw, turned, sems, *, k_main, k_rem, spans):
    slots, block = raw.shape[0], raw.shape[1]
    blocks = k_main // block

    def get(t, size):
        slot = lax.rem(t, slots)
        return pltpu.make_async_copy(
            w_up_t.at[pl.ds(pl.multiple_of(t * block, 8), size)], raw.at[slot, pl.ds(0, size)], sems.at[slot]
        )

    for t in range(slots):
        get(t, block).start()
    turned[...] = jnp.zeros_like(turned)

    def main(t, _):
        get(t, block).wait()
        reorder(raw.at[lax.rem(t, slots)], turned, spans)

        @pl.when(t + slots < blocks)
        def _():
            get(t + slots, block).start()

        @pl.when(t + slots == blocks)
        def _():
            get(t + slots, k_rem).start()

        high, low = split(turned[...])
        up_all[pl.ds(pl.multiple_of(t * block, block), block), :] = high
        up_all[pl.ds(pl.multiple_of(k_main + t * block, block), block), :] = low
        return 0

    lax.fori_loop(0, blocks, main, 0)
    get(blocks, k_rem).wait()
    reorder(raw.at[blocks % slots, pl.ds(0, k_rem)], turned.at[pl.ds(0, k_rem)], spans)
    high, low = split(turned[:k_rem])
    base = 2 * k_main
    up_all[base : base + k_rem] = high
    up_all[base + k_rem : base + 2 * k_rem] = high
    up_all[base + 2 * k_rem : base + 3 * k_rem] = low
    up_all[base + 3 * k_rem :] = jnp.zeros((LANES - 3 * k_rem, up_all.shape[1]), BF16)


def down_kernel(w_down, out_parts, od_fwd, od_bwd, down, product, ordered, sems, *, spans):
    pieces = sems.shape[0]
    piece = down.shape[1] // pieces

    def get(t):
        cols = pl.ds(pl.multiple_of(t * piece, LANES), piece)
        return pltpu.make_async_copy(w_down.at[:, cols], down.at[:, cols], sems.at[t])

    for t in range(pieces):
        get(t).start()
    ordered[...] = jnp.zeros_like(ordered)

    def multiply(t, _):
        cols = pl.ds(pl.multiple_of(t * piece, LANES), piece)
        get(t).wait()
        high, low = split(down[:, cols])
        both = dot(out_parts[...], high)
        product[:, cols] = (both[:SEG] + both[SEG:]) + dot(out_parts[:SEG], low)
        return 0

    lax.fori_loop(0, pieces, multiply, 0)
    reorder(product, ordered.at[pl.ds(0, SEG)], spans)

    def spread(t, _):
        cols = pl.ds(pl.multiple_of(t * CHUNK, CHUNK), CHUNK)
        values = ordered[:, cols]
        high, low = split(values)
        od_bwd[:SEG, cols] = high[:SEG]
        od_bwd[SEG : 2 * SEG, cols] = high[:SEG]
        od_bwd[2 * SEG : 3 * SEG, cols] = low[:SEG]
        od_bwd[3 * SEG :, cols] = jnp.zeros((od_bwd.shape[0] - 3 * SEG, CHUNK), BF16)
        high, low = split(values.T)
        od_fwd[cols, :LANES] = high
        od_fwd[cols, LANES:] = low
        return 0

    lax.fori_loop(0, ordered.shape[1] // CHUNK, spread, 0)


def last_kernel(
    at, masked_hbm, x_hbm, lifts_hbm, lifted_hbm, act_hbm, down_hbm, b_down, sums, taps, up_row, token, table_keep, table_give, hidden_keep, hidden_give,
    table,    masked, x_parts, lifts, lifted, act, down, masked_t, x_t, g_hidden, natural, g_parts, sems, *, spans, blocks,
):
    chunks = act.shape[0]
    half = hidden_keep.shape[1]
    width = table.shape[1]
    scale = (at[1] == 0).astype(F32)
    tap_rows = taps.shape[0]
    pairs = [(masked_hbm, masked), (x_hbm, x_parts), (lifts_hbm, lifts), (lifted_hbm, lifted)]
    firsts = [pltpu.make_async_copy(pair[0], pair[1], sems.at[i]) for i, pair in enumerate(pairs)]
    downs = [
        pltpu.make_async_copy(down_hbm.at[pl.ds(start, size)], down.at[pl.ds(start, size)], sems.at[4 + i])
        for i, (start, size) in enumerate(blocks)
    ]

    def get(t):
        return pltpu.make_async_copy(act_hbm.at[t], act.at[t], sems.at[4 + len(blocks) + t])

    firsts[0].start()
    for t in range(chunks):
        get(t).start()
    for copy in firsts[1:] + downs:
        copy.start()
    firsts[0].wait()
    turned = masked[...].T[:SEG]
    high = turned.astype(BF16)
    masked_t[:SEG] = high
    masked_t[SEG:] = (turned - high.astype(F32)).astype(BF16)
    total = jnp.sum(turned, axis=1, keepdims=True)

    def chunk(t, _):
        get(t).wait()
        high, low = split(act[t])
        both = dot(masked_t[...], high)
        sums_now = (both[:SEG] + both[SEG:]) + dot(masked_t[:SEG], low)
        g_hidden[:, pl.ds(pl.multiple_of(t * CHUNK, CHUNK), CHUNK)] = sums_now
        return 0

    lax.fori_loop(0, chunks, chunk, 0)
    hidden_keep[...] = g_hidden[:, pl.ds(pl.multiple_of(at[0] * half, LANES), half)]
    hidden_give[...] = g_hidden[:, pl.ds(pl.multiple_of((1 - at[0]) * half, LANES), half)]
    for start, size, place in spans:
        natural[:, start : start + size] = g_hidden[:, place : place + size]
    high, low = split(natural[...])
    g_parts[:SEG] = high
    g_parts[SEG:] = low
    for copy in firsts[1:]:
        copy.wait()
    high, low = split(x_parts[...].T)
    x_t[0] = high
    x_t[1] = low
    for start in range(0, width, CHUNK):
        size = min(CHUNK, width - start)
        lanes = slice(start, start + size)
        high, low = split(lifted[:, :, lanes].reshape(lifts.shape[0], size))
        both = dot(masked_t[...], high)
        lifted_sum = (both[:SEG] + both[SEG:]) + dot(masked_t[:SEG], low)
        grads = lifts[:, lanes]
        high, low = split(grads)
        g_in = dot(x_t[0], high) + dot(x_t[1], high) + dot(x_t[0], low)
        table[:88, lanes] = g_in[:88]
        table[88:168, lanes] = g_in[LANES : LANES + 80]
        table[168:224, lanes] = sums[:tap_rows, lanes] + taps[:, lanes]
        table[224:304, lanes] = lifted_sum + total * b_down[:, lanes]
        table[304:311, lanes] = sums[tap_rows : tap_rows + 7, lanes] * scale
        table[311:312, lanes] = jnp.sum(grads, axis=0, keepdims=True)
    for (start, size), copy in zip(blocks, downs):
        copy.wait()
        high, low = split(down[start : start + size])
        both = dot_t(g_parts[...], high)
        g_out = (both[:SEG] + both[SEG:]) + dot_t(g_parts[:SEG], low)
        table[224:304, start : start + size] += g_out
    table[312:] = jnp.zeros((table.shape[0] - 312, width), F32)
    for i, start in enumerate(range(0, up_row.shape[1], width)):
        size = min(width, up_row.shape[1] - start)
        table[312 + i : 313 + i, :size] = up_row[:1, start : start + size] * scale
    table[316:317, :LANES] = jnp.sum(masked[...], axis=0, keepdims=True)
    rows = table_keep.shape[0]
    table_keep[...] = table[pl.ds(pl.multiple_of(at[0] * rows, 8), rows), :]
    table_give[...] = table[pl.ds(pl.multiple_of((1 - at[0]) * rows, 8), rows), :]


def flags(at):
    return at[3], at[4], at[5], at[2]


def cut_first_kernel(at, keep, got, keep_a, give_a, keep_b, give_b, *, rows, cols):
    x, y, _, _ = flags(at)

    def part(row, k):
        here = (slice(row * rows, (row + 1) * rows), slice(k * cols, (k + 1) * cols))
        return keep[here] + got[here]

    for i, (even, odd) in enumerate(((0, 1), (2, 3))):
        one, two = part(0, even), part(0, odd)
        keep_a[i] = jnp.where(x == 0, one, two)
        give_a[i] = jnp.where(x == 0, two, one)
    for i, (low, top) in enumerate(((0, 2), (1, 3))):
        one, two = part(1, low), part(1, top)
        keep_b[i] = jnp.where(y == 0, one, two)
        give_b[i] = jnp.where(y == 0, two, one)


def cut_second_kernel(at, keep_a, got_a, keep_b, got_b, keep_a_out, give_a_out, keep_b_out, give_b_out):
    x, y, _, _ = flags(at)
    for bit, keep, got, keep_out, give_out in (
        (y, keep_a, got_a, keep_a_out, give_a_out),
        (x, keep_b, got_b, keep_b_out, give_b_out),
    ):
        keep_out[...] = keep[bit] + got[bit]
        give_out[...] = keep[1 - bit] + got[1 - bit]


def cut_third_kernel(at, keep_a, got_a, keep_b, got_b, keep_out, give_out):
    _, _, _, side = flags(at)
    one, two = keep_a[...] + got_a[...], keep_b[...] + got_b[...]
    keep_out[...] = jnp.where(side == 0, one, two)
    give_out[...] = jnp.where(side == 0, two, one)


def turn_sum_kernel(at, keep, got, out_ref):
    out_ref[...] = (keep[...] + got[...]).T


def quarter_rows_kernel(at, keep, got, *outs):
    rows = outs[0].shape[0]
    pair = at[5]
    for b, out_ref in enumerate(outs):
        place = pl.multiple_of((pair ^ b) * rows, 8)
        out_ref[...] = keep[pl.ds(place, rows), :] + got[pl.ds(place, rows), :]


def quarter_cols_kernel(at, keep, got, *outs):
    cols = outs[0].shape[1]
    pair = at[5]
    parts = [keep[:, k * cols : (k + 1) * cols] + got[:, k * cols : (k + 1) * cols] for k in range(4)]
    for b, out_ref in enumerate(outs):
        k = pair ^ b
        low = jnp.where(k == 0, parts[0], parts[1])
        top = jnp.where(k == 2, parts[2], parts[3])
        out_ref[...] = jnp.where(k < 2, low, top)


def sum_two_kernel(at, a, b, out_ref):
    out_ref[...] = a[...] + b[...]


def sum_four_kernel(at, a, b, c, d, out_ref):
    out_ref[...] = (a[...] + b[...]) + (c[...] + d[...])


def join_rows_kernel(at, a, b, c, d, out_ref):
    rows = a.shape[0]
    for flip, ref in enumerate((a, b, c, d)):
        out_ref[pl.ds(pl.multiple_of((at[5] ^ flip) * rows, 8), rows), :] = ref[...]


def share_down_kernel(at, a, b, w_hi, w_lo, out_ref):
    high, low = split(a[...] + b[...])
    out_ref[...] = dot(w_hi[...], high) + dot(w_hi[...], low) + dot(w_lo[...], high)


def table_kernel(at, mine, other, g_in, g_dw, g_out, rows_out, *, states, forces):
    core = at[0]
    half = mine.shape[0]
    channels = g_in.shape[1]

    def get(start, size):
        pieces = []
        for base in (0, half):
            low, top = max(start, base), min(start + size, base + half)
            if low < top:
                here = slice(low - base, top - base)
                pieces.append(jnp.where(core == (base > 0), mine[here, :channels], other[here, :channels]))
        return pieces[0] if len(pieces) == 1 else jnp.concatenate(pieces, axis=0)

    g_in[:states] = get(0, 88)[:states]
    g_in[states : 2 * states] = get(88, 80)[:states]
    g_in[2 * states :] = get(0, 88)[states : states + forces]
    taps = get(168, 56)
    for p in range(KW):
        g_dw[p] = taps[p * KW : (p + 1) * KW]
    g_out[...] = get(224, 80)[:states]
    for i, start in enumerate((304, 312)):
        piece = jnp.where(core == (start >= half), mine[start % half : start % half + 8], other[start % half : start % half + 8])
        rows_out[8 * i : 8 * i + 8] = piece


def going_kernel(at, *refs, states, forces):
    homes, out_ref = refs[:-1], refs[-1]
    steps = len(homes)
    block = out_ref.shape[1]
    for j in range(steps):
        out_ref[8 * j : 8 * j + 8] = jnp.concatenate([homes[j][states : states + forces], jnp.zeros((8 - forces, block), F32)], axis=0)
    out_ref[8 * steps : 8 * steps + 80] = homes[0][:80]
    out_ref[8 * steps + 80 :] = homes[0][LANES : LANES + 80]


def roll_kernel(at, states, forces, out_ref):
    steps = out_ref.shape[0]
    high = states.shape[1]
    for i in range(steps):
        here = lax.rem(i - at[6] + steps, steps)
        out_ref[i, :high] = states[here]
        out_ref[i, high:] = forces[pl.ds(pl.multiple_of(here * 8, 8), 8), :]


def home_kernel(at, gone, ending, predicted, grad_forcing, grad_init, *, states):
    steps = gone.shape[0]
    total = gone[0, SEG:]
    for i in range(steps):
        predicted[i] = gone[lax.rem(at[6] - i + steps, steps), :states]
        if i:
            total = total + gone[i, SEG:]
    grad_forcing[...] = total
    base = 8 * steps
    prev, cur = ending[base : base + SEG][:states], ending[base + SEG : base + 2 * SEG][:states]
    single = at[7] == 1
    grad_init[0] = jnp.where(single, 0.0, prev)
    grad_init[1] = jnp.where(single, cur + prev, cur)


def pad_to(values, shape):
    return jnp.pad(values, [(0, size - have) for size, have in zip(shape, values.shape)])


def per_device(
    init_states, forcing, history, land_mask, w_in, b_in, w_dw, bn_gain, bn_bias, w_up, b_up, w_down, b_down, w_out, b_out, cotangent
):
    steps = lax.axis_size("step")
    devices_z = lax.axis_size("rows")
    step = lax.axis_index("step")
    depth = lax.axis_index("rows")
    core, pair = step % 2, step // 2
    side, part = depth % 2, depth // 2
    both_axes = ("step", "rows")
    block = land_mask.shape[0]
    px = 2 * block
    rows = px // COLS
    states = w_out.shape[0]
    forces = forcing.shape[2]
    channels = w_up.shape[1]
    hidden = w_up.shape[0]
    width = round_up(channels, LANES)
    ff_block = hidden // steps
    half = round_up(hidden // 2, LANES)
    wide = 2 * half
    spans = [(s * ff_block, ff_block, (s % 2) * half + (s // 2) * ff_block) for s in range(steps)]
    k_main = channels // CHUNK * CHUNK
    k_rem = channels - k_main
    col_block = channels // devices_z

    def place(s, z):
        return s * devices_z + z

    cells = [(k, c, h, q) for k in range(steps // 2) for c in range(2) for h in range(2) for q in range(2)]
    fetch_perms = [
        [(place(2 * k + q, 2 * c + (b ^ h)), place(2 * k + c, 2 * h + q)) for k, c, h, q in cells] for b in range(2)
    ]

    column_perm = [(place(2 * k + c, 2 * h + q), place(2 * k + q, 2 * c + h)) for k, c, h, q in cells]
    siblings = [(s, s ^ 1) for s in range(steps)]

    def to_sibling(values):
        return lax.ppermute(values, "step", siblings)

    def shift_back(values, j):
        return values if j == 0 else lax.ppermute(values, "step", [((s + j) % steps, s) for s in range(steps)])

    def fetch_own(values):
        got = [lax.ppermute(values, both_axes, perm) for perm in fetch_perms]
        return got

    def turn_round(values):
        n = values.shape[0]
        doubled = jnp.flip(jnp.concatenate([values, values]), axis=0)
        return lax.dynamic_slice_in_dim(doubled, n - 1 - step % n, n, axis=0)

    def rotate(values, by):
        return lax.dynamic_slice_in_dim(jnp.concatenate([values, values]), by, steps, axis=0)

    def from_later(values):
        if steps == ROLL:
            return rotate(lax.all_to_all(turn_round(values), "step", 0, 0, tiled=True), step)
        return jnp.stack([shift_back(values[j], j) for j in range(ROLL)])

    def to_later(values):
        if steps == ROLL:
            return turn_round(lax.all_to_all(rotate(values, (steps - step) % steps), "step", 0, 0, tiled=True))
        return jnp.stack([lax.ppermute(values[j], "step", [(s, (s + j) % steps) for s in range(steps)]) for j in range(ROLL)])

    at = jnp.stack([core, part, side, pair % 2, (pair // 2) % 2, pair, step % ROLL, history[0, 0]]).astype(jnp.int32)
    mask_row = land_mask.astype(F32)[None]
    current = init_states[0, 0, 1]
    previous = jnp.where(history[0, 0] == 2, init_states[0, 0, 0], current)
    payload = jnp.concatenate([previous, forcing[0, 0], current, mask_row], axis=0)
    timed = jnp.concatenate([cotangent[0, :, 0], jnp.broadcast_to(forcing[0], (ROLL,) + forcing.shape[2:])], axis=1)
    payload, timed = lax.optimization_barrier((payload, timed))
    payload = fetch_own(payload)
    timed = from_later(timed)

    def in_rows(values):
        top = jnp.concatenate([values[:states], values[2 * states :]], axis=0)
        bottom = values[states : 2 * states]
        return jnp.concatenate([jnp.pad(v, ((0, LANES - v.shape[0]), (0, 0))) for v in (top, bottom)], axis=0)

    def row(values, size):
        return jnp.pad(values, (0, size - values.shape[0]))[None]

    w_in_hi, w_in_lo = split_outside(pad_to(in_rows(w_in.T), (2 * LANES, width)))
    w_oi = pad_to(in_rows(jnp.dot(w_out, w_in, precision=HIGHEST).T), (2 * LANES, LANES))
    w_oi_hi, w_oi_lo = split_outside(w_oi)
    b_new = row(jnp.dot(w_out, b_in + b_down, precision=HIGHEST) + b_out, LANES)
    taps = jnp.broadcast_to(
        pad_to(w_dw.reshape(channels, KW * KW).T, (KW * KW, width))[:, None], (KW * KW, 8, width)
    )
    gain, bias = row(bn_gain, width), row(bn_bias, width)
    row_hi, row_lo = split_outside(pad_to(w_out, (SEG, channels)))
    out_parts = jnp.concatenate([row_hi, row_lo], axis=0)
    pieces = 5
    w_od_fwd, w_od_bwd = call(
        functools.partial(down_kernel, spans=spans), "down", (w_down, out_parts),
        [out(wide, 2 * LANES, dtype=BF16), out(2 * LANES, wide, dtype=BF16)],
        [pltpu.VMEM((channels, hidden), F32), pltpu.VMEM((SEG, hidden), F32), pltpu.VMEM((LANES, wide), F32), pltpu.SemaphoreType.DMA((pieces,))],
        20, micros=7, hbm=(0,), vmem_outs=(0, 1),
    )
    out_hi, out_lo = split_outside(pad_to(w_out, (SEG, width)))
    w_out_bwd = pad_to(jnp.concatenate([out_hi, out_hi, out_lo], axis=0), (2 * LANES, width))
    b_in_row = row(b_in, width)
    b_up_row = pad_to(b_up.reshape(steps // 2, 2, ff_block).swapaxes(0, 1).reshape(2, hidden // 2), (2, half)).reshape(1, wide)
    b_down_row = row(b_down, width)
    w_block = lax.dynamic_slice_in_dim(w_out, depth * col_block, col_block, axis=1).T
    w_block_hi, w_block_lo = split_outside(pad_to(w_block, (col_block, SEG)))
    prev, cur, ocean, first_sent = call(
        functools.partial(start_kernel, states=states, forces=forces), "start", (at, *payload),
        [out(px, LANES), out(px, LANES), out(px, LANES), out(block + 8, 3 * LANES)], [], 4, micros=1, smem=1,
    )
    first_came = to_sibling(first_sent)
    ready = lax.optimization_barrier(
        (w_up.T, timed, w_in_hi, w_in_lo, w_oi_hi, w_oi_lo, b_new, taps, gain, bias, w_out_bwd, b_in_row, b_up_row, b_down_row, w_block_hi, w_block_lo, at, first_sent)
    )
    up_source, timed, w_in_hi, w_in_lo, w_oi_hi, w_oi_lo, b_new, taps, gain, bias, w_out_bwd, b_in_row, b_up_row, b_down_row, w_block_hi, w_block_lo, at, first_sent = ready
    timed = fetch_own(timed)
    (w_up_all,) = call(
        functools.partial(up_kernel, k_main=k_main, k_rem=k_rem, spans=spans), "up", (up_source,),
        [out(2 * k_main + LANES, wide, dtype=BF16)],
        [pltpu.VMEM((3, k_main // 8, hidden), F32), pltpu.VMEM((k_main // 8, wide), F32), pltpu.SemaphoreType.DMA((3,))],
        10, micros=7, hbm=(0,), vmem_outs=(0,),
    )
    first_came, w_up_all = lax.optimization_barrier((first_came, w_up_all))
    force, force_send, cots = call(
        functools.partial(pack_kernel, states=states, forces=forces), "pack", (at, *timed),
        [out(ROLL, px, LANES), out(ROLL, block, LANES), out(ROLL, px, LANES)], [], 6, micros=2, smem=1,
    )
    force_edge = to_sibling(force_send)

    chunks = wide // CHUNK
    x_all, lifted_all, act_all, state_all = None, None, None, None
    kept = []
    prev_edge, cur_edge, prev_lanes, cur_lanes = first_came, first_came, 0, LANES
    for j in range(ROLL):
        mixed, stats, base, window, x_all, lifted_all = call(
            functools.partial(mix_kernel, turn=j, cur_lanes=cur_lanes, prev_lanes=prev_lanes), "mix",
            (at, cur, cur_edge, prev, prev_edge) + ((force, force_edge) if j else (at, at)) + (w_in_hi, w_in_lo, b_in_row, w_oi_hi, w_oi_lo, b_new, taps, ocean),
            [
                out(px, width), out(8, width), out(px, LANES), out(HALO + 2 * HALO, COLS, width), out(ROLL * block, 2 * LANES),
                out(ROLL * HALO, COLS, width),
            ],
            [
                pltpu.VMEM((rows + 2 * HALO, COLS + 16, width), F32), pltpu.VMEM((KW, rows + 2 * HALO, COLS, LANES), F32),
                pltpu.VMEM((rows, COLS, width), F32), pltpu.VMEM((block, 2 * LANES), F32), pltpu.SemaphoreType.DMA((3,)),
            ],
            12, micros=4.5, smem=1, hbm_outs=(3,), stacked=((4, x_all), (5, lifted_all)),
        )
        stats_other = to_sibling(stats)
        new, new_edge, norm_edge, inv, norm, slope, act_all, state_all = call(
            functools.partial(feed_kernel, turn=j, width=width, k_main=k_main, k_rem=k_rem), "feed",
            (at, mixed, stats, stats_other, first_sent, first_came, gain, bias, ocean, base, w_up_all, b_up_row, w_od_fwd),
            [
                out(px, LANES), out(block, LANES), out(block, width), out(8, width), out(px, width),
                out(chunks, px, CHUNK), out(chunks, ROLL * block, CHUNK), out(ROLL, SEG, block),
            ],
            [
                pltpu.VMEM((2 * px, k_main), BF16), pltpu.VMEM((px, LANES), BF16),
                pltpu.VMEM((px, CHUNK), F32), pltpu.VMEM((px, LANES), F32), pltpu.VMEM((px, CHUNK), F32), pltpu.VMEM((px, CHUNK), F32),
                pltpu.VMEM((px, CHUNK), F32), pltpu.VMEM((px, width), F32), pltpu.VMEM((chunks, px, CHUNK), F32),
                pltpu.VMEM((chunks, block, CHUNK), F32), pltpu.VMEM((SEG, block), F32), pltpu.SemaphoreType.DMA((2 * chunks + 2,)),
            ],
            16, micros=8.5, smem=1, hbm_outs=(4, 5), stacked=((6, act_all), (7, state_all)),
        )
        prev, prev_edge, prev_lanes, cur = cur, cur_edge, cur_lanes, new
        if j < ROLL - 1:
            cur_edge, cur_lanes = to_sibling(new_edge), 0
        norm_edge = to_sibling(norm_edge)
        kept.append((window, norm, norm_edge, slope, inv))

    states_home = lax.ppermute(state_all, both_axes, column_perm)
    quarter = channels // 2
    acc_rows = round_up(quarter + 1, 8)
    tap_rows = round_up(KW * KW, 8)
    carry, pending = None, jnp.zeros((px, LANES), F32)
    previous_step, keep_acc, give_acc, sums, lift_all, masked_all = None, None, None, None, None, None
    homes = []
    begin_scratch = [
        pltpu.VMEM((px, LANES), F32), pltpu.VMEM((chunks, px, CHUNK), F32), pltpu.VMEM((block, LANES), F32),
        pltpu.VMEM((px, wide), F32), pltpu.SemaphoreType.DMA((3,)),
    ]
    finish_scratch = [
        pltpu.VMEM((rows + 2 * HALO, COLS + 16, width), F32), pltpu.VMEM((KW, rows + 2 * HALO, COLS, LANES), F32),
        pltpu.VMEM((rows, COLS, width), F32), pltpu.VMEM((px, width), F32), pltpu.SemaphoreType.DMA,
    ]
    for j in range(ROLL - 1, -2, -1):
        finish, begin = j < ROLL - 1, j >= 0
        if finish:
            pending, keep_acc, give_acc = lax.optimization_barrier((pending, keep_acc, give_acc))
        if j == ROLL - 4:
            pending, states_home = lax.optimization_barrier((pending, states_home))
        args, outs, scratch, stacked, hbm = [at, ocean, pending], [], [], [], ()
        if finish:
            window, norm, norm_edge, slope, inv = kept[j + 1]
            grad_n, sent, came, grad_branch = previous_step
            args += [grad_n, sent, came, norm, norm_edge, inv, gain, first_sent, first_came, grad_branch, window, taps, w_in_hi, w_in_lo]
            outs += [out(px, LANES), out(px, LANES), out(tap_rows, width), out(2 * LANES, block), out(ROLL * block, width)]
            stacked.append((4, lift_all))
            scratch += finish_scratch
        if begin:
            hbm = (len(args), len(args) + 1)
            args += [cots, kept[j][3], kept[j][1], w_out_bwd, w_od_bwd, w_up_all]
            outs += [out(px, width), out(2 * px, wide, dtype=BF16), out(px, width), out(block + 8, width), out(ROLL * block, LANES)]
            stacked.append((len(outs) - 1, masked_all))
            scratch += begin_scratch
        kernel = functools.partial(
            back_kernel, finish=finish, begin=begin, turn=j, width=width, k_main=k_main, k_rem=k_rem, states=states
        )
        results = list(
            call(kernel, "back", args, outs, scratch, 20, micros=7 * finish + 7.5 * begin, smem=1, hbm=hbm, stacked=stacked)
        )
        if finish:
            carry, pending, tap_sum, home, lift_all = results[:5]
            results = results[5:]
            homes.append(home)
        if begin:
            grad_branch, hidden_now, grad_n, sent, masked_all = results
            came = to_sibling(sent)
            previous_step = (grad_n, sent, came, grad_branch)
            keep_acc, give_acc, sums, *up_row = call(
                functools.partial(weight_kernel, quarter=quarter, finish=finish), "weight",
                (at, kept[j][1], gain, bias, hidden_now, sent) + ((tap_sum, keep_acc, give_acc, sums) if finish else ()),
                [out(acc_rows, half), out(acc_rows, half), out(tap_rows + 8, width)] + ([] if j else [out(8, wide)]), [], 8, micros=5, smem=1,
                aliases=({7: 0, 8: 1, 9: 2} if j else {7: 0, 9: 2}) if finish else None, vmem_outs=(0, 1, 2) if j else (),
            )
            if j == 0:
                window, norm, norm_edge, slope, inv = kept[0]
                give_acc, came, norm_edge = lax.optimization_barrier((give_acc, came, norm_edge))
                kept[0] = (window, norm, norm_edge, slope, inv)
                previous_step = (grad_n, sent, came, grad_branch)

    def trade(values, axis, flip):
        return lax.ppermute(values, axis, [(i, i ^ flip) for i in range(lax.axis_size(axis))])

    def pick(first, second, bit):
        return jnp.where(bit == 0, first, second), jnp.where(bit == 0, second, first)

    token = [tap_sum]

    def local(kernel, args, outs, limit=8, **options):
        def body(at_ref, *refs):
            kernel(at_ref, *refs[: len(args)], *refs[len(args) + 1 : -1], **options)
            refs[-1][...] = refs[len(args)][:8, :LANES]

        results = call(body, kernel.__name__, (at, *args, token[0]), outs + [out(8, LANES)], [], limit, micros=1, smem=1)
        token[0] = results[-1]
        return results[:-1]

    direct = steps == 8 and devices_z == 4
    home_outs = [out(ROLL, states, block), out(8, block), out(2, states, block)]
    got = trade(give_acc, "step", 1)
    if direct:
        pieces = [out(2, col_block, ff_block)] * 4
        keep_a, give_a, keep_b, give_b = local(cut_first_kernel, (keep_acc, got), pieces, 16, rows=col_block, cols=ff_block)
        got_a, got_b = trade(give_a, "step", 2), trade(give_b, "step", 4)
    part_px = ROLL * block
    blocks = [(start, min(CHUNK, channels - start)) for start in range(0, channels, CHUNK)]
    table_keep, table_give, hidden_keep, hidden_give = call(
        functools.partial(last_kernel, spans=spans, blocks=blocks), "last",
        (
            at, masked_all, x_all, lift_all, lifted_all, act_all, w_down, b_down_row, sums,
            tap_sum, *up_row, token[0],
        ),
        [out(160, width), out(160, width), out(SEG, half), out(SEG, half)],
        [
            pltpu.VMEM((320, width), F32),
            pltpu.VMEM((part_px, LANES), F32), pltpu.VMEM((part_px, 2 * LANES), F32), pltpu.VMEM((part_px, width), F32),
            pltpu.VMEM(lifted_all.shape, F32), pltpu.VMEM((chunks, part_px, CHUNK), F32), pltpu.VMEM((channels, hidden), F32),
            pltpu.VMEM((2 * SEG, part_px), BF16), pltpu.VMEM((2, 2 * LANES, part_px), BF16), pltpu.VMEM((SEG, wide), F32),
            pltpu.VMEM((SEG, hidden), F32), pltpu.VMEM((2 * SEG, hidden), BF16),
            pltpu.SemaphoreType.DMA((4 + len(blocks) + chunks,)),
        ],
        44, micros=12, smem=1, hbm=(1, 2, 3, 4, 5, 6),
    )
    other = trade(table_give, "step", 1)
    hidden_other = trade(hidden_give, "step", 1)
    if direct:
        fours = (1, 2, 3)
        token[0] = table_keep
        keep_a, give_a, keep_b, give_b = local(cut_second_kernel, (keep_a, got_a, keep_b, got_b), [out(col_block, ff_block)] * 4)
        got_a, got_b = trade(give_a, "step", 4), trade(give_b, "step", 2)
        own = local(quarter_rows_kernel, (table_keep, other), [out(40, width)] * 4)
        from_xy = [trade(own[b], "step", 2 * b) for b in fours]
        h_own = local(quarter_cols_kernel, (hidden_keep, hidden_other), [out(SEG, ff_block)] * 4)
        h_xy = [trade(h_own[b], "step", 2 * b) for b in fours]
        (ending,) = local(going_kernel, homes[::-1], [out(8 * ROLL + 160, block)], states=states, forces=forces)
        ending = lax.ppermute(ending, both_axes, column_perm)
        (piece,) = local(sum_four_kernel, (own[0], *from_xy), [out(40, width)])
        near = trade(piece, "rows", 1)
        (h_piece,) = local(sum_four_kernel, (h_own[0], *h_xy), [out(SEG, ff_block)])
        h_near = trade(h_piece, "rows", 1)
        (piece,) = local(sum_two_kernel, (piece, near), [out(40, width)])
        far = trade(piece, "rows", 2)
        (h_piece,) = local(sum_two_kernel, (h_piece, h_near), [out(SEG, ff_block)])
        h_far = trade(h_piece, "rows", 2)
        keep, give = local(cut_third_kernel, (keep_a, got_a, keep_b, got_b), [out(col_block, ff_block)] * 2)
        got = trade(give, "rows", 1)
        (rolled,) = local(roll_kernel, (states_home, ending), [out(ROLL, 88, block)])
        gone = lax.all_to_all(rolled, "step", 0, 0, tiled=True)
        (piece,) = local(sum_two_kernel, (piece, far), [out(40, width)])
        from_xy = [trade(piece, "step", 2 * b) for b in fours]
        (share_down,) = local(share_down_kernel, (h_piece, h_far, w_block_hi, w_block_lo), [out(col_block, ff_block)])
        (share_up,) = local(turn_sum_kernel, (keep, got), [out(ff_block, col_block)])
        predicted, grad_forcing, grad_init = local(home_kernel, (gone, ending), home_outs, states=states)
        (mine,) = local(join_rows_kernel, (piece, *from_xy), [out(160, width)])
        other = trade(mine, "step", 1)
    else:
        units = steps // 2
        same_core = [[2 * k + c for k in range(units)] for c in range(2)]
        mine_up = keep_acc + got
        share = lax.psum_scatter(mine_up[:, : hidden // 2], "step", scatter_dimension=1, axis_index_groups=same_core, tiled=True)
        keep, give = pick(share[:col_block], share[col_block : 2 * col_block], side)
        share_up = (keep + trade(give, "rows", 1)).T
        mine_down = hidden_keep + hidden_other
        hidden_share = lax.psum(
            lax.psum_scatter(mine_down[:, : hidden // 2], "step", scatter_dimension=1, axis_index_groups=same_core, tiled=True), "rows"
        )
        nothing = jnp.zeros_like(hidden_share)
        (share_down,) = local(share_down_kernel, (hidden_share, nothing, w_block_hi, w_block_lo), [out(col_block, ff_block)])
        mine, other = pick(*[lax.psum(v, both_axes) for v in pick(table_keep, table_give, core)], core)
        (ending,) = local(going_kernel, homes[::-1], [out(8 * ROLL + 160, block)], states=states, forces=forces)
        ending = lax.ppermute(ending, both_axes, column_perm)
        gone = turn_round(to_later(jnp.concatenate([states_home, ending[: 8 * ROLL].reshape(ROLL, 8, block)], axis=1)))
        predicted, grad_forcing, grad_init = local(home_kernel, (gone, ending), home_outs, states=states)
    g_in, g_dw, g_w_out, lines = local(
        table_kernel, (mine, other),
        [out(2 * states + forces, channels), out(KW, KW, channels), out(states, channels), out(16, width)], states=states, forces=forces,
    )
    g_bias, g_gain, g_b_in = lines[0, :channels], lines[1, :channels], lines[7, :channels]
    g_b_up = lines[8:12].reshape(-1)[:wide].reshape(2, half)[:, : hidden // 2].reshape(2, steps // 2, ff_block).swapaxes(0, 1).reshape(-1)
    g_b_out = lines[12, :states]
    g_b_down = jnp.sum(w_out * g_b_out[:, None], axis=0)
    return (
        predicted[None, :, None],
        grad_init[None, None],
        grad_forcing[None, None, :forces],
        g_in.T,
        g_b_in,
        g_dw.transpose(2, 0, 1),
        g_gain,
        g_bias,
        share_up,
        g_b_up,
        share_down,
        g_b_down,
        g_w_out,
        g_b_out,
    )


def solution(mesh):
    state_spec = P("step", None, None, None, "rows")
    force_spec = P("step", None, None, "rows")
    in_specs = (state_spec, force_spec, P("step", None), P("rows")) + (P(),) * 11 + (state_spec,)
    out_specs = (state_spec, state_spec, force_spec) + (P(),) * 5 + (P("step", "rows"), P(), P("rows", "step"), P(), P(), P())
    return jax.shard_map(per_device, mesh=mesh, in_specs=in_specs, out_specs=out_specs, check_vma=False)
```

```python
import functools

import jax
import jax.numpy as jnp
from jax import lax
from jax.experimental import pallas as pl
from jax.experimental.pallas import tpu as pltpu
from jax.sharding import PartitionSpec as P

F32 = jnp.float32
BF16 = jnp.bfloat16
HIGHEST = lax.Precision.HIGHEST
ROLL = 8
COLS = 32
KW = 7
HALO = 3
EPSILON = 1e-05
LANES = 128
CHUNK = 256
SEG = 80
MIB = 2**20

ERF_P = 0.39
ERF_C = (0.23532534, 0.09138764, 0.64956134, -0.63540268, 0.88666585, -0.22753749)


def round_up(value, multiple):
    return -(-value // multiple) * multiple


def split(values):
    high = values.astype(BF16)
    return high, (values - high.astype(F32)).astype(BF16)


def split_outside(values):
    rounded = lax.reduce_precision(values, 8, 7)
    return rounded.astype(BF16), (values - rounded).astype(BF16)


def dot(left, right):
    return jnp.dot(left, right, preferred_element_type=F32)


def dot_t(left, right):
    return lax.dot_general(left, right, (((1,), (1,)), ((), ())), preferred_element_type=F32)


def gelu_both(v):
    e = jnp.exp(v * v * (-0.5))
    t = 1.0 / (1.0 + (ERF_P * 0.7071067811865476) * jnp.abs(v))
    q = 0.5 * ERF_C[5]
    for coefficient in ERF_C[4::-1]:
        q = q * t + 0.5 * coefficient
    q = (q * t) * e
    phi = jnp.where(v >= 0.0, 1.0 - q, q)
    return v * phi, phi + v * (e * 0.3989422804014327)


def depthwise(ext, shifted, kernel, mixed, lanes, flip, rows):
    rows_in = rows + 2 * HALO
    for q in range(KW):
        for r in range(rows_in):
            shifted[q, r] = ext[r, 5 + q : 5 + q + COLS, lanes]
    for v in range(0, COLS, 8):
        total = [None] * rows
        for q in range(KW):
            taps = [
                kernel[(KW * KW - 1 - (p * KW + q)) if flip else (p * KW + q), :, lanes]
                for p in range(KW)
            ]
            for r in range(rows_in):
                cell = shifted[q, r, v : v + 8, :]
                for p in range(KW):
                    i = r - p
                    if 0 <= i < rows:
                        term = taps[p] * cell
                        total[i] = term if total[i] is None else total[i] + term
        for i in range(rows):
            mixed[i, v : v + 8, lanes] = total[i]


def depthwise_direct(ext, kernel, mixed, lanes, rows):
    tiles = range(0, COLS, 8)
    total = [[None] * len(tiles) for _ in range(rows)]
    for q in range(KW):
        taps = [kernel[p * KW + q, :, lanes] for p in range(KW)]
        for r in range(rows + 2 * HALO):
            cells = ext[r, 5 + q : 5 + q + COLS, lanes]
            for t, v in enumerate(tiles):
                cell = cells[v : v + 8]
                for p in range(KW):
                    i = r - p
                    if 0 <= i < rows:
                        term = taps[p] * cell
                        total[i][t] = term if total[i][t] is None else total[i][t] + term
    for i in range(rows):
        for t, v in enumerate(tiles):
            mixed[i, v : v + 8, lanes] = total[i][t]


def ocean_count(sent, came):
    last = sent.shape[0] - 1
    return jnp.maximum(sent[last:, :LANES] + came[last:, :LANES], 1.0)


def group_lanes(group):
    return pl.ds(pl.multiple_of(group * LANES, LANES), LANES)


def mix_kernel(
    at, cur, cur_edge, prev, prev_edge, force, force_edge, w_in_hi, w_in_lo, b_in, w_oi_hi, w_oi_lo, b_new, taps, ocean,
    mixed_out, stats_out, base_out, window_out, x_all, lifted_all,
    ext, mixed, x_part, sems, *, turn, cur_lanes, prev_lanes,
):
    core, part = at[0], at[1]
    px = cur.shape[0]
    edge_px = x_part.shape[0]
    rows = px // COLS
    width = mixed_out.shape[1]
    prev_now, prev_edge_now = prev[...], prev_edge[:edge_px, prev_lanes : prev_lanes + LANES]
    if turn:
        prev_now, prev_edge_now = prev_now + force[turn], prev_edge_now + force_edge[turn]
    own = jnp.concatenate([prev_now, cur[...]], axis=1)
    edge = jnp.concatenate([prev_edge_now, cur_edge[:edge_px, cur_lanes : cur_lanes + LANES]], axis=1)
    own_hi, own_lo = split(own)
    edge_hi, edge_lo = split(edge)
    both = dot(jnp.concatenate([own_hi, edge_hi, own_lo, edge_lo], axis=0), w_in_hi[...])
    high = dot(jnp.concatenate([own_hi, edge_hi], axis=0), w_in_lo[...])
    lifted = (both[: px + edge_px] + both[px + edge_px :]) + (high + b_in[...])
    base_out[...] = dot(own_hi, w_oi_hi[...]) + dot(own_lo, w_oi_hi[...]) + dot(own_hi, w_oi_lo[...]) + b_new[...]
    zeros = jnp.zeros((rows + 2 * HALO, 8, width), F32)
    ext[:, :8, :] = zeros
    ext[:, 8 + COLS :, :] = zeros
    ext[HALO : HALO + rows, 8 : 8 + COLS, :] = lifted[:px].reshape(rows, COLS, width)
    ext[pl.ds((rows + HALO) * (1 - core), HALO), 8 : 8 + COLS, :] = lifted[px:].reshape(HALO, COLS, width)
    ext[pl.ds((rows + HALO) * core, HALO), 8 : 8 + COLS, :] = jnp.zeros((HALO, COLS, width), F32)
    part_rows = window_out.shape[0] - 2 * HALO
    part_px = x_part.shape[0]
    x_part[...] = jnp.where(part == 0, own[:part_px], own[part_px:])
    here = pl.ds(turn * part_rows, part_rows)
    keeps = [
        pltpu.make_async_copy(ext.at[pl.ds(part * part_rows, window_out.shape[0]), 8 : 8 + COLS, :], window_out, sems.at[0]),
        pltpu.make_async_copy(ext.at[pl.ds(part * part_rows + HALO, part_rows), 8 : 8 + COLS, :], lifted_all.at[here], sems.at[1]),
        pltpu.make_async_copy(x_part, x_all.at[pl.ds(turn * part_px, part_px)], sems.at[2]),
    ]
    for keep in keeps:
        keep.start()
    mask = ocean[...]

    def group(g, _):
        lanes = group_lanes(g)
        depthwise_direct(ext, taps, mixed, lanes, rows)
        cells = mixed[:, :, lanes].reshape(px, LANES)
        mixed_out[:, lanes] = cells
        masked = cells * mask
        stats_out[0:1, lanes] = jnp.sum(masked, axis=0, keepdims=True)
        stats_out[1:2, lanes] = jnp.sum(masked * cells, axis=0, keepdims=True)
        return 0

    lax.fori_loop(0, width // LANES, group, 0)
    for keep in keeps:
        keep.wait()


def feed_kernel(
    at, mixed, stats, stats_other, sent, came, gain, bias, ocean, base, w_up, b_up, w_od,
    new_out, new_edge_out, norm_edge_out, inv_out, norm_out, slope_out, act_all, state_all,
    stack, rem, acc, acc_lo, hold_a, hold_b, hold_act, norm, slope, act_part, state, sems, *, turn, width, k_main, k_rem,
):
    core, part = at[0], at[1]
    px = mixed.shape[0]
    chunks = w_up.shape[1] // CHUNK
    part_px = act_part.shape[1]
    total = ocean_count(sent, came)
    keep_norm = pltpu.make_async_copy(norm, norm_out, sems.at[2 * chunks])

    for g in range(width // LANES):
        lanes = slice(g * LANES, (g + 1) * LANES)
        cells = mixed[:, lanes]
        average = (stats[0:1, lanes] + stats_other[0:1, lanes]) / total
        variance = (stats[1:2, lanes] + stats_other[1:2, lanes]) / total - average * average
        inverse = lax.rsqrt(variance + EPSILON)
        inv_out[:, lanes] = jnp.broadcast_to(inverse, (8, LANES))
        normalized = (cells - average) * inverse
        norm[:, lanes] = normalized
        normed = normalized * gain[:, lanes] + bias[:, lanes]
        high = normed.astype(BF16)
        high_f = high.astype(F32)
        low_f = normed - high_f
        if (g + 1) * LANES <= k_main:
            stack[:px, lanes] = high
            stack[px:, lanes] = low_f.astype(BF16)
        else:
            rem[...] = (high_f + pltpu.roll(low_f, k_rem, 1) + pltpu.roll(high_f, 2 * k_rem, 1)).astype(BF16)
    keep_norm.start()
    edge_px = norm_edge_out.shape[0]
    norm_edge_out[...] = norm[pl.ds(pl.multiple_of((1 - core) * (px - edge_px), 8), edge_px), :]

    def up(t, hold):
        cols = pl.ds(pl.multiple_of(t * CHUNK, CHUNK), CHUNK)
        both = dot(stack[...], w_up[:k_main, cols])
        high = dot(stack[:px], w_up[k_main : 2 * k_main, cols])
        rest = dot(rem[...], w_up[2 * k_main :, cols])
        hold[...] = (both[:px] + both[px:]) + (high + rest)

    def keep_slope(t):
        return pltpu.make_async_copy(slope.at[t], slope_out.at[t], sems.at[t])

    def keep_act(t):
        return pltpu.make_async_copy(act_part.at[t], act_all.at[t, pl.ds(turn * part_px, part_px)], sems.at[chunks + t])

    def act(t, hold):
        cols = pl.ds(pl.multiple_of(t * CHUNK, CHUNK), CHUNK)
        activated, slope[t] = gelu_both(hold[...] + b_up[:, cols])
        hold_act[...] = activated
        high, low = split(activated)
        acc[...] += dot(high, w_od[cols, :])
        acc_lo[...] += dot(low, w_od[cols, :LANES])
        act_part[t] = hold_act[pl.ds(pl.multiple_of(part * part_px, 8), part_px), :]
        keep_slope(t).start()
        keep_act(t).start()

    acc[...] = jnp.zeros_like(acc)
    acc_lo[...] = base[...]
    up(0, hold_a)

    def pair(i, _):
        up(2 * i + 1, hold_b)
        act(2 * i, hold_a)
        up(2 * i + 2, hold_a)
        act(2 * i + 1, hold_b)
        return 0

    for i in range(chunks // 2):
        pair(i, 0)
    act(chunks - 1, hold_a)
    new = (acc[:, :LANES] + acc[:, LANES:] + acc_lo[...]) * ocean[...]
    new_out[...] = new
    new_edge_out[...] = new_out[pl.ds(pl.multiple_of((1 - core) * (px - edge_px), 8), edge_px), :]
    mine = jnp.where(part == 0, new[:part_px], new[part_px:])
    state[...] = mine.T[: state.shape[0]]
    keep_state = pltpu.make_async_copy(state, state_all.at[turn], sems.at[2 * chunks + 1])
    keep_state.start()
    keep_norm.wait()
    keep_state.wait()
    for t in range(chunks):
        keep_slope(t).wait()
        keep_act(t).wait()


def back_kernel(*refs, finish, begin, turn, width, k_main, k_rem, states):
    refs = list(refs)

    def take(count):
        out = refs[:count]
        del refs[:count]
        return out

    (at, ocean, pending_in) = take(3)
    if finish:
        (grad_n, sent, came, norm, norm_edge, inv, gain, first_sent, first_came, grad_branch, window, taps, w_in_hi, w_in_lo) = take(14)
    if begin:
        (cots, slope_hbm, norm_now, w_out, w_od, w_up) = take(6)
    if finish:
        (carry_out, pending_out, taps_out, home_out, lift_all) = take(5)
    if begin:
        (branch_out, hidden_out, grad_n_out, send_out, masked_all) = take(5)
    if finish:
        (ext, shifted, mixed, grad_lift, lift_sem) = take(5)
    if begin:
        (cot, slope, masked_part, pulled, begin_sems) = take(5)
    core, part = at[0], at[1]
    px = ocean.shape[0]
    rows = px // COLS
    part_px = px // 2
    if begin:
        get_cot = pltpu.make_async_copy(cots.at[turn], cot, begin_sems.at[0])
        get_slope = pltpu.make_async_copy(slope_hbm, slope, begin_sems.at[1])
        get_cot.start()
        get_slope.start()
    if finish:
        edge_px = norm_edge.shape[0]
        total = ocean_count(first_sent, first_came)
        ocean_edge = first_came[:edge_px, 2 * LANES :]
        zeros = jnp.zeros((rows + 2 * HALO, 8, width), F32)
        ext[:, :8, :] = zeros
        ext[:, 8 + COLS :, :] = zeros
        ext[pl.ds((rows + HALO) * core, HALO), 8 : 8 + COLS, :] = jnp.zeros((HALO, COLS, width), F32)
        part_rows = window.shape[0] - 2 * HALO
        for g in range(width // LANES):
            lanes = slice(g * LANES, (g + 1) * LANES)
            bias_sum = (sent[edge_px : edge_px + 1, lanes] + came[edge_px : edge_px + 1, lanes]) / total
            gain_sum = (sent[edge_px + 1 : edge_px + 2, lanes] + came[edge_px + 1 : edge_px + 2, lanes]) / total
            scale = inv[0:1, lanes] * gain[:, lanes]
            mix = scale * (grad_n[:, lanes] - ocean[...] * (bias_sum + norm[:, lanes] * gain_sum))
            mix_edge = scale * (came[:edge_px, lanes] - ocean_edge * (bias_sum + norm_edge[:, lanes] * gain_sum))
            ext[HALO : HALO + rows, 8 : 8 + COLS, lanes] = mix.reshape(rows, COLS, LANES)
            ext[pl.ds((rows + HALO) * (1 - core), HALO), 8 : 8 + COLS, lanes] = mix_edge.reshape(HALO, COLS, LANES)

        def group(g, _):
            lanes = group_lanes(g)
            depthwise(ext, shifted, taps, mixed, lanes, True, rows)
            grad_lift[:, lanes] = mixed[:, :, lanes].reshape(px, LANES) + grad_branch[:, lanes]
            for q in range(KW):
                sums = [None] * KW
                for i in range(part_rows):
                    for v in range(0, COLS, 8):
                        grad = shifted[KW - 1 - q, HALO + part * part_rows + i, v : v + 8, :]
                        for p in range(KW):
                            term = grad * window[i + p, v : v + 8, lanes]
                            sums[p] = term if sums[p] is None else sums[p] + term
                for p in range(KW):
                    taps_out[p * KW + q : p * KW + q + 1, lanes] = jnp.sum(sums[p], axis=0, keepdims=True)
            return 0

        lax.fori_loop(0, width // LANES, group, 0)
        keep_lift = pltpu.make_async_copy(
            grad_lift.at[pl.ds(pl.multiple_of(part * part_px, 8), part_px)], lift_all.at[pl.ds((turn + 1) * part_px, part_px)], lift_sem
        )
        keep_lift.start()
        high, low = split(grad_lift[...])
        both = dot_t(jnp.concatenate([high, low], axis=0), w_in_hi[...])
        grad_x = (both[:px] + both[px:]) + dot_t(high, w_in_lo[...])
        carry = grad_x[:, LANES:] + pending_in[...]
        carry_out[...] = carry
        pending_out[...] = grad_x[:, :LANES]
        part_x = jnp.where(part == 0, grad_x[:part_px, :LANES], grad_x[part_px:, :LANES])
        part_c = jnp.where(part == 0, carry[:part_px], carry[part_px:])
        home_out[:LANES] = part_x.T
        home_out[LANES:] = part_c.T
    if begin:
        get_cot.wait()
        grad_new = cot[...] + carry if finish else cot[...]
        lane = lax.broadcasted_iota(jnp.int32, (px, LANES), 1)
        masked = jnp.where(lane < states, grad_new * ocean[...], 0.0)
        masked_part[...] = jnp.where(part == 0, masked[:part_px], masked[part_px:])
        keep_masked = pltpu.make_async_copy(masked_part, masked_all.at[pl.ds(turn * part_px, part_px)], begin_sems.at[2])
        keep_masked.start()
        high_f = masked.astype(BF16).astype(F32)
        nothing = jnp.zeros((px, LANES), F32)
        high_w = jnp.concatenate([high_f, nothing], axis=1)
        low_w = jnp.concatenate([masked - high_f, nothing], axis=1)
        left = (high_w + pltpu.roll(low_w, SEG, 1) + pltpu.roll(high_w, 2 * SEG, 1)).astype(BF16)
        branch_out[...] = dot(left, w_out[...])
        chunks = w_od.shape[1] // CHUNK
        get_slope.wait()

        half = w_od.shape[1] // 2

        def pull(t, _):
            cols = pl.ds(pl.multiple_of(t * half, half), half)
            pulled[:, cols] = dot(left, w_od[:, cols])
            return 0

        lax.fori_loop(0, 2, pull, 0)

        def chunk(t, _):
            cols = pl.ds(pl.multiple_of(t * CHUNK, CHUNK), CHUNK)
            high, low = split(pulled[:, cols] * slope[t])
            hidden_out[:px, cols] = high
            hidden_out[px:, cols] = low
            return 0

        lax.fori_loop(0, chunks, chunk, 0)
        both = dot_t(hidden_out[...], w_up[:k_main])
        grad_n_out[:, :k_main] = (both[:px] + both[px:]) + dot_t(hidden_out[:px], w_up[k_main : 2 * k_main])
        rest = dot_t(hidden_out[...], w_up[2 * k_main :])
        tail = rest[:px] + rest[px:] + pltpu.roll(rest[:px], LANES - 2 * k_rem, 1)
        grad_n_out[:, k_main:] = jnp.where(lane < k_rem, tail, 0.0)
        edge_px = send_out.shape[0] - 8
        for g in range(width // LANES):
            lanes = slice(g * LANES, (g + 1) * LANES)
            cells = grad_n_out[:, lanes]
            send_out[edge_px : edge_px + 1, lanes] = jnp.sum(cells, axis=0, keepdims=True)
            send_out[edge_px + 1 : edge_px + 2, lanes] = jnp.sum(cells * norm_now[:, lanes], axis=0, keepdims=True)
        send_out[edge_px + 2 :, :] = jnp.zeros((6, width), F32)
        send_out[:edge_px, :] = grad_n_out[pl.ds(pl.multiple_of((1 - core) * (px - edge_px), 8), edge_px), :]
        keep_masked.wait()
    if finish:
        keep_lift.wait()


def weight_kernel(at, norm, gain, bias, hidden, send, *rest, quarter, finish):
    if finish:
        taps, keep_in, give_in, sums_in, keep_out, give_out, sums_out, *up_row = rest
    else:
        keep_out, give_out, sums_out, *up_row = rest
    core = at[0]
    part = at[1]
    px = norm.shape[0]
    tap_rows = sums_out.shape[0] - 8
    if finish:
        sums_out[:tap_rows] = sums_in[:tap_rows] + taps[...]
        sums_out[tap_rows:] = sums_in[tap_rows:] + send[send.shape[0] - 8 :]
    else:
        sums_out[:tap_rows] = jnp.zeros((tap_rows, sums_out.shape[1]), F32)
        sums_out[tap_rows:] = send[send.shape[0] - 8 :]
    window = round_up(quarter, LANES)
    base = (quarter // LANES) * LANES
    normed = norm[...] * gain[...] + bias[...]
    second = pltpu.roll(normed[:, base : base + window], window - (quarter - base), 1)
    mine = jnp.where(part == 0, normed[:, :window], second)
    lane = lax.broadcasted_iota(jnp.int32, (px, window), 1)
    mine = jnp.where(lane < quarter, mine, jnp.where(lane == quarter, 1.0, 0.0))
    high, low = split(mine.T[: keep_out.shape[0]])
    half = keep_out.shape[1]

    for side, acc_out in enumerate((keep_out, give_out)):
        actual = core if side == 0 else 1 - core
        cols = pl.ds(pl.multiple_of(actual * half, LANES), half)
        new = dot(high, hidden[:px, cols]) + dot(high, hidden[px:, cols]) + dot(low, hidden[:px, cols])
        acc_out[...] = (keep_in, give_in)[side][...] + new if finish else new
    if up_row:
        line = quarter // 8 * 8
        for side, acc_out in ((core, keep_out), (1 - core, give_out)):
            up_row[0][:, pl.ds(pl.multiple_of(side * half, LANES), half)] = acc_out[line : line + 8, :]


VMEM_SPEC = pl.BlockSpec(memory_space=pltpu.VMEM)
SMEM_SPEC = pl.BlockSpec(memory_space=pltpu.SMEM)
HBM_SPEC = pl.BlockSpec(memory_space=pltpu.HBM)


def out(*shape, dtype=F32):
    return jax.ShapeDtypeStruct(shape, dtype)


def in_hbm(values):
    return pltpu.with_memory_space_constraint(values, pltpu.HBM)


def call(kernel, name, args, outs, scratch, limit, *, micros, smem=0, hbm=(), hbm_outs=(), vmem_outs=(), aliases=None, stacked=()):
    args = [in_hbm(a) if i in hbm else a for i, a in enumerate(args)]
    specs = [SMEM_SPEC if i < smem else HBM_SPEC if i in hbm else VMEM_SPEC for i in range(len(args))]
    hbm_outs = tuple(hbm_outs) + tuple(i for i, _ in stacked)
    aliases = dict(aliases or {})
    used = len(args)
    for i, buffer in stacked:
        if buffer is not None:
            aliases[len(args)] = i
            args.append(in_hbm(buffer))
            specs.append(HBM_SPEC)
    extra = len(args) - used

    def body(*refs):
        kernel(*refs[:used], *refs[used + extra :])

    return pl.pallas_call(
        body,
        in_specs=specs,
        out_specs=[HBM_SPEC if i in hbm_outs else VMEM_SPEC for i in range(len(outs))],
        out_shape=[
            pltpu.HBM(o.shape, o.dtype) if i in hbm_outs else pltpu.VMEM(o.shape, o.dtype) if i in vmem_outs else o
            for i, o in enumerate(outs)
        ],
        scratch_shapes=scratch,
        input_output_aliases=aliases,
        compiler_params=pltpu.CompilerParams(vmem_limit_bytes=limit * MIB),
        cost_estimate=pl.CostEstimate(flops=int(micros * 1.1e9), bytes_accessed=1024, transcendentals=0),
        name=name,
    )(*args)


def start_kernel(at, first, second, prev_out, cur_out, ocean_out, send_out, *, states, forces):
    core, part = at[0], at[1]
    block = first.shape[1]
    rows = first.shape[0]
    mask_row = 2 * states + forces

    def turn(values):
        prev = jnp.concatenate([values[: states + forces], jnp.zeros((LANES - states - forces, block), F32)], axis=0).T
        cur = jnp.concatenate([values[states + forces : mask_row], jnp.zeros((LANES - states, block), F32)], axis=0).T
        mask = jnp.broadcast_to(values[mask_row : mask_row + 1], (LANES, block)).T
        return prev, cur, mask

    zero, one = first[...], second[...]
    swap = part == 1
    top, low = jnp.where(swap, one, zero), jnp.where(swap, zero, one)
    count = jnp.sum(top[mask_row : mask_row + 1]) + jnp.sum(low[mask_row : mask_row + 1])
    for i, values in enumerate((top, low)):
        prev, cur, mask = turn(values)
        here = slice(i * block, (i + 1) * block)
        prev_out[here] = prev
        cur_out[here] = cur
        ocean_out[here] = mask
    at_edge = pl.ds(pl.multiple_of((1 - core) * block, 8), block)
    send_out[:block, :LANES] = prev_out[at_edge, :]
    send_out[:block, LANES : 2 * LANES] = cur_out[at_edge, :]
    send_out[:block, 2 * LANES :] = ocean_out[at_edge, :]
    send_out[block:] = jnp.full((8, 3 * LANES), count)


def pack_kernel(at, first, second, force_out, force_send, cot_out, *, states, forces):
    core, part = at[0], at[1]
    steps, rows, block = first.shape
    lane = lax.broadcasted_iota(jnp.int32, (block, LANES), 1)
    for j in range(steps):
        turned = [
            jnp.concatenate([values[j], jnp.zeros((LANES - rows, block), F32)], axis=0).T for values in (first, second)
        ]
        top, low = jnp.where(part == 1, turned[1], turned[0]), jnp.where(part == 1, turned[0], turned[1])
        for i, values in enumerate((top, low)):
            cot_out[j, i * block : (i + 1) * block] = jnp.where(lane < states, values, 0.0)
            force_out[j, i * block : (i + 1) * block] = jnp.where(lane < states, 0.0, values)
        force_send[j] = force_out[j, pl.ds(pl.multiple_of((1 - core) * block, 8), block), :]


def reorder(source, target, spans):
    for start, size, place in spans:
        target[:, place : place + size] = source[:, start : start + size]


def up_kernel(w_up_t, up_all, raw, turned, sems, *, k_main, k_rem, spans):
    slots, block = raw.shape[0], raw.shape[1]
    blocks = k_main // block

    def get(t, size):
        slot = lax.rem(t, slots)
        return pltpu.make_async_copy(
            w_up_t.at[pl.ds(pl.multiple_of(t * block, 8), size)], raw.at[slot, pl.ds(0, size)], sems.at[slot]
        )

    for t in range(slots):
        get(t, block).start()
    turned[...] = jnp.zeros_like(turned)

    def main(t, _):
        get(t, block).wait()
        reorder(raw.at[lax.rem(t, slots)], turned, spans)

        @pl.when(t + slots < blocks)
        def _():
            get(t + slots, block).start()

        @pl.when(t + slots == blocks)
        def _():
            get(t + slots, k_rem).start()

        high, low = split(turned[...])
        up_all[pl.ds(pl.multiple_of(t * block, block), block), :] = high
        up_all[pl.ds(pl.multiple_of(k_main + t * block, block), block), :] = low
        return 0

    lax.fori_loop(0, blocks, main, 0)
    get(blocks, k_rem).wait()
    reorder(raw.at[blocks % slots, pl.ds(0, k_rem)], turned.at[pl.ds(0, k_rem)], spans)
    high, low = split(turned[:k_rem])
    base = 2 * k_main
    up_all[base : base + k_rem] = high
    up_all[base + k_rem : base + 2 * k_rem] = high
    up_all[base + 2 * k_rem : base + 3 * k_rem] = low
    up_all[base + 3 * k_rem :] = jnp.zeros((LANES - 3 * k_rem, up_all.shape[1]), BF16)


def down_kernel(w_down, out_parts, od_fwd, od_bwd, down, product, ordered, sems, *, spans):
    pieces = sems.shape[0]
    piece = down.shape[1] // pieces

    def get(t):
        cols = pl.ds(pl.multiple_of(t * piece, LANES), piece)
        return pltpu.make_async_copy(w_down.at[:, cols], down.at[:, cols], sems.at[t])

    for t in range(pieces):
        get(t).start()
    ordered[...] = jnp.zeros_like(ordered)

    def multiply(t, _):
        cols = pl.ds(pl.multiple_of(t * piece, LANES), piece)
        get(t).wait()
        high, low = split(down[:, cols])
        both = dot(out_parts[...], high)
        product[:, cols] = (both[:SEG] + both[SEG:]) + dot(out_parts[:SEG], low)
        return 0

    lax.fori_loop(0, pieces, multiply, 0)
    reorder(product, ordered.at[pl.ds(0, SEG)], spans)

    def spread(t, _):
        cols = pl.ds(pl.multiple_of(t * CHUNK, CHUNK), CHUNK)
        values = ordered[:, cols]
        high, low = split(values)
        od_bwd[:SEG, cols] = high[:SEG]
        od_bwd[SEG : 2 * SEG, cols] = high[:SEG]
        od_bwd[2 * SEG : 3 * SEG, cols] = low[:SEG]
        od_bwd[3 * SEG :, cols] = jnp.zeros((od_bwd.shape[0] - 3 * SEG, CHUNK), BF16)
        high, low = split(values.T)
        od_fwd[cols, :LANES] = high
        od_fwd[cols, LANES:] = low
        return 0

    lax.fori_loop(0, ordered.shape[1] // CHUNK, spread, 0)


def last_kernel(
    at, masked_hbm, x_hbm, lifts_hbm, lifted_hbm, act_hbm, down_hbm, b_down, sums, taps, up_row, token, table_keep, table_give, hidden_keep, hidden_give,
    table,    masked, x_parts, lifts, lifted, act, down, masked_t, x_t, g_hidden, natural, g_parts, sems, *, spans, blocks,
):
    chunks = act.shape[0]
    half = hidden_keep.shape[1]
    width = table.shape[1]
    scale = (at[1] == 0).astype(F32)
    tap_rows = taps.shape[0]
    pairs = [(masked_hbm, masked), (x_hbm, x_parts), (lifts_hbm, lifts), (lifted_hbm, lifted)]
    firsts = [pltpu.make_async_copy(pair[0], pair[1], sems.at[i]) for i, pair in enumerate(pairs)]
    downs = [
        pltpu.make_async_copy(down_hbm.at[pl.ds(start, size)], down.at[pl.ds(start, size)], sems.at[4 + i])
        for i, (start, size) in enumerate(blocks)
    ]

    def get(t):
        return pltpu.make_async_copy(act_hbm.at[t], act.at[t], sems.at[4 + len(blocks) + t])

    firsts[0].start()
    for t in range(chunks):
        get(t).start()
    for copy in firsts[1:] + downs:
        copy.start()
    firsts[0].wait()
    turned = masked[...].T[:SEG]
    high = turned.astype(BF16)
    masked_t[:SEG] = high
    masked_t[SEG:] = (turned - high.astype(F32)).astype(BF16)
    total = jnp.sum(turned, axis=1, keepdims=True)

    def chunk(t, _):
        get(t).wait()
        high, low = split(act[t])
        both = dot(masked_t[...], high)
        sums_now = (both[:SEG] + both[SEG:]) + dot(masked_t[:SEG], low)
        g_hidden[:, pl.ds(pl.multiple_of(t * CHUNK, CHUNK), CHUNK)] = sums_now
        return 0

    lax.fori_loop(0, chunks, chunk, 0)
    hidden_keep[...] = g_hidden[:, pl.ds(pl.multiple_of(at[0] * half, LANES), half)]
    hidden_give[...] = g_hidden[:, pl.ds(pl.multiple_of((1 - at[0]) * half, LANES), half)]
    for start, size, place in spans:
        natural[:, start : start + size] = g_hidden[:, place : place + size]
    high, low = split(natural[...])
    g_parts[:SEG] = high
    g_parts[SEG:] = low
    for copy in firsts[1:]:
        copy.wait()
    high, low = split(x_parts[...].T)
    x_t[0] = high
    x_t[1] = low
    for start in range(0, width, CHUNK):
        size = min(CHUNK, width - start)
        lanes = slice(start, start + size)
        high, low = split(lifted[:, :, lanes].reshape(lifts.shape[0], size))
        both = dot(masked_t[...], high)
        lifted_sum = (both[:SEG] + both[SEG:]) + dot(masked_t[:SEG], low)
        grads = lifts[:, lanes]
        high, low = split(grads)
        g_in = dot(x_t[0], high) + dot(x_t[1], high) + dot(x_t[0], low)
        table[:88, lanes] = g_in[:88]
        table[88:168, lanes] = g_in[LANES : LANES + 80]
        table[168:224, lanes] = sums[:tap_rows, lanes] + taps[:, lanes]
        table[224:304, lanes] = lifted_sum + total * b_down[:, lanes]
        table[304:311, lanes] = sums[tap_rows : tap_rows + 7, lanes] * scale
        table[311:312, lanes] = jnp.sum(grads, axis=0, keepdims=True)
    for (start, size), copy in zip(blocks, downs):
        copy.wait()
        high, low = split(down[start : start + size])
        both = dot_t(g_parts[...], high)
        g_out = (both[:SEG] + both[SEG:]) + dot_t(g_parts[:SEG], low)
        table[224:304, start : start + size] += g_out
    table[312:] = jnp.zeros((table.shape[0] - 312, width), F32)
    for i, start in enumerate(range(0, up_row.shape[1], width)):
        size = min(width, up_row.shape[1] - start)
        table[312 + i : 313 + i, :size] = up_row[:1, start : start + size] * scale
    table[316:317, :LANES] = jnp.sum(masked[...], axis=0, keepdims=True)
    rows = table_keep.shape[0]
    table_keep[...] = table[pl.ds(pl.multiple_of(at[0] * rows, 8), rows), :]
    table_give[...] = table[pl.ds(pl.multiple_of((1 - at[0]) * rows, 8), rows), :]


def flags(at):
    return at[3], at[4], at[5], at[2]


def cut_first_kernel(at, keep, got, keep_a, give_a, keep_b, give_b, *, rows, cols):
    x, y, _, _ = flags(at)

    def part(row, k):
        here = (slice(row * rows, (row + 1) * rows), slice(k * cols, (k + 1) * cols))
        return keep[here] + got[here]

    for i, (even, odd) in enumerate(((0, 1), (2, 3))):
        one, two = part(0, even), part(0, odd)
        keep_a[i] = jnp.where(x == 0, one, two)
        give_a[i] = jnp.where(x == 0, two, one)
    for i, (low, top) in enumerate(((0, 2), (1, 3))):
        one, two = part(1, low), part(1, top)
        keep_b[i] = jnp.where(y == 0, one, two)
        give_b[i] = jnp.where(y == 0, two, one)


def cut_second_kernel(at, keep_a, got_a, keep_b, got_b, keep_a_out, give_a_out, keep_b_out, give_b_out):
    x, y, _, _ = flags(at)
    for bit, keep, got, keep_out, give_out in (
        (y, keep_a, got_a, keep_a_out, give_a_out),
        (x, keep_b, got_b, keep_b_out, give_b_out),
    ):
        keep_out[...] = keep[bit] + got[bit]
        give_out[...] = keep[1 - bit] + got[1 - bit]


def cut_third_kernel(at, keep_a, got_a, keep_b, got_b, keep_out, give_out):
    _, _, _, side = flags(at)
    one, two = keep_a[...] + got_a[...], keep_b[...] + got_b[...]
    keep_out[...] = jnp.where(side == 0, one, two)
    give_out[...] = jnp.where(side == 0, two, one)


def turn_sum_kernel(at, keep, got, out_ref):
    out_ref[...] = (keep[...] + got[...]).T


def quarter_rows_kernel(at, keep, got, *outs):
    rows = outs[0].shape[0]
    pair = at[5]
    for b, out_ref in enumerate(outs):
        place = pl.multiple_of((pair ^ b) * rows, 8)
        out_ref[...] = keep[pl.ds(place, rows), :] + got[pl.ds(place, rows), :]


def quarter_cols_kernel(at, keep, got, *outs):
    cols = outs[0].shape[1]
    pair = at[5]
    parts = [keep[:, k * cols : (k + 1) * cols] + got[:, k * cols : (k + 1) * cols] for k in range(4)]
    for b, out_ref in enumerate(outs):
        k = pair ^ b
        low = jnp.where(k == 0, parts[0], parts[1])
        top = jnp.where(k == 2, parts[2], parts[3])
        out_ref[...] = jnp.where(k < 2, low, top)


def sum_two_kernel(at, a, b, out_ref):
    out_ref[...] = a[...] + b[...]


def sum_four_kernel(at, a, b, c, d, out_ref):
    out_ref[...] = (a[...] + b[...]) + (c[...] + d[...])


def join_rows_kernel(at, a, b, c, d, out_ref):
    rows = a.shape[0]
    for flip, ref in enumerate((a, b, c, d)):
        out_ref[pl.ds(pl.multiple_of((at[5] ^ flip) * rows, 8), rows), :] = ref[...]


def share_down_kernel(at, a, b, w_hi, w_lo, out_ref):
    high, low = split(a[...] + b[...])
    out_ref[...] = dot(w_hi[...], high) + dot(w_hi[...], low) + dot(w_lo[...], high)


def table_kernel(at, mine, other, g_in, g_dw, g_out, rows_out, *, states, forces):
    core = at[0]
    half = mine.shape[0]
    channels = g_in.shape[1]

    def get(start, size):
        pieces = []
        for base in (0, half):
            low, top = max(start, base), min(start + size, base + half)
            if low < top:
                here = slice(low - base, top - base)
                pieces.append(jnp.where(core == (base > 0), mine[here, :channels], other[here, :channels]))
        return pieces[0] if len(pieces) == 1 else jnp.concatenate(pieces, axis=0)

    g_in[:states] = get(0, 88)[:states]
    g_in[states : 2 * states] = get(88, 80)[:states]
    g_in[2 * states :] = get(0, 88)[states : states + forces]
    taps = get(168, 56)
    for p in range(KW):
        g_dw[p] = taps[p * KW : (p + 1) * KW]
    g_out[...] = get(224, 80)[:states]
    for i, start in enumerate((304, 312)):
        piece = jnp.where(core == (start >= half), mine[start % half : start % half + 8], other[start % half : start % half + 8])
        rows_out[8 * i : 8 * i + 8] = piece


def going_kernel(at, *refs, states, forces):
    homes, out_ref = refs[:-1], refs[-1]
    steps = len(homes)
    block = out_ref.shape[1]
    for j in range(steps):
        out_ref[8 * j : 8 * j + 8] = jnp.concatenate([homes[j][states : states + forces], jnp.zeros((8 - forces, block), F32)], axis=0)
    out_ref[8 * steps : 8 * steps + 80] = homes[0][:80]
    out_ref[8 * steps + 80 :] = homes[0][LANES : LANES + 80]


def roll_kernel(at, states, forces, out_ref):
    steps = out_ref.shape[0]
    high = states.shape[1]
    for i in range(steps):
        here = lax.rem(i - at[6] + steps, steps)
        out_ref[i, :high] = states[here]
        out_ref[i, high:] = forces[pl.ds(pl.multiple_of(here * 8, 8), 8), :]


def home_kernel(at, gone, ending, predicted, grad_forcing, grad_init, *, states):
    steps = gone.shape[0]
    total = gone[0, SEG:]
    for i in range(steps):
        predicted[i] = gone[lax.rem(at[6] - i + steps, steps), :states]
        if i:
            total = total + gone[i, SEG:]
    grad_forcing[...] = total
    base = 8 * steps
    prev, cur = ending[base : base + SEG][:states], ending[base + SEG : base + 2 * SEG][:states]
    single = at[7] == 1
    grad_init[0] = jnp.where(single, 0.0, prev)
    grad_init[1] = jnp.where(single, cur + prev, cur)


def pad_to(values, shape):
    return jnp.pad(values, [(0, size - have) for size, have in zip(shape, values.shape)])


def per_device(
    init_states, forcing, history, land_mask, w_in, b_in, w_dw, bn_gain, bn_bias, w_up, b_up, w_down, b_down, w_out, b_out, cotangent
):
    steps = lax.axis_size("step")
    devices_z = lax.axis_size("rows")
    step = lax.axis_index("step")
    depth = lax.axis_index("rows")
    core, pair = step % 2, step // 2
    side, part = depth % 2, depth // 2
    both_axes = ("step", "rows")
    block = land_mask.shape[0]
    px = 2 * block
    rows = px // COLS
    states = w_out.shape[0]
    forces = forcing.shape[2]
    channels = w_up.shape[1]
    hidden = w_up.shape[0]
    width = round_up(channels, LANES)
    ff_block = hidden // steps
    half = round_up(hidden // 2, LANES)
    wide = 2 * half
    spans = [(s * ff_block, ff_block, (s % 2) * half + (s // 2) * ff_block) for s in range(steps)]
    k_main = channels // CHUNK * CHUNK
    k_rem = channels - k_main
    col_block = channels // devices_z

    def place(s, z):
        return s * devices_z + z

    cells = [(k, c, h, q) for k in range(steps // 2) for c in range(2) for h in range(2) for q in range(2)]
    fetch_perms = [
        [(place(2 * k + q, 2 * c + (b ^ h)), place(2 * k + c, 2 * h + q)) for k, c, h, q in cells] for b in range(2)
    ]

    column_perm = [(place(2 * k + c, 2 * h + q), place(2 * k + q, 2 * c + h)) for k, c, h, q in cells]
    siblings = [(s, s ^ 1) for s in range(steps)]

    def to_sibling(values):
        return lax.ppermute(values, "step", siblings)

    def shift_back(values, j):
        return values if j == 0 else lax.ppermute(values, "step", [((s + j) % steps, s) for s in range(steps)])

    def fetch_own(values):
        got = [lax.ppermute(values, both_axes, perm) for perm in fetch_perms]
        return got

    def turn_round(values):
        n = values.shape[0]
        doubled = jnp.flip(jnp.concatenate([values, values]), axis=0)
        return lax.dynamic_slice_in_dim(doubled, n - 1 - step % n, n, axis=0)

    def rotate(values, by):
        return lax.dynamic_slice_in_dim(jnp.concatenate([values, values]), by, steps, axis=0)

    def from_later(values):
        if steps == ROLL:
            return rotate(lax.all_to_all(turn_round(values), "step", 0, 0, tiled=True), step)
        return jnp.stack([shift_back(values[j], j) for j in range(ROLL)])

    def to_later(values):
        if steps == ROLL:
            return turn_round(lax.all_to_all(rotate(values, (steps - step) % steps), "step", 0, 0, tiled=True))
        return jnp.stack([lax.ppermute(values[j], "step", [(s, (s + j) % steps) for s in range(steps)]) for j in range(ROLL)])

    at = jnp.stack([core, part, side, pair % 2, (pair // 2) % 2, pair, step % ROLL, history[0, 0]]).astype(jnp.int32)
    mask_row = land_mask.astype(F32)[None]
    current = init_states[0, 0, 1]
    previous = jnp.where(history[0, 0] == 2, init_states[0, 0, 0], current)
    payload = jnp.concatenate([previous, forcing[0, 0], current, mask_row], axis=0)
    timed = jnp.concatenate([cotangent[0, :, 0], jnp.broadcast_to(forcing[0], (ROLL,) + forcing.shape[2:])], axis=1)
    payload, timed = lax.optimization_barrier((payload, timed))
    payload = fetch_own(payload)
    timed = from_later(timed)

    def in_rows(values):
        top = jnp.concatenate([values[:states], values[2 * states :]], axis=0)
        bottom = values[states : 2 * states]
        return jnp.concatenate([jnp.pad(v, ((0, LANES - v.shape[0]), (0, 0))) for v in (top, bottom)], axis=0)

    def row(values, size):
        return jnp.pad(values, (0, size - values.shape[0]))[None]

    w_in_hi, w_in_lo = split_outside(pad_to(in_rows(w_in.T), (2 * LANES, width)))
    w_oi = pad_to(in_rows(jnp.dot(w_out, w_in, precision=HIGHEST).T), (2 * LANES, LANES))
    w_oi_hi, w_oi_lo = split_outside(w_oi)
    b_new = row(jnp.dot(w_out, b_in + b_down, precision=HIGHEST) + b_out, LANES)
    taps = jnp.broadcast_to(
        pad_to(w_dw.reshape(channels, KW * KW).T, (KW * KW, width))[:, None], (KW * KW, 8, width)
    )
    gain, bias = row(bn_gain, width), row(bn_bias, width)
    row_hi, row_lo = split_outside(pad_to(w_out, (SEG, channels)))
    out_parts = jnp.concatenate([row_hi, row_lo], axis=0)
    pieces = 5
    w_od_fwd, w_od_bwd = call(
        functools.partial(down_kernel, spans=spans), "down", (w_down, out_parts),
        [out(wide, 2 * LANES, dtype=BF16), out(2 * LANES, wide, dtype=BF16)],
        [pltpu.VMEM((channels, hidden), F32), pltpu.VMEM((SEG, hidden), F32), pltpu.VMEM((LANES, wide), F32), pltpu.SemaphoreType.DMA((pieces,))],
        20, micros=7, hbm=(0,), vmem_outs=(0, 1),
    )
    out_hi, out_lo = split_outside(pad_to(w_out, (SEG, width)))
    w_out_bwd = pad_to(jnp.concatenate([out_hi, out_hi, out_lo], axis=0), (2 * LANES, width))
    b_in_row = row(b_in, width)
    b_up_row = pad_to(b_up.reshape(steps // 2, 2, ff_block).swapaxes(0, 1).reshape(2, hidden // 2), (2, half)).reshape(1, wide)
    b_down_row = row(b_down, width)
    w_block = lax.dynamic_slice_in_dim(w_out, depth * col_block, col_block, axis=1).T
    w_block_hi, w_block_lo = split_outside(pad_to(w_block, (col_block, SEG)))
    prev, cur, ocean, first_sent = call(
        functools.partial(start_kernel, states=states, forces=forces), "start", (at, *payload),
        [out(px, LANES), out(px, LANES), out(px, LANES), out(block + 8, 3 * LANES)], [], 4, micros=1, smem=1,
    )
    first_came = to_sibling(first_sent)
    ready = lax.optimization_barrier(
        (w_up.T, timed, w_in_hi, w_in_lo, w_oi_hi, w_oi_lo, b_new, taps, gain, bias, w_out_bwd, b_in_row, b_up_row, b_down_row, w_block_hi, w_block_lo, at, first_sent)
    )
    up_source, timed, w_in_hi, w_in_lo, w_oi_hi, w_oi_lo, b_new, taps, gain, bias, w_out_bwd, b_in_row, b_up_row, b_down_row, w_block_hi, w_block_lo, at, first_sent = ready
    timed = fetch_own(timed)
    (w_up_all,) = call(
        functools.partial(up_kernel, k_main=k_main, k_rem=k_rem, spans=spans), "up", (up_source,),
        [out(2 * k_main + LANES, wide, dtype=BF16)],
        [pltpu.VMEM((3, k_main // 8, hidden), F32), pltpu.VMEM((k_main // 8, wide), F32), pltpu.SemaphoreType.DMA((3,))],
        10, micros=7, hbm=(0,), vmem_outs=(0,),
    )
    first_came, w_up_all = lax.optimization_barrier((first_came, w_up_all))
    force, force_send, cots = call(
        functools.partial(pack_kernel, states=states, forces=forces), "pack", (at, *timed),
        [out(ROLL, px, LANES), out(ROLL, block, LANES), out(ROLL, px, LANES)], [], 6, micros=2, smem=1,
    )
    force_edge = to_sibling(force_send)

    chunks = wide // CHUNK
    x_all, lifted_all, act_all, state_all = None, None, None, None
    kept = []
    prev_edge, cur_edge, prev_lanes, cur_lanes = first_came, first_came, 0, LANES
    for j in range(ROLL):
        mixed, stats, base, window, x_all, lifted_all = call(
            functools.partial(mix_kernel, turn=j, cur_lanes=cur_lanes, prev_lanes=prev_lanes), "mix",
            (at, cur, cur_edge, prev, prev_edge) + ((force, force_edge) if j else (at, at)) + (w_in_hi, w_in_lo, b_in_row, w_oi_hi, w_oi_lo, b_new, taps, ocean),
            [
                out(px, width), out(8, width), out(px, LANES), out(HALO + 2 * HALO, COLS, width), out(ROLL * block, 2 * LANES),
                out(ROLL * HALO, COLS, width),
            ],
            [
                pltpu.VMEM((rows + 2 * HALO, COLS + 16, width), F32),
                pltpu.VMEM((rows, COLS, width), F32), pltpu.VMEM((block, 2 * LANES), F32), pltpu.SemaphoreType.DMA((3,)),
            ],
            12, micros=4.5, smem=1, hbm_outs=(3,), stacked=((4, x_all), (5, lifted_all)),
        )
        stats_other = to_sibling(stats)
        new, new_edge, norm_edge, inv, norm, slope, act_all, state_all = call(
            functools.partial(feed_kernel, turn=j, width=width, k_main=k_main, k_rem=k_rem), "feed",
            (at, mixed, stats, stats_other, first_sent, first_came, gain, bias, ocean, base, w_up_all, b_up_row, w_od_fwd),
            [
                out(px, LANES), out(block, LANES), out(block, width), out(8, width), out(px, width),
                out(chunks, px, CHUNK), out(chunks, ROLL * block, CHUNK), out(ROLL, SEG, block),
            ],
            [
                pltpu.VMEM((2 * px, k_main), BF16), pltpu.VMEM((px, LANES), BF16),
                pltpu.VMEM((px, CHUNK), F32), pltpu.VMEM((px, LANES), F32), pltpu.VMEM((px, CHUNK), F32), pltpu.VMEM((px, CHUNK), F32),
                pltpu.VMEM((px, CHUNK), F32), pltpu.VMEM((px, width), F32), pltpu.VMEM((chunks, px, CHUNK), F32),
                pltpu.VMEM((chunks, block, CHUNK), F32), pltpu.VMEM((SEG, block), F32), pltpu.SemaphoreType.DMA((2 * chunks + 2,)),
            ],
            14, micros=8.5, smem=1, hbm_outs=(4, 5), stacked=((6, act_all), (7, state_all)),
        )
        prev, prev_edge, prev_lanes, cur = cur, cur_edge, cur_lanes, new
        if j < ROLL - 1:
            cur_edge, cur_lanes = to_sibling(new_edge), 0
        norm_edge = to_sibling(norm_edge)
        kept.append((window, norm, norm_edge, slope, inv))

    states_home = lax.ppermute(state_all, both_axes, column_perm)
    quarter = channels // 2
    acc_rows = round_up(quarter + 1, 8)
    tap_rows = round_up(KW * KW, 8)
    carry, pending = None, jnp.zeros((px, LANES), F32)
    previous_step, keep_acc, give_acc, sums, lift_all, masked_all = None, None, None, None, None, None
    homes = []
    begin_scratch = [
        pltpu.VMEM((px, LANES), F32), pltpu.VMEM((chunks, px, CHUNK), F32), pltpu.VMEM((block, LANES), F32),
        pltpu.VMEM((px, wide), F32), pltpu.SemaphoreType.DMA((3,)),
    ]
    finish_scratch = [
        pltpu.VMEM((rows + 2 * HALO, COLS + 16, width), F32), pltpu.VMEM((KW, rows + 2 * HALO, COLS, LANES), F32),
        pltpu.VMEM((rows, COLS, width), F32), pltpu.VMEM((px, width), F32), pltpu.SemaphoreType.DMA,
    ]
    for j in range(ROLL - 1, -2, -1):
        finish, begin = j < ROLL - 1, j >= 0
        if finish:
            pending, keep_acc, give_acc = lax.optimization_barrier((pending, keep_acc, give_acc))
        if j == ROLL - 4:
            pending, states_home = lax.optimization_barrier((pending, states_home))
        args, outs, scratch, stacked, hbm = [at, ocean, pending], [], [], [], ()
        if finish:
            window, norm, norm_edge, slope, inv = kept[j + 1]
            grad_n, sent, came, grad_branch = previous_step
            args += [grad_n, sent, came, norm, norm_edge, inv, gain, first_sent, first_came, grad_branch, window, taps, w_in_hi, w_in_lo]
            outs += [out(px, LANES), out(px, LANES), out(tap_rows, width), out(2 * LANES, block), out(ROLL * block, width)]
            stacked.append((4, lift_all))
            scratch += finish_scratch
        if begin:
            hbm = (len(args), len(args) + 1)
            args += [cots, kept[j][3], kept[j][1], w_out_bwd, w_od_bwd, w_up_all]
            outs += [out(px, width), out(2 * px, wide, dtype=BF16), out(px, width), out(block + 8, width), out(ROLL * block, LANES)]
            stacked.append((len(outs) - 1, masked_all))
            scratch += begin_scratch
        kernel = functools.partial(
            back_kernel, finish=finish, begin=begin, turn=j, width=width, k_main=k_main, k_rem=k_rem, states=states
        )
        results = list(
            call(kernel, "back", args, outs, scratch, 18, micros=7 * finish + 7.5 * begin, smem=1, hbm=hbm, stacked=stacked)
        )
        if finish:
            carry, pending, tap_sum, home, lift_all = results[:5]
            results = results[5:]
            homes.append(home)
        if begin:
            grad_branch, hidden_now, grad_n, sent, masked_all = results
            came = to_sibling(sent)
            previous_step = (grad_n, sent, came, grad_branch)
            keep_acc, give_acc, sums, *up_row = call(
                functools.partial(weight_kernel, quarter=quarter, finish=finish), "weight",
                (at, kept[j][1], gain, bias, hidden_now, sent) + ((tap_sum, keep_acc, give_acc, sums) if finish else ()),
                [out(acc_rows, half), out(acc_rows, half), out(tap_rows + 8, width)] + ([] if j else [out(8, wide)]), [], 8, micros=5, smem=1,
                aliases=({7: 0, 8: 1, 9: 2} if j else {7: 0, 9: 2}) if finish else None, vmem_outs=(0, 1, 2) if j else (),
            )
            if j == 0:
                window, norm, norm_edge, slope, inv = kept[0]
                give_acc, came, norm_edge = lax.optimization_barrier((give_acc, came, norm_edge))
                kept[0] = (window, norm, norm_edge, slope, inv)
                previous_step = (grad_n, sent, came, grad_branch)

    def trade(values, axis, flip):
        return lax.ppermute(values, axis, [(i, i ^ flip) for i in range(lax.axis_size(axis))])

    def pick(first, second, bit):
        return jnp.where(bit == 0, first, second), jnp.where(bit == 0, second, first)

    token = [tap_sum]

    def local(kernel, args, outs, limit=8, **options):
        def body(at_ref, *refs):
            kernel(at_ref, *refs[: len(args)], *refs[len(args) + 1 : -1], **options)
            refs[-1][...] = refs[len(args)][:8, :LANES]

        results = call(body, kernel.__name__, (at, *args, token[0]), outs + [out(8, LANES)], [], limit, micros=1, smem=1)
        token[0] = results[-1]
        return results[:-1]

    direct = steps == 8 and devices_z == 4
    home_outs = [out(ROLL, states, block), out(8, block), out(2, states, block)]
    got = trade(give_acc, "step", 1)
    if direct:
        pieces = [out(2, col_block, ff_block)] * 4
        keep_a, give_a, keep_b, give_b = local(cut_first_kernel, (keep_acc, got), pieces, 16, rows=col_block, cols=ff_block)
        got_a, got_b = trade(give_a, "step", 2), trade(give_b, "step", 4)
    part_px = ROLL * block
    blocks = [(start, min(CHUNK, channels - start)) for start in range(0, channels, CHUNK)]
    table_keep, table_give, hidden_keep, hidden_give = call(
        functools.partial(last_kernel, spans=spans, blocks=blocks), "last",
        (
            at, masked_all, x_all, lift_all, lifted_all, act_all, w_down, b_down_row, sums,
            tap_sum, *up_row, token[0],
        ),
        [out(160, width), out(160, width), out(SEG, half), out(SEG, half)],
        [
            pltpu.VMEM((320, width), F32),
            pltpu.VMEM((part_px, LANES), F32), pltpu.VMEM((part_px, 2 * LANES), F32), pltpu.VMEM((part_px, width), F32),
            pltpu.VMEM(lifted_all.shape, F32), pltpu.VMEM((chunks, part_px, CHUNK), F32), pltpu.VMEM((channels, hidden), F32),
            pltpu.VMEM((2 * SEG, part_px), BF16), pltpu.VMEM((2, 2 * LANES, part_px), BF16), pltpu.VMEM((SEG, wide), F32),
            pltpu.VMEM((SEG, hidden), F32), pltpu.VMEM((2 * SEG, hidden), BF16),
            pltpu.SemaphoreType.DMA((4 + len(blocks) + chunks,)),
        ],
        44, micros=12, smem=1, hbm=(1, 2, 3, 4, 5, 6),
    )
    other = trade(table_give, "step", 1)
    hidden_other = trade(hidden_give, "step", 1)
    if direct:
        fours = (1, 2, 3)
        token[0] = table_keep
        keep_a, give_a, keep_b, give_b = local(cut_second_kernel, (keep_a, got_a, keep_b, got_b), [out(col_block, ff_block)] * 4)
        got_a, got_b = trade(give_a, "step", 4), trade(give_b, "step", 2)
        own = local(quarter_rows_kernel, (table_keep, other), [out(40, width)] * 4)
        from_xy = [trade(own[b], "step", 2 * b) for b in fours]
        h_own = local(quarter_cols_kernel, (hidden_keep, hidden_other), [out(SEG, ff_block)] * 4)
        h_xy = [trade(h_own[b], "step", 2 * b) for b in fours]
        (ending,) = local(going_kernel, homes[::-1], [out(8 * ROLL + 160, block)], states=states, forces=forces)
        ending = lax.ppermute(ending, both_axes, column_perm)
        (piece,) = local(sum_four_kernel, (own[0], *from_xy), [out(40, width)])
        near = trade(piece, "rows", 1)
        (h_piece,) = local(sum_four_kernel, (h_own[0], *h_xy), [out(SEG, ff_block)])
        h_near = trade(h_piece, "rows", 1)
        (piece,) = local(sum_two_kernel, (piece, near), [out(40, width)])
        far = trade(piece, "rows", 2)
        (h_piece,) = local(sum_two_kernel, (h_piece, h_near), [out(SEG, ff_block)])
        h_far = trade(h_piece, "rows", 2)
        keep, give = local(cut_third_kernel, (keep_a, got_a, keep_b, got_b), [out(col_block, ff_block)] * 2)
        got = trade(give, "rows", 1)
        (rolled,) = local(roll_kernel, (states_home, ending), [out(ROLL, 88, block)])
        gone = lax.all_to_all(rolled, "step", 0, 0, tiled=True)
        (piece,) = local(sum_two_kernel, (piece, far), [out(40, width)])
        from_xy = [trade(piece, "step", 2 * b) for b in fours]
        (share_down,) = local(share_down_kernel, (h_piece, h_far, w_block_hi, w_block_lo), [out(col_block, ff_block)])
        (share_up,) = local(turn_sum_kernel, (keep, got), [out(ff_block, col_block)])
        predicted, grad_forcing, grad_init = local(home_kernel, (gone, ending), home_outs, states=states)
        (mine,) = local(join_rows_kernel, (piece, *from_xy), [out(160, width)])
        other = trade(mine, "step", 1)
    else:
        units = steps // 2
        same_core = [[2 * k + c for k in range(units)] for c in range(2)]
        mine_up = keep_acc + got
        share = lax.psum_scatter(mine_up[:, : hidden // 2], "step", scatter_dimension=1, axis_index_groups=same_core, tiled=True)
        keep, give = pick(share[:col_block], share[col_block : 2 * col_block], side)
        share_up = (keep + trade(give, "rows", 1)).T
        mine_down = hidden_keep + hidden_other
        hidden_share = lax.psum(
            lax.psum_scatter(mine_down[:, : hidden // 2], "step", scatter_dimension=1, axis_index_groups=same_core, tiled=True), "rows"
        )
        nothing = jnp.zeros_like(hidden_share)
        (share_down,) = local(share_down_kernel, (hidden_share, nothing, w_block_hi, w_block_lo), [out(col_block, ff_block)])
        mine, other = pick(*[lax.psum(v, both_axes) for v in pick(table_keep, table_give, core)], core)
        (ending,) = local(going_kernel, homes[::-1], [out(8 * ROLL + 160, block)], states=states, forces=forces)
        ending = lax.ppermute(ending, both_axes, column_perm)
        gone = turn_round(to_later(jnp.concatenate([states_home, ending[: 8 * ROLL].reshape(ROLL, 8, block)], axis=1)))
        predicted, grad_forcing, grad_init = local(home_kernel, (gone, ending), home_outs, states=states)
    g_in, g_dw, g_w_out, lines = local(
        table_kernel, (mine, other),
        [out(2 * states + forces, channels), out(KW, KW, channels), out(states, channels), out(16, width)], states=states, forces=forces,
    )
    g_bias, g_gain, g_b_in = lines[0, :channels], lines[1, :channels], lines[7, :channels]
    g_b_up = lines[8:12].reshape(-1)[:wide].reshape(2, half)[:, : hidden // 2].reshape(2, steps // 2, ff_block).swapaxes(0, 1).reshape(-1)
    g_b_out = lines[12, :states]
    g_b_down = jnp.sum(w_out * g_b_out[:, None], axis=0)
    return (
        predicted[None, :, None],
        grad_init[None, None],
        grad_forcing[None, None, :forces],
        g_in.T,
        g_b_in,
        g_dw.transpose(2, 0, 1),
        g_gain,
        g_bias,
        share_up,
        g_b_up,
        share_down,
        g_b_down,
        g_w_out,
        g_b_out,
    )


def solution(mesh):
    state_spec = P("step", None, None, None, "rows")
    force_spec = P("step", None, None, "rows")
    in_specs = (state_spec, force_spec, P("step", None), P("rows")) + (P(),) * 11 + (state_spec,)
    out_specs = (state_spec, state_spec, force_spec) + (P(),) * 5 + (P("step", "rows"), P(), P("rows", "step"), P(), P(), P())
    return jax.shard_map(per_device, mesh=mesh, in_specs=in_specs, out_specs=out_specs, check_vma=False)
```

```python
import functools

import jax
import jax.numpy as jnp
from jax import lax
from jax.experimental import pallas as pl
from jax.experimental.pallas import tpu as pltpu
from jax.sharding import PartitionSpec as P

F32 = jnp.float32
BF16 = jnp.bfloat16
HIGHEST = lax.Precision.HIGHEST
ROLL = 8
COLS = 32
KW = 7
HALO = 3
EPSILON = 1e-05
LANES = 128
CHUNK = 256
SEG = 80
MIB = 2**20

ERF_P = 0.39
ERF_C = (0.23532534, 0.09138764, 0.64956134, -0.63540268, 0.88666585, -0.22753749)


def round_up(value, multiple):
    return -(-value // multiple) * multiple


def split(values):
    high = values.astype(BF16)
    return high, (values - high.astype(F32)).astype(BF16)


def split_outside(values):
    rounded = lax.reduce_precision(values, 8, 7)
    return rounded.astype(BF16), (values - rounded).astype(BF16)


def dot(left, right):
    return jnp.dot(left, right, preferred_element_type=F32)


def dot_t(left, right):
    return lax.dot_general(left, right, (((1,), (1,)), ((), ())), preferred_element_type=F32)


def gelu_both(v):
    e = jnp.exp(v * v * (-0.5))
    t = 1.0 / (1.0 + (ERF_P * 0.7071067811865476) * jnp.abs(v))
    q = 0.5 * ERF_C[5]
    for coefficient in ERF_C[4::-1]:
        q = q * t + 0.5 * coefficient
    q = (q * t) * e
    phi = jnp.where(v >= 0.0, 1.0 - q, q)
    return v * phi, phi + v * (e * 0.3989422804014327)


def depthwise(ext, shifted, kernel, mixed, lanes, flip, rows):
    rows_in = rows + 2 * HALO
    for q in range(KW):
        for r in range(rows_in):
            shifted[q, r] = ext[r, 5 + q : 5 + q + COLS, lanes]
    for v in range(0, COLS, 8):
        total = [None] * rows
        for q in range(KW):
            taps = [
                kernel[(KW * KW - 1 - (p * KW + q)) if flip else (p * KW + q), :, lanes]
                for p in range(KW)
            ]
            for r in range(rows_in):
                cell = shifted[q, r, v : v + 8, :]
                for p in range(KW):
                    i = r - p
                    if 0 <= i < rows:
                        term = taps[p] * cell
                        total[i] = term if total[i] is None else total[i] + term
        for i in range(rows):
            mixed[i, v : v + 8, lanes] = total[i]


def depthwise_direct(ext, kernel, mixed, lanes, rows):
    tiles = range(0, COLS, 8)
    total = [[None] * len(tiles) for _ in range(rows)]
    for q in range(KW):
        taps = [kernel[p * KW + q, :, lanes] for p in range(KW)]
        for r in range(rows + 2 * HALO):
            cells = ext[r, 5 + q : 5 + q + COLS, lanes]
            for t, v in enumerate(tiles):
                cell = cells[v : v + 8]
                for p in range(KW):
                    i = r - p
                    if 0 <= i < rows:
                        term = taps[p] * cell
                        total[i][t] = term if total[i][t] is None else total[i][t] + term
    for i in range(rows):
        for t, v in enumerate(tiles):
            mixed[i, v : v + 8, lanes] = total[i][t]


def ocean_count(sent, came):
    last = sent.shape[0] - 1
    return jnp.maximum(sent[last:, :LANES] + came[last:, :LANES], 1.0)


def group_lanes(group):
    return pl.ds(pl.multiple_of(group * LANES, LANES), LANES)


def mix_kernel(
    at, cur, cur_edge, prev, prev_edge, force, force_edge, w_in_hi, w_in_lo, b_in, b_new, taps, ocean,
    mixed_out, stats_out, base_out, window_out, x_all, lifted_all,
    ext, mixed, x_part, sems, *, turn, cur_lanes, prev_lanes,
):
    core, part = at[0], at[1]
    px = cur.shape[0]
    edge_px = x_part.shape[0]
    rows = px // COLS
    width = mixed_out.shape[1]
    prev_now, prev_edge_now = prev[...], prev_edge[:edge_px, prev_lanes : prev_lanes + LANES]
    if turn:
        prev_now, prev_edge_now = prev_now + force[turn], prev_edge_now + force_edge[turn]
    own = jnp.concatenate([prev_now, cur[...]], axis=1)
    edge = jnp.concatenate([prev_edge_now, cur_edge[:edge_px, cur_lanes : cur_lanes + LANES]], axis=1)
    own_hi, own_lo = split(own)
    edge_hi, edge_lo = split(edge)
    both = dot(jnp.concatenate([own_hi, edge_hi, own_lo, edge_lo], axis=0), w_in_hi[...])
    high = dot(jnp.concatenate([own_hi, edge_hi], axis=0), w_in_lo[...])
    both = (both[: px + edge_px] + both[px + edge_px :]) + high
    lifted = both[:, :width] + b_in[...]
    base_out[...] = both[:px, width:] + b_new[...]
    zeros = jnp.zeros((rows + 2 * HALO, 8, width), F32)
    ext[:, :8, :] = zeros
    ext[:, 8 + COLS :, :] = zeros
    ext[HALO : HALO + rows, 8 : 8 + COLS, :] = lifted[:px].reshape(rows, COLS, width)
    ext[pl.ds((rows + HALO) * (1 - core), HALO), 8 : 8 + COLS, :] = lifted[px:].reshape(HALO, COLS, width)
    ext[pl.ds((rows + HALO) * core, HALO), 8 : 8 + COLS, :] = jnp.zeros((HALO, COLS, width), F32)
    part_rows = window_out.shape[0] - 2 * HALO
    part_px = x_part.shape[0]
    x_part[...] = jnp.where(part == 0, own[:part_px], own[part_px:])
    here = pl.ds(turn * part_rows, part_rows)
    keeps = [
        pltpu.make_async_copy(ext.at[pl.ds(part * part_rows, window_out.shape[0]), 8 : 8 + COLS, :], window_out, sems.at[0]),
        pltpu.make_async_copy(ext.at[pl.ds(part * part_rows + HALO, part_rows), 8 : 8 + COLS, :], lifted_all.at[here], sems.at[1]),
        pltpu.make_async_copy(x_part, x_all.at[pl.ds(turn * part_px, part_px)], sems.at[2]),
    ]
    for keep in keeps:
        keep.start()
    mask = ocean[...]

    def group(g, _):
        lanes = group_lanes(g)
        depthwise_direct(ext, taps, mixed, lanes, rows)
        cells = mixed[:, :, lanes].reshape(px, LANES)
        mixed_out[:, lanes] = cells
        masked = cells * mask
        stats_out[0:1, lanes] = jnp.sum(masked, axis=0, keepdims=True)
        stats_out[1:2, lanes] = jnp.sum(masked * cells, axis=0, keepdims=True)
        return 0

    lax.fori_loop(0, width // LANES, group, 0)
    for keep in keeps:
        keep.wait()


def feed_kernel(
    at, mixed, stats, stats_other, sent, came, gain, bias, ocean, base, w_up, b_up, w_od,
    new_out, new_edge_out, norm_edge_out, inv_out, norm_out, slope_out, act_all, state_all,
    stack, rem, acc, acc_lo, hold_a, hold_b, hold_act, norm, slope, act_part, state, sems, *, turn, width, k_main, k_rem,
):
    core, part = at[0], at[1]
    px = mixed.shape[0]
    chunks = w_up.shape[1] // CHUNK
    part_px = act_part.shape[1]
    total = ocean_count(sent, came)
    keep_norm = pltpu.make_async_copy(norm, norm_out, sems.at[2 * chunks])

    for g in range(width // LANES):
        lanes = slice(g * LANES, (g + 1) * LANES)
        cells = mixed[:, lanes]
        average = (stats[0:1, lanes] + stats_other[0:1, lanes]) / total
        variance = (stats[1:2, lanes] + stats_other[1:2, lanes]) / total - average * average
        inverse = lax.rsqrt(variance + EPSILON)
        inv_out[:, lanes] = jnp.broadcast_to(inverse, (8, LANES))
        normalized = (cells - average) * inverse
        norm[:, lanes] = normalized
        normed = normalized * gain[:, lanes] + bias[:, lanes]
        high = normed.astype(BF16)
        high_f = high.astype(F32)
        low_f = normed - high_f
        if (g + 1) * LANES <= k_main:
            stack[:px, lanes] = high
            stack[px:, lanes] = low_f.astype(BF16)
        else:
            rem[...] = (high_f + pltpu.roll(low_f, k_rem, 1) + pltpu.roll(high_f, 2 * k_rem, 1)).astype(BF16)
    keep_norm.start()
    edge_px = norm_edge_out.shape[0]
    norm_edge_out[...] = norm[pl.ds(pl.multiple_of((1 - core) * (px - edge_px), 8), edge_px), :]

    def up(t, hold):
        cols = pl.ds(pl.multiple_of(t * CHUNK, CHUNK), CHUNK)
        both = dot(stack[...], w_up[:k_main, cols])
        high = dot(stack[:px], w_up[k_main : 2 * k_main, cols])
        rest = dot(rem[...], w_up[2 * k_main :, cols])
        hold[...] = (both[:px] + both[px:]) + (high + rest)

    def keep_slope(t):
        return pltpu.make_async_copy(slope.at[t], slope_out.at[t], sems.at[t])

    def keep_act(t):
        return pltpu.make_async_copy(act_part.at[t], act_all.at[t, pl.ds(turn * part_px, part_px)], sems.at[chunks + t])

    def act(t, hold):
        cols = pl.ds(pl.multiple_of(t * CHUNK, CHUNK), CHUNK)
        activated, slope[t] = gelu_both(hold[...] + b_up[:, cols])
        hold_act[...] = activated
        high, low = split(activated)
        acc[...] += dot(high, w_od[cols, :])
        acc_lo[...] += dot(low, w_od[cols, :LANES])
        act_part[t] = hold_act[pl.ds(pl.multiple_of(part * part_px, 8), part_px), :]
        keep_slope(t).start()
        keep_act(t).start()

    acc[...] = jnp.zeros_like(acc)
    acc_lo[...] = base[...]
    up(0, hold_a)

    def pair(i, _):
        up(2 * i + 1, hold_b)
        act(2 * i, hold_a)
        up(2 * i + 2, hold_a)
        act(2 * i + 1, hold_b)
        return 0

    for i in range(chunks // 2):
        pair(i, 0)
    act(chunks - 1, hold_a)
    new = (acc[:, :LANES] + acc[:, LANES:] + acc_lo[...]) * ocean[...]
    new_out[...] = new
    new_edge_out[...] = new_out[pl.ds(pl.multiple_of((1 - core) * (px - edge_px), 8), edge_px), :]
    mine = jnp.where(part == 0, new[:part_px], new[part_px:])
    state[...] = mine.T[: state.shape[0]]
    keep_state = pltpu.make_async_copy(state, state_all.at[turn], sems.at[2 * chunks + 1])
    keep_state.start()
    keep_norm.wait()
    keep_state.wait()
    for t in range(chunks):
        keep_slope(t).wait()
        keep_act(t).wait()


def back_kernel(*refs, finish, begin, turn, width, k_main, k_rem, states):
    refs = list(refs)

    def take(count):
        out = refs[:count]
        del refs[:count]
        return out

    (at, ocean, pending_in) = take(3)
    if finish:
        (grad_n, sent, came, norm, norm_edge, inv, gain, first_sent, first_came, grad_branch, window, taps, w_in_hi, w_in_lo) = take(14)
    if begin:
        (cots, slope_hbm, norm_now, w_out, w_od, w_up) = take(6)
    if finish:
        (carry_out, pending_out, taps_out, home_out, lift_all) = take(5)
    if begin:
        (branch_out, hidden_out, grad_n_out, send_out, masked_all) = take(5)
    if finish:
        (ext, shifted, mixed, grad_lift, lift_sem) = take(5)
    if begin:
        (cot, slope, masked_part, pulled, begin_sems) = take(5)
    core, part = at[0], at[1]
    px = ocean.shape[0]
    rows = px // COLS
    part_px = px // 2
    if begin:
        get_cot = pltpu.make_async_copy(cots.at[turn], cot, begin_sems.at[0])
        get_slope = pltpu.make_async_copy(slope_hbm, slope, begin_sems.at[1])
        get_cot.start()
        get_slope.start()
    if finish:
        edge_px = norm_edge.shape[0]
        total = ocean_count(first_sent, first_came)
        ocean_edge = first_came[:edge_px, 2 * LANES :]
        zeros = jnp.zeros((rows + 2 * HALO, 8, width), F32)
        ext[:, :8, :] = zeros
        ext[:, 8 + COLS :, :] = zeros
        ext[pl.ds((rows + HALO) * core, HALO), 8 : 8 + COLS, :] = jnp.zeros((HALO, COLS, width), F32)
        part_rows = window.shape[0] - 2 * HALO
        for g in range(width // LANES):
            lanes = slice(g * LANES, (g + 1) * LANES)
            bias_sum = (sent[edge_px : edge_px + 1, lanes] + came[edge_px : edge_px + 1, lanes]) / total
            gain_sum = (sent[edge_px + 1 : edge_px + 2, lanes] + came[edge_px + 1 : edge_px + 2, lanes]) / total
            scale = inv[0:1, lanes] * gain[:, lanes]
            mix = scale * (grad_n[:, lanes] - ocean[...] * (bias_sum + norm[:, lanes] * gain_sum))
            mix_edge = scale * (came[:edge_px, lanes] - ocean_edge * (bias_sum + norm_edge[:, lanes] * gain_sum))
            ext[HALO : HALO + rows, 8 : 8 + COLS, lanes] = mix.reshape(rows, COLS, LANES)
            ext[pl.ds((rows + HALO) * (1 - core), HALO), 8 : 8 + COLS, lanes] = mix_edge.reshape(HALO, COLS, LANES)

        def group(g, _):
            lanes = group_lanes(g)
            depthwise(ext, shifted, taps, mixed, lanes, True, rows)
            grad_lift[:, lanes] = mixed[:, :, lanes].reshape(px, LANES) + grad_branch[:, lanes]
            for q in range(KW):
                sums = [None] * KW
                for i in range(part_rows):
                    for v in range(0, COLS, 8):
                        grad = shifted[KW - 1 - q, HALO + part * part_rows + i, v : v + 8, :]
                        for p in range(KW):
                            term = grad * window[i + p, v : v + 8, lanes]
                            sums[p] = term if sums[p] is None else sums[p] + term
                for p in range(KW):
                    taps_out[p * KW + q : p * KW + q + 1, lanes] = jnp.sum(sums[p], axis=0, keepdims=True)
            return 0

        lax.fori_loop(0, width // LANES, group, 0)
        keep_lift = pltpu.make_async_copy(
            grad_lift.at[pl.ds(pl.multiple_of(part * part_px, 8), part_px)], lift_all.at[pl.ds((turn + 1) * part_px, part_px)], lift_sem
        )
        keep_lift.start()
        high, low = split(grad_lift[...])
        both = dot_t(jnp.concatenate([high, low], axis=0), w_in_hi[:, :width])
        grad_x = (both[:px] + both[px:]) + dot_t(high, w_in_lo[:, :width])
        carry = grad_x[:, LANES:] + pending_in[...]
        carry_out[...] = carry
        pending_out[...] = grad_x[:, :LANES]
        part_x = jnp.where(part == 0, grad_x[:part_px, :LANES], grad_x[part_px:, :LANES])
        part_c = jnp.where(part == 0, carry[:part_px], carry[part_px:])
        home_out[:LANES] = part_x.T
        home_out[LANES:] = part_c.T
    if begin:
        get_cot.wait()
        grad_new = cot[...] + carry if finish else cot[...]
        lane = lax.broadcasted_iota(jnp.int32, (px, LANES), 1)
        masked = jnp.where(lane < states, grad_new * ocean[...], 0.0)
        masked_part[...] = jnp.where(part == 0, masked[:part_px], masked[part_px:])
        keep_masked = pltpu.make_async_copy(masked_part, masked_all.at[pl.ds(turn * part_px, part_px)], begin_sems.at[2])
        keep_masked.start()
        high_f = masked.astype(BF16).astype(F32)
        nothing = jnp.zeros((px, LANES), F32)
        high_w = jnp.concatenate([high_f, nothing], axis=1)
        low_w = jnp.concatenate([masked - high_f, nothing], axis=1)
        left = (high_w + pltpu.roll(low_w, SEG, 1) + pltpu.roll(high_w, 2 * SEG, 1)).astype(BF16)
        branch_out[...] = dot(left, w_out[...])
        chunks = w_od.shape[1] // CHUNK
        get_slope.wait()

        half = w_od.shape[1] // 2

        def pull(t, _):
            cols = pl.ds(pl.multiple_of(t * half, half), half)
            pulled[:, cols] = dot(left, w_od[:, cols])
            return 0

        pull(0, 0)
        pull(1, 0)

        def chunk(t, _):
            cols = pl.ds(pl.multiple_of(t * CHUNK, CHUNK), CHUNK)
            high, low = split(pulled[:, cols] * slope[t])
            hidden_out[:px, cols] = high
            hidden_out[px:, cols] = low
            return 0

        for t in range(chunks):
            chunk(t, 0)
        both = dot_t(hidden_out[...], w_up[:k_main])
        grad_n_out[:, :k_main] = (both[:px] + both[px:]) + dot_t(hidden_out[:px], w_up[k_main : 2 * k_main])
        rest = dot_t(hidden_out[...], w_up[2 * k_main :])
        tail = rest[:px] + rest[px:] + pltpu.roll(rest[:px], LANES - 2 * k_rem, 1)
        grad_n_out[:, k_main:] = jnp.where(lane < k_rem, tail, 0.0)
        edge_px = send_out.shape[0] - 8
        for g in range(width // LANES):
            lanes = slice(g * LANES, (g + 1) * LANES)
            cells = grad_n_out[:, lanes]
            send_out[edge_px : edge_px + 1, lanes] = jnp.sum(cells, axis=0, keepdims=True)
            send_out[edge_px + 1 : edge_px + 2, lanes] = jnp.sum(cells * norm_now[:, lanes], axis=0, keepdims=True)
        send_out[edge_px + 2 :, :] = jnp.zeros((6, width), F32)
        send_out[:edge_px, :] = grad_n_out[pl.ds(pl.multiple_of((1 - core) * (px - edge_px), 8), edge_px), :]
        keep_masked.wait()
    if finish:
        keep_lift.wait()


def weight_kernel(at, norm, gain, bias, hidden, send, *rest, quarter, finish):
    if finish:
        taps, keep_in, give_in, sums_in, keep_out, give_out, sums_out, *up_row = rest
    else:
        keep_out, give_out, sums_out, *up_row = rest
    core = at[0]
    part = at[1]
    px = norm.shape[0]
    tap_rows = sums_out.shape[0] - 8
    if finish:
        sums_out[:tap_rows] = sums_in[:tap_rows] + taps[...]
        sums_out[tap_rows:] = sums_in[tap_rows:] + send[send.shape[0] - 8 :]
    else:
        sums_out[:tap_rows] = jnp.zeros((tap_rows, sums_out.shape[1]), F32)
        sums_out[tap_rows:] = send[send.shape[0] - 8 :]
    window = round_up(quarter, LANES)
    base = (quarter // LANES) * LANES
    normed = norm[...] * gain[...] + bias[...]
    second = pltpu.roll(normed[:, base : base + window], window - (quarter - base), 1)
    mine = jnp.where(part == 0, normed[:, :window], second)
    lane = lax.broadcasted_iota(jnp.int32, (px, window), 1)
    mine = jnp.where(lane < quarter, mine, jnp.where(lane == quarter, 1.0, 0.0))
    high, low = split(mine.T[: keep_out.shape[0]])
    half = keep_out.shape[1]

    for side, acc_out in enumerate((keep_out, give_out)):
        actual = core if side == 0 else 1 - core
        cols = pl.ds(pl.multiple_of(actual * half, LANES), half)
        new = dot(high, hidden[:px, cols]) + dot(high, hidden[px:, cols]) + dot(low, hidden[:px, cols])
        acc_out[...] = (keep_in, give_in)[side][...] + new if finish else new
    if up_row:
        line = quarter // 8 * 8
        for side, acc_out in ((core, keep_out), (1 - core, give_out)):
            up_row[0][:, pl.ds(pl.multiple_of(side * half, LANES), half)] = acc_out[line : line + 8, :]


VMEM_SPEC = pl.BlockSpec(memory_space=pltpu.VMEM)
SMEM_SPEC = pl.BlockSpec(memory_space=pltpu.SMEM)
HBM_SPEC = pl.BlockSpec(memory_space=pltpu.HBM)


def out(*shape, dtype=F32):
    return jax.ShapeDtypeStruct(shape, dtype)


def in_hbm(values):
    return pltpu.with_memory_space_constraint(values, pltpu.HBM)


def call(kernel, name, args, outs, scratch, limit, *, micros, smem=0, hbm=(), hbm_outs=(), vmem_outs=(), aliases=None, stacked=()):
    args = [in_hbm(a) if i in hbm else a for i, a in enumerate(args)]
    specs = [SMEM_SPEC if i < smem else HBM_SPEC if i in hbm else VMEM_SPEC for i in range(len(args))]
    hbm_outs = tuple(hbm_outs) + tuple(i for i, _ in stacked)
    aliases = dict(aliases or {})
    used = len(args)
    for i, buffer in stacked:
        if buffer is not None:
            aliases[len(args)] = i
            args.append(in_hbm(buffer))
            specs.append(HBM_SPEC)
    extra = len(args) - used

    def body(*refs):
        kernel(*refs[:used], *refs[used + extra :])

    return pl.pallas_call(
        body,
        in_specs=specs,
        out_specs=[HBM_SPEC if i in hbm_outs else VMEM_SPEC for i in range(len(outs))],
        out_shape=[
            pltpu.HBM(o.shape, o.dtype) if i in hbm_outs else pltpu.VMEM(o.shape, o.dtype) if i in vmem_outs else o
            for i, o in enumerate(outs)
        ],
        scratch_shapes=scratch,
        input_output_aliases=aliases,
        compiler_params=pltpu.CompilerParams(vmem_limit_bytes=limit * MIB),
        cost_estimate=pl.CostEstimate(flops=int(micros * 1.1e9), bytes_accessed=1024, transcendentals=0),
        name=name,
    )(*args)


def start_kernel(at, first, second, prev_out, cur_out, ocean_out, send_out, *, states, forces):
    core, part = at[0], at[1]
    block = first.shape[1]
    rows = first.shape[0]
    mask_row = 2 * states + forces

    def turn(values):
        prev = jnp.concatenate([values[: states + forces], jnp.zeros((LANES - states - forces, block), F32)], axis=0).T
        cur = jnp.concatenate([values[states + forces : mask_row], jnp.zeros((LANES - states, block), F32)], axis=0).T
        mask = jnp.broadcast_to(values[mask_row : mask_row + 1], (LANES, block)).T
        return prev, cur, mask

    zero, one = first[...], second[...]
    swap = part == 1
    top, low = jnp.where(swap, one, zero), jnp.where(swap, zero, one)
    count = jnp.sum(top[mask_row : mask_row + 1]) + jnp.sum(low[mask_row : mask_row + 1])
    for i, values in enumerate((top, low)):
        prev, cur, mask = turn(values)
        here = slice(i * block, (i + 1) * block)
        prev_out[here] = prev
        cur_out[here] = cur
        ocean_out[here] = mask
    at_edge = pl.ds(pl.multiple_of((1 - core) * block, 8), block)
    send_out[:block, :LANES] = prev_out[at_edge, :]
    send_out[:block, LANES : 2 * LANES] = cur_out[at_edge, :]
    send_out[:block, 2 * LANES :] = ocean_out[at_edge, :]
    send_out[block:] = jnp.full((8, 3 * LANES), count)


def pack_kernel(at, first, second, force_out, force_send, cot_out, *, states, forces):
    core, part = at[0], at[1]
    steps, rows, block = first.shape
    lane = lax.broadcasted_iota(jnp.int32, (block, LANES), 1)
    for j in range(steps):
        turned = [
            jnp.concatenate([values[j], jnp.zeros((LANES - rows, block), F32)], axis=0).T for values in (first, second)
        ]
        top, low = jnp.where(part == 1, turned[1], turned[0]), jnp.where(part == 1, turned[0], turned[1])
        for i, values in enumerate((top, low)):
            cot_out[j, i * block : (i + 1) * block] = jnp.where(lane < states, values, 0.0)
            force_out[j, i * block : (i + 1) * block] = jnp.where(lane < states, 0.0, values)
        force_send[j] = force_out[j, pl.ds(pl.multiple_of((1 - core) * block, 8), block), :]


def reorder(source, target, spans):
    for start, size, place in spans:
        target[:, place : place + size] = source[:, start : start + size]


def up_kernel(w_up_t, up_all, raw, turned, sems, *, k_main, k_rem, spans):
    slots, block = raw.shape[0], raw.shape[1]
    blocks = k_main // block

    def get(t, size):
        slot = lax.rem(t, slots)
        return pltpu.make_async_copy(
            w_up_t.at[pl.ds(pl.multiple_of(t * block, 8), size)], raw.at[slot, pl.ds(0, size)], sems.at[slot]
        )

    for t in range(slots):
        get(t, block).start()
    turned[...] = jnp.zeros_like(turned)

    def main(t, _):
        get(t, block).wait()
        reorder(raw.at[lax.rem(t, slots)], turned, spans)

        @pl.when(t + slots < blocks)
        def _():
            get(t + slots, block).start()

        @pl.when(t + slots == blocks)
        def _():
            get(t + slots, k_rem).start()

        high, low = split(turned[...])
        up_all[pl.ds(pl.multiple_of(t * block, block), block), :] = high
        up_all[pl.ds(pl.multiple_of(k_main + t * block, block), block), :] = low
        return 0

    lax.fori_loop(0, blocks, main, 0)
    get(blocks, k_rem).wait()
    reorder(raw.at[blocks % slots, pl.ds(0, k_rem)], turned.at[pl.ds(0, k_rem)], spans)
    high, low = split(turned[:k_rem])
    base = 2 * k_main
    up_all[base : base + k_rem] = high
    up_all[base + k_rem : base + 2 * k_rem] = high
    up_all[base + 2 * k_rem : base + 3 * k_rem] = low
    up_all[base + 3 * k_rem :] = jnp.zeros((LANES - 3 * k_rem, up_all.shape[1]), BF16)


def down_kernel(w_down, out_parts, od_fwd, od_bwd, down, product, ordered, sems, *, spans):
    pieces = sems.shape[0]
    piece = down.shape[1] // pieces

    def get(t):
        cols = pl.ds(pl.multiple_of(t * piece, LANES), piece)
        return pltpu.make_async_copy(w_down.at[:, cols], down.at[:, cols], sems.at[t])

    for t in range(pieces):
        get(t).start()
    ordered[...] = jnp.zeros_like(ordered)

    def multiply(t, _):
        cols = pl.ds(pl.multiple_of(t * piece, LANES), piece)
        get(t).wait()
        high, low = split(down[:, cols])
        both = dot(out_parts[...], high)
        product[:, cols] = (both[:SEG] + both[SEG:]) + dot(out_parts[:SEG], low)
        return 0

    lax.fori_loop(0, pieces, multiply, 0)
    reorder(product, ordered.at[pl.ds(0, SEG)], spans)

    def spread(t, _):
        cols = pl.ds(pl.multiple_of(t * CHUNK, CHUNK), CHUNK)
        values = ordered[:, cols]
        high, low = split(values)
        od_bwd[:SEG, cols] = high[:SEG]
        od_bwd[SEG : 2 * SEG, cols] = high[:SEG]
        od_bwd[2 * SEG : 3 * SEG, cols] = low[:SEG]
        od_bwd[3 * SEG :, cols] = jnp.zeros((od_bwd.shape[0] - 3 * SEG, CHUNK), BF16)
        high, low = split(values.T)
        od_fwd[cols, :LANES] = high
        od_fwd[cols, LANES:] = low
        return 0

    lax.fori_loop(0, ordered.shape[1] // CHUNK, spread, 0)


def last_kernel(
    at, masked_hbm, x_hbm, lifts_hbm, lifted_hbm, act_hbm, down_hbm, b_down, sums, taps, up_row, token, table_keep, table_give, hidden_keep, hidden_give,
    table,    masked, x_parts, lifts, lifted, act, down, masked_t, x_t, g_hidden, natural, g_parts, sems, *, spans, blocks,
):
    chunks = act.shape[0]
    half = hidden_keep.shape[1]
    width = table.shape[1]
    scale = (at[1] == 0).astype(F32)
    tap_rows = taps.shape[0]
    pairs = [(masked_hbm, masked), (x_hbm, x_parts), (lifts_hbm, lifts), (lifted_hbm, lifted)]
    firsts = [pltpu.make_async_copy(pair[0], pair[1], sems.at[i]) for i, pair in enumerate(pairs)]
    downs = [
        pltpu.make_async_copy(down_hbm.at[pl.ds(start, size)], down.at[pl.ds(start, size)], sems.at[4 + i])
        for i, (start, size) in enumerate(blocks)
    ]

    def get(t):
        return pltpu.make_async_copy(act_hbm.at[t], act.at[t], sems.at[4 + len(blocks) + t])

    firsts[0].start()
    for t in range(chunks):
        get(t).start()
    for copy in firsts[1:] + downs:
        copy.start()
    firsts[0].wait()
    turned = masked[...].T[:SEG]
    high = turned.astype(BF16)
    masked_t[:SEG] = high
    masked_t[SEG:] = (turned - high.astype(F32)).astype(BF16)
    total = jnp.sum(turned, axis=1, keepdims=True)

    def chunk(t, _):
        get(t).wait()
        high, low = split(act[t])
        both = dot(masked_t[...], high)
        sums_now = (both[:SEG] + both[SEG:]) + dot(masked_t[:SEG], low)
        g_hidden[:, pl.ds(pl.multiple_of(t * CHUNK, CHUNK), CHUNK)] = sums_now
        return 0

    lax.fori_loop(0, chunks, chunk, 0)
    hidden_keep[...] = g_hidden[:, pl.ds(pl.multiple_of(at[0] * half, LANES), half)]
    hidden_give[...] = g_hidden[:, pl.ds(pl.multiple_of((1 - at[0]) * half, LANES), half)]
    for start, size, place in spans:
        natural[:, start : start + size] = g_hidden[:, place : place + size]
    high, low = split(natural[...])
    g_parts[:SEG] = high
    g_parts[SEG:] = low
    for copy in firsts[1:]:
        copy.wait()
    high, low = split(x_parts[...].T)
    x_t[0] = high
    x_t[1] = low
    for start in range(0, width, CHUNK):
        size = min(CHUNK, width - start)
        lanes = slice(start, start + size)
        high, low = split(lifted[:, :, lanes].reshape(lifts.shape[0], size))
        both = dot(masked_t[...], high)
        lifted_sum = (both[:SEG] + both[SEG:]) + dot(masked_t[:SEG], low)
        grads = lifts[:, lanes]
        high, low = split(grads)
        g_in = dot(x_t[0], high) + dot(x_t[1], high) + dot(x_t[0], low)
        table[:88, lanes] = g_in[:88]
        table[88:168, lanes] = g_in[LANES : LANES + 80]
        table[168:224, lanes] = sums[:tap_rows, lanes] + taps[:, lanes]
        table[224:304, lanes] = lifted_sum + total * b_down[:, lanes]
        table[304:311, lanes] = sums[tap_rows : tap_rows + 7, lanes] * scale
        table[311:312, lanes] = jnp.sum(grads, axis=0, keepdims=True)
    for (start, size), copy in zip(blocks, downs):
        copy.wait()
        high, low = split(down[start : start + size])
        both = dot_t(g_parts[...], high)
        g_out = (both[:SEG] + both[SEG:]) + dot_t(g_parts[:SEG], low)
        table[224:304, start : start + size] += g_out
    table[312:] = jnp.zeros((table.shape[0] - 312, width), F32)
    for i, start in enumerate(range(0, up_row.shape[1], width)):
        size = min(width, up_row.shape[1] - start)
        table[312 + i : 313 + i, :size] = up_row[:1, start : start + size] * scale
    table[316:317, :LANES] = jnp.sum(masked[...], axis=0, keepdims=True)
    rows = table_keep.shape[0]
    table_keep[...] = table[pl.ds(pl.multiple_of(at[0] * rows, 8), rows), :]
    table_give[...] = table[pl.ds(pl.multiple_of((1 - at[0]) * rows, 8), rows), :]


def flags(at):
    return at[3], at[4], at[5], at[2]


def cut_first_kernel(at, keep, got, keep_a, give_a, keep_b, give_b, *, rows, cols):
    x, y, _, _ = flags(at)

    def part(row, k):
        here = (slice(row * rows, (row + 1) * rows), slice(k * cols, (k + 1) * cols))
        return keep[here] + got[here]

    for i, (even, odd) in enumerate(((0, 1), (2, 3))):
        one, two = part(0, even), part(0, odd)
        keep_a[i] = jnp.where(x == 0, one, two)
        give_a[i] = jnp.where(x == 0, two, one)
    for i, (low, top) in enumerate(((0, 2), (1, 3))):
        one, two = part(1, low), part(1, top)
        keep_b[i] = jnp.where(y == 0, one, two)
        give_b[i] = jnp.where(y == 0, two, one)


def cut_second_kernel(at, keep_a, got_a, keep_b, got_b, keep_a_out, give_a_out, keep_b_out, give_b_out):
    x, y, _, _ = flags(at)
    for bit, keep, got, keep_out, give_out in (
        (y, keep_a, got_a, keep_a_out, give_a_out),
        (x, keep_b, got_b, keep_b_out, give_b_out),
    ):
        keep_out[...] = keep[bit] + got[bit]
        give_out[...] = keep[1 - bit] + got[1 - bit]


def cut_third_kernel(at, keep_a, got_a, keep_b, got_b, keep_out, give_out):
    _, _, _, side = flags(at)
    one, two = keep_a[...] + got_a[...], keep_b[...] + got_b[...]
    keep_out[...] = jnp.where(side == 0, one, two)
    give_out[...] = jnp.where(side == 0, two, one)


def turn_sum_kernel(at, keep, got, out_ref):
    out_ref[...] = (keep[...] + got[...]).T


def quarter_rows_kernel(at, keep, got, *outs):
    rows = outs[0].shape[0]
    pair = at[5]
    for b, out_ref in enumerate(outs):
        place = pl.multiple_of((pair ^ b) * rows, 8)
        out_ref[...] = keep[pl.ds(place, rows), :] + got[pl.ds(place, rows), :]


def quarter_cols_kernel(at, keep, got, *outs):
    cols = outs[0].shape[1]
    pair = at[5]
    parts = [keep[:, k * cols : (k + 1) * cols] + got[:, k * cols : (k + 1) * cols] for k in range(4)]
    for b, out_ref in enumerate(outs):
        k = pair ^ b
        low = jnp.where(k == 0, parts[0], parts[1])
        top = jnp.where(k == 2, parts[2], parts[3])
        out_ref[...] = jnp.where(k < 2, low, top)


def sum_two_kernel(at, a, b, out_ref):
    out_ref[...] = a[...] + b[...]


def sum_four_kernel(at, a, b, c, d, out_ref):
    out_ref[...] = (a[...] + b[...]) + (c[...] + d[...])


def join_rows_kernel(at, a, b, c, d, out_ref):
    rows = a.shape[0]
    for flip, ref in enumerate((a, b, c, d)):
        out_ref[pl.ds(pl.multiple_of((at[5] ^ flip) * rows, 8), rows), :] = ref[...]


def share_down_kernel(at, a, b, w_hi, w_lo, out_ref):
    high, low = split(a[...] + b[...])
    out_ref[...] = dot(w_hi[...], high) + dot(w_hi[...], low) + dot(w_lo[...], high)


def table_kernel(at, mine, other, g_in, g_dw, g_out, rows_out, *, states, forces):
    core = at[0]
    half = mine.shape[0]
    channels = g_in.shape[1]

    def get(start, size):
        pieces = []
        for base in (0, half):
            low, top = max(start, base), min(start + size, base + half)
            if low < top:
                here = slice(low - base, top - base)
                pieces.append(jnp.where(core == (base > 0), mine[here, :channels], other[here, :channels]))
        return pieces[0] if len(pieces) == 1 else jnp.concatenate(pieces, axis=0)

    g_in[:states] = get(0, 88)[:states]
    g_in[states : 2 * states] = get(88, 80)[:states]
    g_in[2 * states :] = get(0, 88)[states : states + forces]
    taps = get(168, 56)
    for p in range(KW):
        g_dw[p] = taps[p * KW : (p + 1) * KW]
    g_out[...] = get(224, 80)[:states]
    for i, start in enumerate((304, 312)):
        piece = jnp.where(core == (start >= half), mine[start % half : start % half + 8], other[start % half : start % half + 8])
        rows_out[8 * i : 8 * i + 8] = piece


def going_kernel(at, *refs, states, forces):
    homes, out_ref = refs[:-1], refs[-1]
    steps = len(homes)
    block = out_ref.shape[1]
    for j in range(steps):
        out_ref[8 * j : 8 * j + 8] = jnp.concatenate([homes[j][states : states + forces], jnp.zeros((8 - forces, block), F32)], axis=0)
    out_ref[8 * steps : 8 * steps + 80] = homes[0][:80]
    out_ref[8 * steps + 80 :] = homes[0][LANES : LANES + 80]


def roll_kernel(at, states, forces, out_ref):
    steps = out_ref.shape[0]
    high = states.shape[1]
    for i in range(steps):
        here = lax.rem(i - at[6] + steps, steps)
        out_ref[i, :high] = states[here]
        out_ref[i, high:] = forces[pl.ds(pl.multiple_of(here * 8, 8), 8), :]


def home_kernel(at, gone, ending, predicted, grad_forcing, grad_init, *, states):
    steps = gone.shape[0]
    total = gone[0, SEG:]
    for i in range(steps):
        predicted[i] = gone[lax.rem(at[6] - i + steps, steps), :states]
        if i:
            total = total + gone[i, SEG:]
    grad_forcing[...] = total
    base = 8 * steps
    prev, cur = ending[base : base + SEG][:states], ending[base + SEG : base + 2 * SEG][:states]
    single = at[7] == 1
    grad_init[0] = jnp.where(single, 0.0, prev)
    grad_init[1] = jnp.where(single, cur + prev, cur)


def pad_to(values, shape):
    return jnp.pad(values, [(0, size - have) for size, have in zip(shape, values.shape)])


def per_device(
    init_states, forcing, history, land_mask, w_in, b_in, w_dw, bn_gain, bn_bias, w_up, b_up, w_down, b_down, w_out, b_out, cotangent
):
    steps = lax.axis_size("step")
    devices_z = lax.axis_size("rows")
    step = lax.axis_index("step")
    depth = lax.axis_index("rows")
    core, pair = step % 2, step // 2
    side, part = depth % 2, depth // 2
    both_axes = ("step", "rows")
    block = land_mask.shape[0]
    px = 2 * block
    rows = px // COLS
    states = w_out.shape[0]
    forces = forcing.shape[2]
    channels = w_up.shape[1]
    hidden = w_up.shape[0]
    width = round_up(channels, LANES)
    ff_block = hidden // steps
    half = round_up(hidden // 2, LANES)
    wide = 2 * half
    spans = [(s * ff_block, ff_block, (s % 2) * half + (s // 2) * ff_block) for s in range(steps)]
    k_main = channels // CHUNK * CHUNK
    k_rem = channels - k_main
    col_block = channels // devices_z

    def place(s, z):
        return s * devices_z + z

    cells = [(k, c, h, q) for k in range(steps // 2) for c in range(2) for h in range(2) for q in range(2)]
    fetch_perms = [
        [(place(2 * k + q, 2 * c + (b ^ h)), place(2 * k + c, 2 * h + q)) for k, c, h, q in cells] for b in range(2)
    ]

    column_perm = [(place(2 * k + c, 2 * h + q), place(2 * k + q, 2 * c + h)) for k, c, h, q in cells]
    siblings = [(s, s ^ 1) for s in range(steps)]

    def to_sibling(values):
        return lax.ppermute(values, "step", siblings)

    def shift_back(values, j):
        return values if j == 0 else lax.ppermute(values, "step", [((s + j) % steps, s) for s in range(steps)])

    def fetch_own(values):
        got = [lax.ppermute(values, both_axes, perm) for perm in fetch_perms]
        return got

    def turn_round(values):
        n = values.shape[0]
        doubled = jnp.flip(jnp.concatenate([values, values]), axis=0)
        return lax.dynamic_slice_in_dim(doubled, n - 1 - step % n, n, axis=0)

    def rotate(values, by):
        return lax.dynamic_slice_in_dim(jnp.concatenate([values, values]), by, steps, axis=0)

    def from_later(values):
        if steps == ROLL:
            return rotate(lax.all_to_all(turn_round(values), "step", 0, 0, tiled=True), step)
        return jnp.stack([shift_back(values[j], j) for j in range(ROLL)])

    def to_later(values):
        if steps == ROLL:
            return turn_round(lax.all_to_all(rotate(values, (steps - step) % steps), "step", 0, 0, tiled=True))
        return jnp.stack([lax.ppermute(values[j], "step", [(s, (s + j) % steps) for s in range(steps)]) for j in range(ROLL)])

    at = jnp.stack([core, part, side, pair % 2, (pair // 2) % 2, pair, step % ROLL, history[0, 0]]).astype(jnp.int32)
    mask_row = land_mask.astype(F32)[None]
    current = init_states[0, 0, 1]
    previous = jnp.where(history[0, 0] == 2, init_states[0, 0, 0], current)
    payload = jnp.concatenate([previous, forcing[0, 0], current, mask_row], axis=0)
    timed = jnp.concatenate([cotangent[0, :, 0], jnp.broadcast_to(forcing[0], (ROLL,) + forcing.shape[2:])], axis=1)
    payload, timed = lax.optimization_barrier((payload, timed))
    payload = fetch_own(payload)
    timed = from_later(timed)

    def in_rows(values):
        top = jnp.concatenate([values[:states], values[2 * states :]], axis=0)
        bottom = values[states : 2 * states]
        return jnp.concatenate([jnp.pad(v, ((0, LANES - v.shape[0]), (0, 0))) for v in (top, bottom)], axis=0)

    def row(values, size):
        return jnp.pad(values, (0, size - values.shape[0]))[None]

    w_oi = jnp.dot(w_out, w_in, precision=HIGHEST)
    w_first = jnp.concatenate([pad_to(in_rows(v.T), (2 * LANES, round_up(v.shape[0], LANES))) for v in (w_in, w_oi)], axis=1)
    w_in_hi, w_in_lo = split_outside(w_first)
    b_new = row(jnp.dot(w_out, b_in + b_down, precision=HIGHEST) + b_out, LANES)
    taps = jnp.broadcast_to(
        pad_to(w_dw.reshape(channels, KW * KW).T, (KW * KW, width))[:, None], (KW * KW, 8, width)
    )
    gain, bias = row(bn_gain, width), row(bn_bias, width)
    row_hi, row_lo = split_outside(pad_to(w_out, (SEG, channels)))
    out_parts = jnp.concatenate([row_hi, row_lo], axis=0)
    pieces = 5
    w_od_fwd, w_od_bwd = call(
        functools.partial(down_kernel, spans=spans), "down", (w_down, out_parts),
        [out(wide, 2 * LANES, dtype=BF16), out(2 * LANES, wide, dtype=BF16)],
        [pltpu.VMEM((channels, hidden), F32), pltpu.VMEM((SEG, hidden), F32), pltpu.VMEM((LANES, wide), F32), pltpu.SemaphoreType.DMA((pieces,))],
        20, micros=7, hbm=(0,), vmem_outs=(0, 1),
    )
    out_hi, out_lo = split_outside(pad_to(w_out, (SEG, width)))
    w_out_bwd = pad_to(jnp.concatenate([out_hi, out_hi, out_lo], axis=0), (2 * LANES, width))
    b_in_row = row(b_in, width)
    b_up_row = pad_to(b_up.reshape(steps // 2, 2, ff_block).swapaxes(0, 1).reshape(2, hidden // 2), (2, half)).reshape(1, wide)
    b_down_row = row(b_down, width)
    w_block = lax.dynamic_slice_in_dim(w_out, depth * col_block, col_block, axis=1).T
    w_block_hi, w_block_lo = split_outside(pad_to(w_block, (col_block, SEG)))
    prev, cur, ocean, first_sent = call(
        functools.partial(start_kernel, states=states, forces=forces), "start", (at, *payload),
        [out(px, LANES), out(px, LANES), out(px, LANES), out(block + 8, 3 * LANES)], [], 4, micros=1, smem=1,
    )
    first_came = to_sibling(first_sent)
    ready = lax.optimization_barrier(
        (w_up.T, timed, w_in_hi, w_in_lo, b_new, taps, gain, bias, w_out_bwd, b_in_row, b_up_row, b_down_row, w_block_hi, w_block_lo, at, first_sent)
    )
    up_source, timed, w_in_hi, w_in_lo, b_new, taps, gain, bias, w_out_bwd, b_in_row, b_up_row, b_down_row, w_block_hi, w_block_lo, at, first_sent = ready
    timed = fetch_own(timed)
    (w_up_all,) = call(
        functools.partial(up_kernel, k_main=k_main, k_rem=k_rem, spans=spans), "up", (up_source,),
        [out(2 * k_main + LANES, wide, dtype=BF16)],
        [pltpu.VMEM((3, k_main // 8, hidden), F32), pltpu.VMEM((k_main // 8, wide), F32), pltpu.SemaphoreType.DMA((3,))],
        10, micros=7, hbm=(0,), vmem_outs=(0,),
    )
    first_came, w_up_all = lax.optimization_barrier((first_came, w_up_all))
    force, force_send, cots = call(
        functools.partial(pack_kernel, states=states, forces=forces), "pack", (at, *timed),
        [out(ROLL, px, LANES), out(ROLL, block, LANES), out(ROLL, px, LANES)], [], 6, micros=2, smem=1,
    )
    force_edge = to_sibling(force_send)

    chunks = wide // CHUNK
    x_all, lifted_all, act_all, state_all = None, None, None, None
    kept = []
    prev_edge, cur_edge, prev_lanes, cur_lanes = first_came, first_came, 0, LANES
    for j in range(ROLL):
        mixed, stats, base, window, x_all, lifted_all = call(
            functools.partial(mix_kernel, turn=j, cur_lanes=cur_lanes, prev_lanes=prev_lanes), "mix",
            (at, cur, cur_edge, prev, prev_edge) + ((force, force_edge) if j else (at, at)) + (w_in_hi, w_in_lo, b_in_row, b_new, taps, ocean),
            [
                out(px, width), out(8, width), out(px, LANES), out(HALO + 2 * HALO, COLS, width), out(ROLL * block, 2 * LANES),
                out(ROLL * HALO, COLS, width),
            ],
            [
                pltpu.VMEM((rows + 2 * HALO, COLS + 16, width), F32),
                pltpu.VMEM((rows, COLS, width), F32), pltpu.VMEM((block, 2 * LANES), F32), pltpu.SemaphoreType.DMA((3,)),
            ],
            12, micros=4.5, smem=1, hbm_outs=(3,), stacked=((4, x_all), (5, lifted_all)),
        )
        stats_other = to_sibling(stats)
        new, new_edge, norm_edge, inv, norm, slope, act_all, state_all = call(
            functools.partial(feed_kernel, turn=j, width=width, k_main=k_main, k_rem=k_rem), "feed",
            (at, mixed, stats, stats_other, first_sent, first_came, gain, bias, ocean, base, w_up_all, b_up_row, w_od_fwd),
            [
                out(px, LANES), out(block, LANES), out(block, width), out(8, width), out(px, width),
                out(chunks, px, CHUNK), out(chunks, ROLL * block, CHUNK), out(ROLL, SEG, block),
            ],
            [
                pltpu.VMEM((2 * px, k_main), BF16), pltpu.VMEM((px, LANES), BF16),
                pltpu.VMEM((px, CHUNK), F32), pltpu.VMEM((px, LANES), F32), pltpu.VMEM((px, CHUNK), F32), pltpu.VMEM((px, CHUNK), F32),
                pltpu.VMEM((px, CHUNK), F32), pltpu.VMEM((px, width), F32), pltpu.VMEM((chunks, px, CHUNK), F32),
                pltpu.VMEM((chunks, block, CHUNK), F32), pltpu.VMEM((SEG, block), F32), pltpu.SemaphoreType.DMA((2 * chunks + 2,)),
            ],
            14, micros=8.5, smem=1, hbm_outs=(4, 5), stacked=((6, act_all), (7, state_all)),
        )
        prev, prev_edge, prev_lanes, cur = cur, cur_edge, cur_lanes, new
        if j < ROLL - 1:
            cur_edge, cur_lanes = to_sibling(new_edge), 0
        norm_edge = to_sibling(norm_edge)
        kept.append((window, norm, norm_edge, slope, inv))

    states_home = lax.ppermute(state_all, both_axes, column_perm)
    quarter = channels // 2
    acc_rows = round_up(quarter + 1, 8)
    tap_rows = round_up(KW * KW, 8)
    carry, pending = None, jnp.zeros((px, LANES), F32)
    previous_step, keep_acc, give_acc, sums, lift_all, masked_all = None, None, None, None, None, None
    homes = []
    begin_scratch = [
        pltpu.VMEM((px, LANES), F32), pltpu.VMEM((chunks, px, CHUNK), F32), pltpu.VMEM((block, LANES), F32),
        pltpu.VMEM((px, wide), F32), pltpu.SemaphoreType.DMA((3,)),
    ]
    finish_scratch = [
        pltpu.VMEM((rows + 2 * HALO, COLS + 16, width), F32), pltpu.VMEM((KW, rows + 2 * HALO, COLS, LANES), F32),
        pltpu.VMEM((rows, COLS, width), F32), pltpu.VMEM((px, width), F32), pltpu.SemaphoreType.DMA,
    ]
    for j in range(ROLL - 1, -2, -1):
        finish, begin = j < ROLL - 1, j >= 0
        if finish:
            pending, keep_acc, give_acc = lax.optimization_barrier((pending, keep_acc, give_acc))
        if j == ROLL - 4:
            pending, states_home = lax.optimization_barrier((pending, states_home))
        args, outs, scratch, stacked, hbm = [at, ocean, pending], [], [], [], ()
        if finish:
            window, norm, norm_edge, slope, inv = kept[j + 1]
            grad_n, sent, came, grad_branch = previous_step
            args += [grad_n, sent, came, norm, norm_edge, inv, gain, first_sent, first_came, grad_branch, window, taps, w_in_hi, w_in_lo]
            outs += [out(px, LANES), out(px, LANES), out(tap_rows, width), out(2 * LANES, block), out(ROLL * block, width)]
            stacked.append((4, lift_all))
            scratch += finish_scratch
        if begin:
            hbm = (len(args), len(args) + 1)
            args += [cots, kept[j][3], kept[j][1], w_out_bwd, w_od_bwd, w_up_all]
            outs += [out(px, width), out(2 * px, wide, dtype=BF16), out(px, width), out(block + 8, width), out(ROLL * block, LANES)]
            stacked.append((len(outs) - 1, masked_all))
            scratch += begin_scratch
        kernel = functools.partial(
            back_kernel, finish=finish, begin=begin, turn=j, width=width, k_main=k_main, k_rem=k_rem, states=states
        )
        results = list(
            call(kernel, "back", args, outs, scratch, 18, micros=7 * finish + 7.5 * begin, smem=1, hbm=hbm, stacked=stacked)
        )
        if finish:
            carry, pending, tap_sum, home, lift_all = results[:5]
            results = results[5:]
            homes.append(home)
        if begin:
            grad_branch, hidden_now, grad_n, sent, masked_all = results
            came = to_sibling(sent)
            previous_step = (grad_n, sent, came, grad_branch)
            keep_acc, give_acc, sums, *up_row = call(
                functools.partial(weight_kernel, quarter=quarter, finish=finish), "weight",
                (at, kept[j][1], gain, bias, hidden_now, sent) + ((tap_sum, keep_acc, give_acc, sums) if finish else ()),
                [out(acc_rows, half), out(acc_rows, half), out(tap_rows + 8, width)] + ([] if j else [out(8, wide)]), [], 8, micros=5, smem=1,
                aliases=({7: 0, 8: 1, 9: 2} if j else {7: 0, 9: 2}) if finish else None, vmem_outs=(0, 1, 2) if j else (),
            )
            if j == 0:
                window, norm, norm_edge, slope, inv = kept[0]
                give_acc, came, norm_edge = lax.optimization_barrier((give_acc, came, norm_edge))
                kept[0] = (window, norm, norm_edge, slope, inv)
                previous_step = (grad_n, sent, came, grad_branch)

    def trade(values, axis, flip):
        return lax.ppermute(values, axis, [(i, i ^ flip) for i in range(lax.axis_size(axis))])

    def pick(first, second, bit):
        return jnp.where(bit == 0, first, second), jnp.where(bit == 0, second, first)

    token = [tap_sum]

    def local(kernel, args, outs, limit=8, **options):
        def body(at_ref, *refs):
            kernel(at_ref, *refs[: len(args)], *refs[len(args) + 1 : -1], **options)
            refs[-1][...] = refs[len(args)][:8, :LANES]

        results = call(body, kernel.__name__, (at, *args, token[0]), outs + [out(8, LANES)], [], limit, micros=1, smem=1)
        token[0] = results[-1]
        return results[:-1]

    direct = steps == 8 and devices_z == 4
    home_outs = [out(ROLL, states, block), out(8, block), out(2, states, block)]
    got = trade(give_acc, "step", 1)
    if direct:
        pieces = [out(2, col_block, ff_block)] * 4
        keep_a, give_a, keep_b, give_b = local(cut_first_kernel, (keep_acc, got), pieces, 16, rows=col_block, cols=ff_block)
        got_a, got_b = trade(give_a, "step", 2), trade(give_b, "step", 4)
    part_px = ROLL * block
    blocks = [(start, min(CHUNK, channels - start)) for start in range(0, channels, CHUNK)]
    table_keep, table_give, hidden_keep, hidden_give = call(
        functools.partial(last_kernel, spans=spans, blocks=blocks), "last",
        (
            at, masked_all, x_all, lift_all, lifted_all, act_all, w_down, b_down_row, sums,
            tap_sum, *up_row, token[0],
        ),
        [out(160, width), out(160, width), out(SEG, half), out(SEG, half)],
        [
            pltpu.VMEM((320, width), F32),
            pltpu.VMEM((part_px, LANES), F32), pltpu.VMEM((part_px, 2 * LANES), F32), pltpu.VMEM((part_px, width), F32),
            pltpu.VMEM(lifted_all.shape, F32), pltpu.VMEM((chunks, part_px, CHUNK), F32), pltpu.VMEM((channels, hidden), F32),
            pltpu.VMEM((2 * SEG, part_px), BF16), pltpu.VMEM((2, 2 * LANES, part_px), BF16), pltpu.VMEM((SEG, wide), F32),
            pltpu.VMEM((SEG, hidden), F32), pltpu.VMEM((2 * SEG, hidden), BF16),
            pltpu.SemaphoreType.DMA((4 + len(blocks) + chunks,)),
        ],
        44, micros=12, smem=1, hbm=(1, 2, 3, 4, 5, 6),
    )
    other = trade(table_give, "step", 1)
    hidden_other = trade(hidden_give, "step", 1)
    if direct:
        fours = (1, 2, 3)
        token[0] = table_keep
        keep_a, give_a, keep_b, give_b = local(cut_second_kernel, (keep_a, got_a, keep_b, got_b), [out(col_block, ff_block)] * 4)
        got_a, got_b = trade(give_a, "step", 4), trade(give_b, "step", 2)
        own = local(quarter_rows_kernel, (table_keep, other), [out(40, width)] * 4)
        from_xy = [trade(own[b], "step", 2 * b) for b in fours]
        h_own = local(quarter_cols_kernel, (hidden_keep, hidden_other), [out(SEG, ff_block)] * 4)
        h_xy = [trade(h_own[b], "step", 2 * b) for b in fours]
        (ending,) = local(going_kernel, homes[::-1], [out(8 * ROLL + 160, block)], states=states, forces=forces)
        ending = lax.ppermute(ending, both_axes, column_perm)
        (piece,) = local(sum_four_kernel, (own[0], *from_xy), [out(40, width)])
        near = trade(piece, "rows", 1)
        (h_piece,) = local(sum_four_kernel, (h_own[0], *h_xy), [out(SEG, ff_block)])
        h_near = trade(h_piece, "rows", 1)
        (piece,) = local(sum_two_kernel, (piece, near), [out(40, width)])
        far = trade(piece, "rows", 2)
        (h_piece,) = local(sum_two_kernel, (h_piece, h_near), [out(SEG, ff_block)])
        h_far = trade(h_piece, "rows", 2)
        keep, give = local(cut_third_kernel, (keep_a, got_a, keep_b, got_b), [out(col_block, ff_block)] * 2)
        got = trade(give, "rows", 1)
        (rolled,) = local(roll_kernel, (states_home, ending), [out(ROLL, 88, block)])
        gone = lax.all_to_all(rolled, "step", 0, 0, tiled=True)
        (piece,) = local(sum_two_kernel, (piece, far), [out(40, width)])
        from_xy = [trade(piece, "step", 2 * b) for b in fours]
        (share_down,) = local(share_down_kernel, (h_piece, h_far, w_block_hi, w_block_lo), [out(col_block, ff_block)])
        (share_up,) = local(turn_sum_kernel, (keep, got), [out(ff_block, col_block)])
        predicted, grad_forcing, grad_init = local(home_kernel, (gone, ending), home_outs, states=states)
        (mine,) = local(join_rows_kernel, (piece, *from_xy), [out(160, width)])
        other = trade(mine, "step", 1)
    else:
        units = steps // 2
        same_core = [[2 * k + c for k in range(units)] for c in range(2)]
        mine_up = keep_acc + got
        share = lax.psum_scatter(mine_up[:, : hidden // 2], "step", scatter_dimension=1, axis_index_groups=same_core, tiled=True)
        keep, give = pick(share[:col_block], share[col_block : 2 * col_block], side)
        share_up = (keep + trade(give, "rows", 1)).T
        mine_down = hidden_keep + hidden_other
        hidden_share = lax.psum(
            lax.psum_scatter(mine_down[:, : hidden // 2], "step", scatter_dimension=1, axis_index_groups=same_core, tiled=True), "rows"
        )
        nothing = jnp.zeros_like(hidden_share)
        (share_down,) = local(share_down_kernel, (hidden_share, nothing, w_block_hi, w_block_lo), [out(col_block, ff_block)])
        mine, other = pick(*[lax.psum(v, both_axes) for v in pick(table_keep, table_give, core)], core)
        (ending,) = local(going_kernel, homes[::-1], [out(8 * ROLL + 160, block)], states=states, forces=forces)
        ending = lax.ppermute(ending, both_axes, column_perm)
        gone = turn_round(to_later(jnp.concatenate([states_home, ending[: 8 * ROLL].reshape(ROLL, 8, block)], axis=1)))
        predicted, grad_forcing, grad_init = local(home_kernel, (gone, ending), home_outs, states=states)
    g_in, g_dw, g_w_out, lines = local(
        table_kernel, (mine, other),
        [out(2 * states + forces, channels), out(KW, KW, channels), out(states, channels), out(16, width)], states=states, forces=forces,
    )
    g_bias, g_gain, g_b_in = lines[0, :channels], lines[1, :channels], lines[7, :channels]
    g_b_up = lines[8:12].reshape(-1)[:wide].reshape(2, half)[:, : hidden // 2].reshape(2, steps // 2, ff_block).swapaxes(0, 1).reshape(-1)
    g_b_out = lines[12, :states]
    g_b_down = jnp.sum(w_out * g_b_out[:, None], axis=0)
    return (
        predicted[None, :, None],
        grad_init[None, None],
        grad_forcing[None, None, :forces],
        g_in.T,
        g_b_in,
        g_dw.transpose(2, 0, 1),
        g_gain,
        g_bias,
        share_up,
        g_b_up,
        share_down,
        g_b_down,
        g_w_out,
        g_b_out,
    )


def solution(mesh):
    state_spec = P("step", None, None, None, "rows")
    force_spec = P("step", None, None, "rows")
    in_specs = (state_spec, force_spec, P("step", None), P("rows")) + (P(),) * 11 + (state_spec,)
    out_specs = (state_spec, state_spec, force_spec) + (P(),) * 5 + (P("step", "rows"), P(), P("rows", "step"), P(), P(), P())
    return jax.shard_map(per_device, mesh=mesh, in_specs=in_specs, out_specs=out_specs, check_vma=False)
```
